32 devices in a mesh: space: 4 (over y, core), vel: 8 (over z, x).
Axes of the slice: x: 2, y: 2, z: 4, core: 2. Of those that a mesh axis runs over, the one named last changes fastest.
Arguments:
- distribution: float32 [4, 256, 13824], P('space', None, 'vel'), may hold values from -6 to 6
- neighbours: int32 [4, 4], P('space'), may hold values from -1 to 3, as said below
- block_level: int32 [4], P('space'), may hold values from 0 to 2
- collide_mask: int32 [1024], P('space'), may hold values from 0 to 1, as said below
- gain_first: float32 [6, 13824], replicated, may hold values from -1.8 to 1.8
- gain_second: float32 [6, 13824], replicated, may hold values from -1.8 to 1.8
- loss_rates: float32 [13824], replicated, may hold values from 0.2 to 2
Outputs:
- distribution_next: float32 [4, 256, 13824], P('space', None, 'vel')
The draws below stay inside these ranges and needn't reach their ends.
Inputs may be any that keep to these rules, and one draw needn't show every extreme that they name: `neighbours`: each entry is -1 or a block held by the same index of space as the block itself or by the index one below or one above (index s holds blocks s * 1 to (s + 1) - 1). `collide_mask`: the cells of one index of space (its 1 block) hold at most 128 ones, and some index holds exactly 128.
All inputs are finite; a program needn't handle non-finite values.
Results may differ from the reference program's by a relative error of at most 0.0003.
Values sent between devices are 32-bit elements; how exact they have to be, the bound alone decides.
A program may use at most 128 MiB of HBM per device.

```python
import math
import jax
import jax.numpy as jnp
from jax import lax

BSIDE = 16
VDIM = 24
TERMS = 6
LEVELS = 3
BLK_DEV = 1
NB = 4
ACT = 128
NV = 13824


def draw_neighbours(key, part):
    spaces = NB // BLK_DEV
    blocks = jnp.arange(NB, dtype=jnp.int32)
    owner_index = blocks // BLK_DEV
    key_kind, key_within = jax.random.split(jax.random.fold_in(key, 11), 2)
    face_kind = jax.random.randint(key_kind, (NB, 4), 0, 8)
    offset = jnp.where(face_kind <= 2, -1, jnp.where(face_kind <= 5, 0, 1))
    first_block = (blocks % BLK_DEV == 0) & (owner_index > 0)
    final_block = (blocks % BLK_DEV == BLK_DEV - 1) & (owner_index < spaces - 1)
    offset = offset.at[:, 2].set(jnp.where(first_block, -1, offset[:, 2]))
    offset = offset.at[:, 3].set(jnp.where(final_block, 1, offset[:, 3]))
    face_kind = face_kind.at[:, 2].set(jnp.where(first_block, 1, face_kind[:, 2]))
    face_kind = face_kind.at[:, 3].set(jnp.where(final_block, 7, face_kind[:, 3]))
    target = owner_index[:, None] + offset
    within = jax.random.randint(key_within, (NB, 4), 0, BLK_DEV)
    source = target * BLK_DEV + within
    usable = (face_kind != 0) & (target >= 0) & (target < spaces)
    source = jnp.where(usable, source, -1)
    source = source.at[0, 0].set(-1)
    source = source.at[NB - 2, 1].set(NB - 1)
    return source.astype(jnp.int32)


def draw_collide_mask(key, part):
    spaces = NB // BLK_DEV
    per_space = BLK_DEV * BSIDE * BSIDE
    key_count, key_full, key_order = jax.random.split(jax.random.fold_in(key, 23), 3)
    counts = jax.random.randint(key_count, (spaces,), ACT // 2, ACT + 1)
    busiest = jax.random.randint(key_full, (), 0, spaces)
    counts = counts.at[busiest].set(ACT)

    def one_order(single):
        return jax.random.permutation(single, per_space)
    orders = jax.vmap(one_order)(jax.random.split(key_order, spaces))
    return (orders < counts[:, None]).astype(jnp.int32).reshape(-1)


def set_ends(array, rng, least, top_value):
    longest = array.shape.index(max(array.shape))
    spots = []
    for shift in (0, 1):
        where = [jax.random.randint(jax.random.fold_in(rng, axis), (), 0, length) for axis, length in enumerate(array.shape)]
        where[longest] = (where[longest] + shift) % array.shape[longest]
        spots.append(tuple(where))
    return array.at[spots[0]].set(least).at[spots[1]].set(top_value)


def shard_levels(stream_key, shape, cuts, low, largest):
    level, own = 1.0, jax.random.fold_in(stream_key, 6)
    for position, shards_of in cuts:
        steps = jnp.exp(jax.random.uniform(jax.random.fold_in(own, position), (shards_of,), jnp.float32, low / len(cuts), largest / len(cuts)))
        level = level * jnp.repeat(steps, shape[position] // shards_of).reshape([-1 if axis == position else 1 for axis in range(len(shape))])
    return level


def bell_draw(own_key, shape, spread, limit, cuts=(), kind=jnp.bfloat16):
    values = jax.random.normal(own_key, shape, jnp.float32) * spread
    if len(cuts) > 0:
        values = shard_levels(own_key, shape, cuts, -0.22, 0.18) * values
    return jnp.clip(values, min=-limit, max=limit).astype(kind)


def setup_inputs(seed: int = 0) -> dict:
    key_list = jax.random.split(jax.random.key(seed), 8)
    distribution = bell_draw(key_list[0], (NB, BSIDE * BSIDE, NV), 1.0, 6.0, ((0, 4), (2, 8)), jnp.float32)
    neighbours = draw_neighbours(jax.random.fold_in(key_list[7], 71), 0)
    block_level = set_ends(jax.random.randint(key_list[2], (NB,), 0, LEVELS), jax.random.fold_in(key_list[2], 1), 0, LEVELS - 1).astype(jnp.int32)
    collide_mask = draw_collide_mask(jax.random.fold_in(key_list[7], 71), 0)
    gain_first = bell_draw(key_list[4], (TERMS, NV), 0.3, 1.8, (), jnp.float32)
    gain_second = bell_draw(key_list[5], (TERMS, NV), 0.3, 1.8, (), jnp.float32)
    loss_rates = jnp.clip(jnp.exp(jax.random.uniform(key_list[6], (NV,), jnp.float32, math.log(0.2), math.log(2.0))), 0.2, 2.0)
    return dict(distribution=distribution, neighbours=neighbours, block_level=block_level, collide_mask=collide_mask, gain_first=gain_first, gain_second=gain_second, loss_rates=loss_rates)


weno_eps = 1e-06
courant = 0.2

def weno_value(minus_two, minus_one, middle, plus_one, plus_two):
    guess_low = (2.0 * minus_two - 7.0 * minus_one + 11.0 * middle) / 6.0
    guess_mid = (-minus_one + 5.0 * middle + 2.0 * plus_one) / 6.0
    guess_high = (2.0 * middle + 5.0 * plus_one - plus_two) / 6.0
    rough_low = 13.0 / 12.0 * (minus_two - 2.0 * minus_one + middle) ** 2 + 0.25 * (minus_two - 4.0 * minus_one + 3.0 * middle) ** 2
    rough_mid = 13.0 / 12.0 * (minus_one - 2.0 * middle + plus_one) ** 2 + 0.25 * (minus_one - plus_one) ** 2
    rough_high = 13.0 / 12.0 * (middle - 2.0 * plus_one + plus_two) ** 2 + 0.25 * (3.0 * middle - 4.0 * plus_one + plus_two) ** 2
    weight_low = 0.1 / (weno_eps + rough_low) ** 2
    weight_mid = 0.6 / (weno_eps + rough_mid) ** 2
    weight_high = 0.3 / (weno_eps + rough_high) ** 2
    return (weight_low * guess_low + weight_mid * guess_mid + weight_high * guess_high) / (weight_low + weight_mid + weight_high)

def edge_values(padded, along, cell_count):

    def shifted(offset):
        return lax.slice_in_dim(padded, offset, offset + cell_count + 1, axis=along)
    upwind_low = weno_value(shifted(0), shifted(1), shifted(2), shifted(3), shifted(4))
    upwind_high = weno_value(shifted(5), shifted(4), shifted(3), shifted(2), shifted(1))
    return (upwind_low, upwind_high)

def flux_change(padded, along, cell_count, velocity):
    from_low, from_high = edge_values(padded, along, cell_count)
    step_low = lax.slice_in_dim(from_low, 1, cell_count + 1, axis=along) - lax.slice_in_dim(from_low, 0, cell_count, axis=along)
    step_high = lax.slice_in_dim(from_high, 1, cell_count + 1, axis=along) - lax.slice_in_dim(from_high, 0, cell_count, axis=along)
    return jnp.maximum(velocity, 0.0) * step_low + jnp.minimum(velocity, 0.0) * step_high

def transport_rate(padded_first, padded_second, along, cell_count, speed_first, speed_second, courant_ratio):
    change = flux_change(padded_first, along, cell_count, speed_first) + flux_change(padded_second, along + 1, cell_count, speed_second)
    return -courant_ratio * change

def grid_speeds(vel_start, vel_width, vdim):
    index = vel_start + jnp.arange(vel_width, dtype=jnp.int32)
    first_index = index // (vdim * vdim)
    second_index = index // vdim % vdim
    half = (vdim - 1) / 2.0
    return ((first_index.astype(jnp.float32) - half) / half, (second_index.astype(jnp.float32) - half) / half)

def hartley(length):
    grid_index = jnp.arange(length, dtype=jnp.float32)
    angle_table = 2.0 * jnp.pi * grid_index[:, None] * grid_index[None, :] / length
    return (jnp.cos(angle_table) + jnp.sin(angle_table)) / jnp.sqrt(jnp.float32(length))

def hartley_cube(velocity_cube, hartley_table):
    highest = lax.Precision.HIGHEST
    velocity_cube = jnp.einsum('cijk,kl->cijl', velocity_cube, hartley_table, precision=highest)
    velocity_cube = jnp.einsum('cijk,jl->cilk', velocity_cube, hartley_table, precision=highest)
    return jnp.einsum('cijk,il->cljk', velocity_cube, hartley_table, precision=highest)

def collide(cell_rows, gain_first, gain_second, loss_rates, hartley_table):
    row_count = cell_rows.shape[0]
    vdim = hartley_table.shape[0]
    velocity_cube = cell_rows.reshape(row_count, vdim, vdim, vdim)
    spectrum = hartley_cube(velocity_cube, hartley_table)
    gain_total = jnp.zeros_like(velocity_cube)
    for term_index in range(gain_first.shape[0]):
        gain_one = hartley_cube(spectrum * gain_first[term_index].reshape(vdim, vdim, vdim), hartley_table)
        gain_two = hartley_cube(spectrum * gain_second[term_index].reshape(vdim, vdim, vdim), hartley_table)
        gain_total = gain_total + gain_one * gain_two
    loss_part = hartley_cube(spectrum * loss_rates.reshape(vdim, vdim, vdim), hartley_table)
    return (gain_total - velocity_cube * loss_part).reshape(row_count, -1)

def block_rates(density, neighbours, block_level, speed_first, speed_second):
    block_side = density.shape[1]

    def one_block(block_index):
        own_block = density[block_index]
        sources = neighbours[block_index]

        def ghost(face_index):
            source = sources[face_index]
            return density[jnp.maximum(source, 0)] * (source >= 0).astype(jnp.float32)
        ghost_west = ghost(0)[block_side - 3:]
        ghost_east = ghost(1)[:3]
        ghost_south = ghost(2)[:, block_side - 3:]
        ghost_north = ghost(3)[:, :3]
        padded_first = jnp.concatenate([ghost_west, own_block, ghost_east], axis=0)
        padded_second = jnp.concatenate([ghost_south, own_block, ghost_north], axis=1)
        courant_ratio = courant * jnp.exp2(block_level[block_index].astype(jnp.float32))
        return transport_rate(padded_first, padded_second, 0, block_side, speed_first, speed_second, courant_ratio)
    return lax.map(one_block, jnp.arange(NB, dtype=jnp.int32))

def reference(distribution, neighbours, block_level, collide_mask, gain_first, gain_second, loss_rates):
    density = distribution.reshape(NB, BSIDE, BSIDE, NV)
    speed_first, speed_second = grid_speeds(0, NV, VDIM)
    section_one = density + block_rates(density, neighbours, block_level, speed_first, speed_second)
    section_two = 0.5 * density + 0.5 * (section_one + block_rates(section_one, neighbours, block_level, speed_first, speed_second))
    hartley_table = hartley(VDIM)
    flat_cells = section_two.reshape(NB, BSIDE * BSIDE, NV)
    marked = collide_mask.reshape(NB, BSIDE * BSIDE).astype(jnp.float32)

    def collide_block(inputs):
        cell_rows, block_marks = inputs
        return cell_rows + block_marks[:, None] * collide(cell_rows, gain_first, gain_second, loss_rates, hartley_table)
    return lax.map(collide_block, (flat_cells, marked))
```

```python
import functools

import jax
import jax.numpy as jnp
import numpy as np
from jax import lax
from jax.experimental import pallas as pl
from jax.experimental.pallas import tpu as pltpu
from jax.sharding import PartitionSpec as P

BSIDE = 16
VDIM = 24
ACT = 128
LANES = 128
GROUP = 8


weno_eps = 1e-06
courant = 0.2


def speed_rows(vel_start, vel_width):
    index = vel_start + jnp.arange(vel_width, dtype=jnp.int32)
    half = (VDIM - 1) / 2.0
    first = ((index // (VDIM * VDIM)).astype(jnp.float32) - half) / half
    second = ((index // VDIM % VDIM).astype(jnp.float32) - half) / half
    rows = [jnp.abs(first), jnp.abs(second), jnp.where(first < 0, 1.0, 0.0), jnp.where(second < 0, 1.0, 0.0)]
    return jnp.stack(rows + [jnp.zeros_like(first)] * 4)


def pack_strips(cells_ref, against_first, against_second, strips_ref):
    side = BSIDE

    def first(n):
        return cells_ref[n * side : (n + 1) * side]

    def second(n):
        return cells_ref[pl.ds(n, side, stride=side), :]

    at = 0
    for line, against in ((first, against_first), (second, against_second)):
        far = jnp.where(against, line(2), line(side - 3))
        for layer in (line(0), line(1), far, line(side - 2), line(side - 1)):
            strips_ref[at : at + side] = layer
            at += side


def sweep(line, against, speed, flux_ref):
    side = BSIDE

    def oriented(n):
        return jnp.where(against, line(side + 5 - n), line(n))

    values = [oriented(n) for n in range(4)]
    slopes = [values[n + 1] - values[n] for n in range(3)]
    bends = []
    for n in range(2):
        bend = slopes[n + 1] - slopes[n]
        bends.append(bend * bend * (13.0 / 3.0) + 4.0 * weno_eps)
    before = None
    for i in range(side + 1):
        values.append(oriented(i + 4))
        slopes.append(values[i + 4] - values[i + 3])
        bend = slopes[i + 3] - slopes[i + 2]
        bends.append(bend * bend * (13.0 / 3.0) + 4.0 * weno_eps)
        d0, d1, d2, d3 = slopes[i : i + 4]
        tilt_low = 3.0 * d1 - d0
        tilt_mid = d1 + d2
        tilt_high = d3 - 3.0 * d2
        rough_low = bends[i] + tilt_low * tilt_low
        rough_mid = bends[i + 1] + tilt_mid * tilt_mid
        rough_high = bends[i + 2] + tilt_high * tilt_high
        low2 = rough_low * rough_low
        mid2 = rough_mid * rough_mid
        high2 = rough_high * rough_high
        weight_low = mid2 * high2
        low3 = 3.0 * low2
        weight_mid = (low3 + low3) * high2
        weight_high = low3 * mid2
        guess_low = 5.0 * d1 - 2.0 * d0
        guess_mid = d1 + (d2 + d2)
        guess_high = 4.0 * d2 - d3
        above = weight_low * guess_low + weight_mid * guess_mid + weight_high * guess_high
        below = weight_low + weight_mid + weight_high
        edge = values[i + 2] + above / (6.0 * below)
        if before is not None:
            flux_ref[(i - 1) * side : i * side] = speed * (edge - before)
        before = edge


def advance(source_ref, ratio, u_ref, base_ref, left_ref, right_ref, speed_ref, out_ref, fluxes):
    side = BSIDE
    lanes = u_ref.shape[1]
    flux_one, flux_two, flux_turned = fluxes

    def first_line(n):
        return u_ref[n * side : (n + 1) * side]

    def second_line(n):
        return u_ref[pl.ds(n, side, stride=side), :]

    def ghost(face, block, own):
        at = block * side
        return (
            source_ref[3 * face] * left_ref[at : at + side]
            + source_ref[3 * face + 1] * own
            + source_ref[3 * face + 2] * right_ref[at : at + side]
        )

    def padded(line, faces, start):
        ghosts = {}
        for layer in range(3):
            ghosts[layer] = ghost(faces[0], start + 2 + layer, line(side - 3 + layer))
            ghosts[side + 3 + layer] = ghost(faces[1], start + layer, line(layer))
        return lambda n: ghosts[n] if n in ghosts else line(n - 3)

    against_first, against_second = against_masks(speed_ref)
    sweep(padded(first_line, (0, 1), 0), against_first, spread(speed_ref, 0), flux_one)
    sweep(padded(second_line, (2, 3), 5), against_second, spread(speed_ref, 1), flux_two)
    for n in range(side):
        back = side - 1 - n
        flux_turned[n * side : (n + 1) * side] = jnp.where(
            against_second, flux_two[back * side : (back + 1) * side], flux_two[n * side : (n + 1) * side]
        )
    for n in range(side):
        back = side - 1 - n
        rows = slice(n * side, (n + 1) * side)
        change = jnp.where(against_first, flux_one[back * side : (back + 1) * side], flux_one[rows])
        change = change + flux_turned[pl.ds(n, side, stride=side), :]
        moved = u_ref[rows] - ratio * change
        if base_ref is not None:
            moved = 0.5 * base_ref[rows] + 0.5 * moved
        out_ref[rows] = moved


def spread(speed_ref, row):
    return jnp.broadcast_to(speed_ref[row : row + 1], (BSIDE, speed_ref.shape[1]))


def against_masks(speed_ref):
    return spread(speed_ref, 2) > 0.5, spread(speed_ref, 3) > 0.5


def transport_kernel(
    source_ref, ratio_ref, u_ref, speed_ref, out_ref,
    one_ref, flux_one, flux_two, flux_turned,
    strips, from_left, from_right, sent_left, sent_right, got_left, got_right,
):
    tiles = u_ref.shape[0]
    me = lax.axis_index("space")
    count = lax.axis_size("space")
    has_left, has_right = me > 0, me < count - 1
    left, right = lax.rem(me + count - 1, count), lax.rem(me + 1, count)
    mesh_ids = pl.DeviceIdType.MESH
    ratio = ratio_ref[0]
    fluxes = (flux_one, flux_two, flux_turned)

    barrier = pltpu.get_barrier_semaphore()

    @pl.when(has_left)
    def _():
        pl.semaphore_signal(barrier, inc=1, device_id={"space": left}, device_id_type=mesh_ids)

    @pl.when(has_right)
    def _():
        pl.semaphore_signal(barrier, inc=1, device_id={"space": right}, device_id_type=mesh_ids)

    pl.semaphore_wait(barrier, has_left.astype(jnp.int32) + has_right.astype(jnp.int32))

    def to_right(turn, tile):
        return pltpu.make_async_remote_copy(
            src_ref=strips.at[turn, tile], dst_ref=from_left.at[turn, tile],
            send_sem=sent_right.at[turn, tile], recv_sem=got_left.at[turn, tile],
            device_id={"space": right}, device_id_type=mesh_ids,
        )

    def to_left(turn, tile):
        return pltpu.make_async_remote_copy(
            src_ref=strips.at[turn, tile], dst_ref=from_right.at[turn, tile],
            send_sem=sent_left.at[turn, tile], recv_sem=got_right.at[turn, tile],
            device_id={"space": left}, device_id_type=mesh_ids,
        )

    def send(turn, tile, cells_ref):
        pack_strips(cells_ref.at[tile], *against_masks(speed_ref.at[tile]), strips.at[turn, tile])

        @pl.when(has_right)
        def _():
            to_right(turn, tile).start()

        @pl.when(has_left)
        def _():
            to_left(turn, tile).start()

    def receive(turn, tile):
        @pl.when(has_left)
        def _():
            to_right(turn, tile).wait_recv()

        @pl.when(has_right)
        def _():
            to_left(turn, tile).wait_recv()

    def begin(tile, carry):
        send(0, tile, u_ref)
        return carry

    lax.fori_loop(0, tiles, begin, 0)

    @pl.when(me == 0)
    def _():
        from_left[...] = jnp.zeros_like(from_left)

    @pl.when(me == count - 1)
    def _():
        from_right[...] = jnp.zeros_like(from_right)

    def first(tile, carry):
        receive(0, tile)
        advance(
            source_ref, ratio, u_ref.at[tile], None, from_left.at[0, tile], from_right.at[0, tile],
            speed_ref.at[tile], one_ref.at[tile], fluxes,
        )
        send(1, tile, one_ref)
        return carry

    lax.fori_loop(0, tiles, first, 0)

    def second(tile, carry):
        receive(1, tile)
        advance(
            source_ref, ratio, one_ref.at[tile], u_ref.at[tile], from_left.at[1, tile], from_right.at[1, tile],
            speed_ref.at[tile], out_ref.at[tile], fluxes,
        )
        return carry

    lax.fori_loop(0, tiles, second, 0)

    def finish(tile, carry):
        for turn in range(2):

            @pl.when(has_right)
            def _():
                to_right(turn, tile).wait_send()

            @pl.when(has_left)
            def _():
                to_left(turn, tile).wait_send()

        return carry

    lax.fori_loop(0, tiles, finish, 0)


def transport(source, ratio, cells, speeds):
    tiles, count, lanes = cells.shape
    smem = pl.BlockSpec(memory_space=pltpu.SMEM)
    vmem = pl.BlockSpec(memory_space=pltpu.VMEM)
    strips = pltpu.VMEM((2, tiles, 10 * BSIDE, lanes), jnp.float32)
    return pl.pallas_call(
        transport_kernel,
        in_specs=[smem, smem, vmem, vmem],
        out_specs=vmem,
        out_shape=jax.ShapeDtypeStruct(cells.shape, jnp.float32),
        scratch_shapes=[pltpu.VMEM(cells.shape, jnp.float32)]
        + [pltpu.VMEM((count, lanes), jnp.float32)] * 3
        + [strips] * 3
        + [pltpu.SemaphoreType.DMA((2, tiles))] * 4,
        compiler_params=pltpu.CompilerParams(
            collective_id=0, has_side_effects=True, vmem_limit_bytes=48 * 1024 * 1024
        ),
    )(source, ratio, cells, speeds)


def tiled(rows):
    count, width = rows.shape
    tiles = pl.cdiv(width, LANES)
    rows = jnp.pad(rows, ((0, 0), (0, tiles * LANES - width)))
    return rows.reshape(count, tiles, LANES).transpose(1, 0, 2)


def lane_pieces(tiles, width):
    return [(t, t * LANES, min(width, (t + 1) * LANES)) for t in range(tiles)]


def gather_kernel(chosen_ref, cells_ref, out_ref, picked_ref, rows_ref):
    parts, planes, each, plane = out_ref.shape
    tiles = cells_ref.shape[0]

    def one(slot, carry):
        row = chosen_ref[slot]
        for tile in range(tiles):
            picked_ref[tile, pl.ds(slot, 1), :] = cells_ref[tile, pl.ds(row, 1), :]
        return carry

    lax.fori_loop(0, parts * each, one, 0, unroll=8)
    for tile in range(tiles):
        rows_ref[:, tile * LANES : (tile + 1) * LANES] = picked_ref[tile]
    for part in range(parts):
        for n in range(planes):
            out_ref[part, n] = rows_ref[part * each : (part + 1) * each, n * plane : (n + 1) * plane]


def gather(chosen, cells, shape):
    return pl.pallas_call(
        gather_kernel,
        in_specs=[pl.BlockSpec(memory_space=pltpu.SMEM), pl.BlockSpec(memory_space=pltpu.VMEM)],
        out_specs=pl.BlockSpec(memory_space=pltpu.VMEM),
        out_shape=jax.ShapeDtypeStruct(shape, jnp.float32),
        scratch_shapes=[
            pltpu.VMEM((cells.shape[0], shape[0] * shape[2], LANES), jnp.float32),
            pltpu.VMEM((shape[0] * shape[2], cells.shape[0] * LANES), jnp.float32),
        ],
    )(chosen, cells)


def scatter_kernel(chosen_ref, count_ref, cells_ref, change_ref, out_ref, rows_ref):
    parts, planes, each, plane = change_ref.shape
    for tile, begin, end in lane_pieces(cells_ref.shape[0], out_ref.shape[1]):
        out_ref[:, begin:end] = cells_ref[tile, :, : end - begin]
    for part in range(parts):
        for n in range(planes):
            rows_ref[part * each : (part + 1) * each, n * plane : (n + 1) * plane] = change_ref[part, n]

    def one(slot, carry):
        row = pl.ds(chosen_ref[slot], 1)
        out_ref[row, :] += rows_ref[pl.ds(slot, 1), :]
        return carry

    lax.fori_loop(0, count_ref[0], one, 0)


def scatter(chosen, count, cells, change):
    smem = pl.BlockSpec(memory_space=pltpu.SMEM)
    vmem = pl.BlockSpec(memory_space=pltpu.VMEM)
    parts, planes, each, plane = change.shape
    return pl.pallas_call(
        scatter_kernel,
        in_specs=[smem, smem, vmem, vmem],
        out_specs=vmem,
        out_shape=jax.ShapeDtypeStruct((cells.shape[1], planes * plane), jnp.float32),
        scratch_shapes=[pltpu.VMEM((parts * each, planes * plane), jnp.float32)],
    )(chosen, count, cells, change)


def halves(table):
    high = table.astype(jnp.bfloat16)
    low = (table - high.astype(jnp.float32)).astype(jnp.bfloat16)
    return high, low


def dot(left, right):
    return jnp.dot(left, right, preferred_element_type=jnp.float32)


def collision(values, tables, depth):
    first_ref, second_ref, loss_ref, plane_ref, line_ref = tables
    size, plane = values.shape
    group = size // depth

    def transforms(cubes):
        high, low = halves(jnp.concatenate(cubes, axis=0) if len(cubes) > 1 else cubes[0])
        rows = high.shape[0]
        wide = dot(jnp.concatenate([high, low], axis=0), plane_ref[0])
        mapped = wide[:rows] + (wide[rows:] + dot(high, plane_ref[1]))
        results = []
        for n in range(len(cubes)):
            high, low = halves(mapped[n * size : (n + 1) * size])
            wide = dot(line_ref[...], high)
            results.append(wide[:size] + (wide[size:] + dot(line_ref[:size], low)))
        return results

    spectrum = transforms([values])[0].reshape(depth, group, plane)

    def scaled(multiplier):
        return (spectrum * multiplier[:, None, :]).reshape(size, plane)

    total = -values * transforms([scaled(loss_ref[...])])[0]

    def one(term, total):
        image_one, image_two = transforms([scaled(first_ref[term]), scaled(second_ref[term])])
        return total + image_one * image_two

    return lax.fori_loop(0, first_ref.shape[0], one, total)


def collide_kernel(cells_ref, *refs):
    depth, group, plane = cells_ref.shape
    out_ref = refs[-1]
    total = collision(cells_ref[...].reshape(depth * group, plane), refs[:-1], depth)
    out_ref[...] = total.reshape(depth, group, plane)


def swap_collide_kernel(
    cells_ref, first_ref, second_ref, loss_ref, plane_ref, line_ref, out_ref,
    first_cube, second_cube, loss_cube,
    got, result, sent_in, got_in, own_in, sent_out, got_out, own_out,
):
    parts = lax.axis_size("vel")
    blocks, planes, group, plane = cells_ref.shape
    chunks = blocks // parts
    me = lax.axis_index("vel")
    mesh_ids = pl.DeviceIdType.MESH
    peers = [lax.rem(me + n, parts) for n in range(parts)]
    tables = (first_cube, second_cube, loss_cube, plane_ref, line_ref)

    barrier = pltpu.get_barrier_semaphore()
    for peer in peers[1:]:
        pl.semaphore_signal(barrier, inc=1, device_id={"vel": peer}, device_id_type=mesh_ids)
    pl.semaphore_wait(barrier, parts - 1)

    def swap(chunk, from_ref, to_ref, send_sem, recv_sem, own_sem):
        mine = chunk * parts + me
        copies = []
        for n, peer in enumerate(peers):
            source = from_ref.at[chunk * parts + peer]
            if n == 0:
                copies.append(pltpu.make_async_copy(source, to_ref.at[mine], own_sem.at[chunk]))
            else:
                copies.append(
                    pltpu.make_async_remote_copy(
                        src_ref=source, dst_ref=to_ref.at[mine],
                        send_sem=send_sem.at[chunk, n], recv_sem=recv_sem.at[chunk, n],
                        device_id={"vel": peer}, device_id_type=mesh_ids,
                    )
                )
            copies[-1].start()
        return copies

    incoming = [swap(chunk, cells_ref, got, sent_in, got_in, own_in) for chunk in range(chunks)]
    for row in range(parts * planes):
        columns = slice(row * plane, (row + 1) * plane)
        for term in range(first_ref.shape[0]):
            first_cube[term, row : row + 1, :] = first_ref[term : term + 1, columns]
            second_cube[term, row : row + 1, :] = second_ref[term : term + 1, columns]
        loss_cube[row : row + 1, :] = loss_ref[:, columns]
    outgoing = []
    for chunk in range(chunks):
        for copy in incoming[chunk][1:]:
            copy.wait_recv()
        incoming[chunk][0].wait()
        held = slice(chunk * parts, (chunk + 1) * parts)
        values = got[held].reshape(parts * planes * group, plane)
        result[held] = collision(values, tables, parts * planes).reshape(parts, planes, group, plane)
        outgoing.append(swap(chunk, result, out_ref, sent_out, got_out, own_out))
    for copies in outgoing:
        copies[0].wait()
        for copy in copies[1:]:
            copy.wait_recv()
    for copies in incoming + outgoing:
        for copy in copies[1:]:
            copy.wait_send()


def hartley_tables(vdim):
    index = np.arange(vdim, dtype=np.float64)
    angle = 2.0 * np.pi * np.outer(index, index) / vdim
    table = (np.cos(angle) + np.sin(angle)) / np.sqrt(vdim)

    def split(wide):
        wide = wide.astype(np.float32)
        high = wide.astype(jnp.bfloat16)
        return np.stack([high, (wide - high.astype(np.float32)).astype(jnp.bfloat16)])

    return split(np.kron(table, table)), np.concatenate(split(np.kron(table, np.eye(GROUP))))


def collision_operands(gain_first, gain_second, loss_rates):
    plane_table, line_table = hartley_tables(VDIM)
    return gain_first, gain_second, loss_rates[None], jnp.asarray(plane_table), jnp.asarray(line_table)


def collide(cells, operands):
    depth, count, plane = cells.shape
    gain_first, gain_second, loss_rates = operands[:3]
    cube = (gain_first.shape[0], depth, plane)
    operands = (gain_first.reshape(cube), gain_second.reshape(cube), loss_rates.reshape(cube[1:])) + operands[3:]
    spare = -count % GROUP
    if spare:
        cells = jnp.pad(cells, ((0, 0), (0, spare), (0, 0)))
    cell_spec = pl.BlockSpec((depth, GROUP, plane), lambda n: (0, n, 0))

    def whole(shape):
        return pl.BlockSpec(shape, lambda n: (0,) * len(shape))

    result = pl.pallas_call(
        collide_kernel,
        grid=((count + spare) // GROUP,),
        in_specs=[cell_spec] + [whole(array.shape) for array in operands],
        out_specs=cell_spec,
        out_shape=jax.ShapeDtypeStruct(cells.shape, jnp.float32),
        compiler_params=pltpu.CompilerParams(vmem_limit_bytes=56 * 1024 * 1024),
    )(cells, *operands)
    return result[:, :count]


def swap_collide(cells, operands):
    chunks, parts = cells.shape[0] // lax.axis_size("vel"), lax.axis_size("vel")
    vmem = pl.BlockSpec(memory_space=pltpu.VMEM)
    across = pltpu.SemaphoreType.DMA((chunks, parts))
    own = pltpu.SemaphoreType.DMA((chunks,))
    cube = (VDIM, cells.shape[3])
    gains = pltpu.VMEM((operands[0].shape[0],) + cube, jnp.float32)
    return pl.pallas_call(
        swap_collide_kernel,
        in_specs=[vmem] * (1 + len(operands)),
        out_specs=vmem,
        out_shape=jax.ShapeDtypeStruct(cells.shape, jnp.float32),
        scratch_shapes=[gains, gains, pltpu.VMEM(cube, jnp.float32)]
        + [pltpu.VMEM(cells.shape, jnp.float32)] * 2
        + [across, across, own] * 2,
        compiler_params=pltpu.CompilerParams(
            collective_id=1, has_side_effects=True, vmem_limit_bytes=56 * 1024 * 1024
        ),
    )(cells, *operands)


def dht8(x):
    e = [x[n] + x[n + 4] for n in range(4)]
    o = [x[n] - x[n + 4] for n in range(4)]
    a, b = e[0] + e[2], e[0] - e[2]
    c, d = e[1] + e[3], e[1] - e[3]
    p, q = o[0] + o[2], o[0] - o[2]
    root = float(np.sqrt(2.0))
    r, s = root * o[1], root * o[3]
    return [a + c, p + r, b + d, q + s, a - c, p - r, b - d, q - s]


def dht24(x):
    plain, even, odd = [], [], []
    for n in range(8):
        x0, x1, x2 = x[(3 * n) % 24], x[(3 * n + 8) % 24], x[(3 * n + 16) % 24]
        total = x1 + x2
        plain.append(x0 + total)
        even.append(x0 - 0.5 * total)
        odd.append(float(np.sqrt(0.75)) * (x1 - x2))
    plain, even, odd = dht8(plain), dht8(even), dht8(odd)
    result = []
    for f in range(24):
        back = odd[-f % 8]
        result.append((plain[f % 8], even[f % 8] + back, even[f % 8] - back)[f % 3])
    return result


LAG = 2


def fused_kernel(
    near_ref, level_ref, x_ref, mask_ref, first_ref, second_ref, loss_ref, plane_ref, speed_ref, out_ref,
    u_ref, one_ref, two_ref, flux_one, flux_two, flux_turned, speeds, strips, from_left, from_right,
    pick, spread_back, table, first_cube, second_cube, loss_cube, lhs, mapped, spectrum, total,
    sent, got, result, back,
    sent_left, sent_right, got_left, got_right, sent_in, got_in, own_in, sent_out, got_out, own_out,
):
    tiles, count, lanes = u_ref.shape
    width = x_ref.shape[0]
    parts, each, wide = got.shape
    chunks = result.shape[0]
    plane = VDIM * VDIM
    planes = width // plane
    terms = first_ref.shape[0]
    me = lax.axis_index("vel")
    row = lax.axis_index("space")
    rows = lax.axis_size("space")
    has_left, has_right = row > 0, row < rows - 1
    left, right = lax.rem(row + rows - 1, rows), lax.rem(row + 1, rows)
    peers = [lax.rem(me + n, parts) for n in range(parts)]
    mesh_ids = pl.DeviceIdType.MESH
    fluxes = (flux_one, flux_two, flux_turned)

    barrier = pltpu.get_barrier_semaphore()

    @pl.when(has_left)
    def _():
        pl.semaphore_signal(barrier, inc=1, device_id={"space": left}, device_id_type=mesh_ids)

    @pl.when(has_right)
    def _():
        pl.semaphore_signal(barrier, inc=1, device_id={"space": right}, device_id_type=mesh_ids)

    for peer in peers[1:]:
        pl.semaphore_signal(barrier, inc=1, device_id={"vel": peer}, device_id_type=mesh_ids)

    ratio = courant * jnp.left_shift(1, level_ref[0]).astype(jnp.float32)
    source = []
    for face in range(4):
        for step in (-1, 0, 1):
            held = (near_ref[face] == row + step) & (near_ref[face] >= 0)
            source.append(jnp.where(held, 1.0, 0.0))

    half = (VDIM - 1) / 2.0
    start = (me * planes).astype(jnp.float32)
    toward = (speed_ref[:, 0, :] + start - half) / half
    across = speed_ref[:, 1, :]
    for n, value in enumerate(
        (jnp.abs(toward), jnp.abs(across), jnp.where(toward < 0, 1.0, 0.0), jnp.where(across < 0, 1.0, 0.0))
    ):
        speeds[:, n, :] = value
    full = width // lanes
    rest = width - full * lanes

    def turn(tile, carry):
        u_ref[tile] = x_ref[pl.ds(pl.multiple_of(tile * lanes, lanes), lanes), :].T
        return carry

    lax.fori_loop(0, full, turn, 0)
    if rest:
        u_ref[full] = jnp.zeros_like(u_ref[full])
        u_ref[full, :, :rest] = x_ref[full * lanes :, :].T

    pl.semaphore_wait(barrier, has_left.astype(jnp.int32) + has_right.astype(jnp.int32) + (parts - 1))

    def to_right(turn, tile):
        return pltpu.make_async_remote_copy(
            src_ref=strips.at[turn, tile], dst_ref=from_left.at[turn, tile],
            send_sem=sent_right.at[turn, tile], recv_sem=got_left.at[turn, tile],
            device_id={"space": right}, device_id_type=mesh_ids,
        )

    def to_left(turn, tile):
        return pltpu.make_async_remote_copy(
            src_ref=strips.at[turn, tile], dst_ref=from_right.at[turn, tile],
            send_sem=sent_left.at[turn, tile], recv_sem=got_right.at[turn, tile],
            device_id={"space": left}, device_id_type=mesh_ids,
        )

    def send(turn, tile, cells_ref):
        pack_strips(cells_ref.at[tile], *against_masks(speeds.at[tile]), strips.at[turn, tile])

        @pl.when(has_right)
        def _():
            to_right(turn, tile).start()

        @pl.when(has_left)
        def _():
            to_left(turn, tile).start()

    def receive(turn, tile):
        @pl.when(has_left)
        def _():
            to_right(turn, tile).wait_recv()

        @pl.when(has_right)
        def _():
            to_left(turn, tile).wait_recv()

    def begin(tile, carry):
        send(0, tile, u_ref)
        return carry

    lax.fori_loop(0, tiles, begin, 0)

    @pl.when(row == 0)
    def _():
        from_left[...] = jnp.zeros_like(from_left)

    @pl.when(row == rows - 1)
    def _():
        from_right[...] = jnp.zeros_like(from_right)

    marks = jnp.broadcast_to(mask_ref[...], (GROUP, count)).astype(jnp.float32)
    before = lax.broadcasted_iota(jnp.int32, (count, count), 0) < lax.broadcasted_iota(jnp.int32, (count, count), 1)
    rank = dot(marks.astype(jnp.bfloat16), jnp.where(before, 1.0, 0.0).astype(jnp.bfloat16))
    rank = jnp.where(marks > 0.5, rank, -1.0)[:1].astype(jnp.int32)
    slot = lax.broadcasted_iota(jnp.int32, (ACT, count), 0)
    hit = jnp.where(slot == rank, 1.0, 0.0).astype(jnp.bfloat16)
    pick[:, :count] = hit
    pick[:, count:] = hit
    inner = slot % (parts * GROUP)
    home = (inner // GROUP) * each + (slot // (parts * GROUP)) * GROUP + slot % GROUP
    hit = jnp.where(home == rank, 1.0, 0.0).T.astype(jnp.bfloat16)
    spread_back[:, :ACT] = hit
    spread_back[:, ACT:] = hit

    body = plane // 256 * 256
    tail = plane - body
    table[0:body] = plane_ref[0, :body]
    table[body : 2 * body] = plane_ref[0, :body]
    table[2 * body : 3 * body] = plane_ref[1, :body]
    at = 3 * body
    for part in (0, 0, 1):
        table[at : at + tail] = plane_ref[part, body:]
        at += tail
    if at < table.shape[0]:
        table[at:] = jnp.zeros_like(table[at:])
    for i in range(VDIM):
        columns = slice(i * plane, (i + 1) * plane)
        first_cube[i] = first_ref[:, columns]
        second_cube[i] = second_ref[:, columns]
        loss_cube[i : i + 1] = loss_ref[:, columns]

    def in_copy(tile, n):
        lane = pl.ds(pl.multiple_of(tile * lanes, lanes), lanes)
        if n == 0:
            return pltpu.make_async_copy(sent.at[tile, me], got.at[me, :, lane], own_in.at[tile])
        return pltpu.make_async_remote_copy(
            src_ref=sent.at[tile, peers[n]], dst_ref=got.at[me, :, lane],
            send_sem=sent_in.at[tile, n], recv_sem=got_in.at[tile, n],
            device_id={"vel": peers[n]}, device_id_type=mesh_ids,
        )

    def first(tile):
        receive(0, tile)
        advance(
            source, ratio, u_ref.at[tile], None, from_left.at[0, tile], from_right.at[0, tile],
            speeds.at[tile], one_ref.at[tile], fluxes,
        )
        send(1, tile, one_ref)

    def second(tile):
        receive(1, tile)
        advance(
            source, ratio, one_ref.at[tile], u_ref.at[tile], from_left.at[1, tile], from_right.at[1, tile],
            speeds.at[tile], two_ref.at[tile], fluxes,
        )
        high, low = halves(two_ref[tile])
        sent[tile] = dot(pick[...], jnp.concatenate([high, low], axis=0)).reshape(parts, each, lanes)
        for n in range(parts):
            in_copy(tile, n).start()

    def early(tile, carry):
        first(tile)
        return carry

    def steady(tile, carry):
        first(tile)
        second(tile - LAG)
        return carry

    def late(tile, carry):
        second(tile)
        return carry

    lax.fori_loop(0, LAG, early, 0)
    lax.fori_loop(LAG, tiles, steady, 0)
    lax.fori_loop(tiles - LAG, tiles, late, 0)

    def arrive(tile, carry):
        in_copy(tile, 0).wait()
        for n in range(1, parts):
            in_copy(tile, n).wait_recv()
        return carry

    lax.fori_loop(0, tiles, arrive, 0)

    def write_lhs(at, value):
        high, low = halves(value)
        span = slice(at, at + value.shape[0])
        lhs[span, :body] = high[:, :body]
        lhs[span, body : 2 * body] = low[:, :body]
        lhs[span, 2 * body : 3 * body] = high[:, :body]
        pieces = [high[:, body:], low[:, body:], high[:, body:]]
        spare = lhs.shape[1] - 3 * plane
        if spare:
            pieces.append(jnp.zeros((value.shape[0], spare), jnp.bfloat16))
        lhs[span, 3 * body :] = jnp.concatenate(pieces, axis=1)

    column_slices = [slice(c, min(c + LANES, plane)) for c in range(0, plane, LANES)]

    def transform(size):
        mapped[:size] = dot(lhs[:size], table[...])

    def line(columns, step, offset):
        return dht24(
            [mapped[i * step + offset : i * step + offset + GROUP, columns] for i in range(VDIM)]
        )

    def out_copy(chunk, n):
        if n == 0:
            return pltpu.make_async_copy(result.at[chunk, me], back.at[chunk, me], own_out.at[chunk])
        return pltpu.make_async_remote_copy(
            src_ref=result.at[chunk, peers[n]], dst_ref=back.at[chunk, me],
            send_sem=sent_out.at[chunk, n], recv_sem=got_out.at[chunk, n],
            device_id={"vel": peers[n]}, device_id_type=mesh_ids,
        )

    for chunk in range(chunks):
        cells = slice(chunk * GROUP, (chunk + 1) * GROUP)

        def cube(i):
            v, r = divmod(i, planes)
            return got[v, cells, r * plane : (r + 1) * plane]

        for i in range(0, VDIM, 2):
            pair = jnp.concatenate([cube(i), cube(i + 1)], axis=0)
            total[i * GROUP : (i + 2) * GROUP] = -pair
            write_lhs(i * GROUP, pair)
        transform(VDIM * GROUP)
        for columns in column_slices:
            for i, value in enumerate(line(columns, GROUP, 0)):
                spectrum[i * GROUP : (i + 1) * GROUP, columns] = value
        for i in range(0, VDIM, 2):
            pair = [
                spectrum[n * GROUP : (n + 1) * GROUP] * loss_cube[n : n + 1] for n in (i, i + 1)
            ]
            write_lhs(i * GROUP, jnp.concatenate(pair, axis=0))
        transform(VDIM * GROUP)
        for columns in column_slices:
            for i, value in enumerate(line(columns, GROUP, 0)):
                at = slice(i * GROUP, (i + 1) * GROUP)
                total[at, columns] = total[at, columns] * value

        def one(term, carry):
            for i in range(VDIM):
                value = spectrum[i * GROUP : (i + 1) * GROUP]
                pair = [value * cube_ref[i, pl.ds(term, 1), :] for cube_ref in (first_cube, second_cube)]
                write_lhs(i * 2 * GROUP, jnp.concatenate(pair, axis=0))
            transform(2 * VDIM * GROUP)
            for columns in column_slices:
                image_one = line(columns, 2 * GROUP, 0)
                image_two = line(columns, 2 * GROUP, GROUP)
                for i in range(VDIM):
                    at = slice(i * GROUP, (i + 1) * GROUP)
                    total[at, columns] += image_one[i] * image_two[i]
            return carry

        lax.fori_loop(0, terms, one, 0)
        for i in range(VDIM):
            v, r = divmod(i, planes)
            result[chunk, v, :, r * plane : (r + 1) * plane] = total[i * GROUP : (i + 1) * GROUP]
        for n in range(parts):
            out_copy(chunk, n).start()

    for chunk in range(chunks):
        out_copy(chunk, 0).wait()
        for n in range(1, parts):
            out_copy(chunk, n).wait_recv()

    def final(tile):
        lane = pl.ds(pl.multiple_of(tile * lanes, lanes), lanes)
        high, low = halves(back[:, :, :, lane].reshape(ACT, lanes))
        change = dot(spread_back[...], jnp.concatenate([high, low], axis=0))
        return (two_ref[tile] + change).T

    def finish(tile, carry):
        out_ref[pl.ds(pl.multiple_of(tile * lanes, lanes), lanes), :] = final(tile)
        return carry

    lax.fori_loop(0, full, finish, 0)
    if rest:
        out_ref[full * lanes :, :] = final(full)[:rest]

    def sent_all(tile, carry):
        for turn in range(2):

            @pl.when(has_right)
            def _():
                to_right(turn, tile).wait_send()

            @pl.when(has_left)
            def _():
                to_left(turn, tile).wait_send()

        for n in range(1, parts):
            in_copy(tile, n).wait_send()
        return carry

    lax.fori_loop(0, tiles, sent_all, 0)
    for chunk in range(chunks):
        for n in range(1, parts):
            out_copy(chunk, n).wait_send()


def fused_tables(width):
    plane = VDIM * VDIM
    tiles = -(-width // LANES)
    index = np.arange(tiles * LANES) % width
    half = (VDIM - 1) / 2.0
    speed = np.zeros((tiles, 8, LANES), np.float32)
    speed[:, 0] = (index // plane).reshape(tiles, LANES)
    second = ((index // VDIM % VDIM).astype(np.float32) - np.float32(half)) / np.float32(half)
    speed[:, 1] = second.reshape(tiles, LANES)
    grid = np.arange(VDIM, dtype=np.float64)
    angle = 2.0 * np.pi * np.outer(grid, grid) / VDIM
    line = (np.cos(angle) + np.sin(angle)) / np.sqrt(VDIM)
    wide = (np.kron(line, line) / np.sqrt(VDIM)).astype(np.float32)
    high = wide.astype(jnp.bfloat16)
    return speed, np.stack([high, (wide - high.astype(np.float32)).astype(jnp.bfloat16)])


def fused(distribution, neighbours, block_level, collide_mask, gain_first, gain_second, loss_rates):
    _, count, width = distribution.shape
    parts = lax.axis_size("vel")
    plane = VDIM * VDIM
    tiles = pl.cdiv(width, LANES)
    wide = tiles * LANES
    each = ACT // parts
    chunks = each // GROUP
    terms = gain_first.shape[0]
    depth = pl.cdiv(3 * plane, 256) * 256
    smem = pl.BlockSpec(memory_space=pltpu.SMEM)
    vmem = pl.BlockSpec(memory_space=pltpu.VMEM)
    speed, planes = fused_tables(width)
    f32, bf16 = jnp.float32, jnp.bfloat16
    strips = pltpu.VMEM((2, tiles, 10 * BSIDE, LANES), f32)
    dma = pltpu.SemaphoreType.DMA
    return pl.pallas_call(
        fused_kernel,
        in_specs=[smem, smem] + [vmem] * 7,
        out_specs=vmem,
        out_shape=jax.ShapeDtypeStruct((width, count), f32),
        scratch_shapes=[pltpu.VMEM((tiles, count, LANES), f32)] * 3
        + [pltpu.VMEM((count, LANES), f32)] * 3
        + [pltpu.VMEM((tiles, 8, LANES), f32)]
        + [strips] * 3
        + [pltpu.VMEM((ACT, 2 * count), bf16), pltpu.VMEM((count, 2 * ACT), bf16)]
        + [pltpu.VMEM((depth, plane), bf16)]
        + [pltpu.VMEM((VDIM, terms, plane), f32)] * 2
        + [pltpu.VMEM((VDIM, plane), f32)]
        + [pltpu.VMEM((2 * VDIM * GROUP, depth), bf16), pltpu.VMEM((2 * VDIM * GROUP, plane), f32)]
        + [pltpu.VMEM((VDIM * GROUP, plane), f32)] * 2
        + [pltpu.VMEM((tiles, parts, each, LANES), f32), pltpu.VMEM((parts, each, wide), f32)]
        + [pltpu.VMEM((chunks, parts, GROUP, wide), f32)] * 2
        + [dma((2, tiles))] * 4
        + [dma((tiles, parts)), dma((tiles, parts)), dma((tiles,))]
        + [dma((chunks, parts)), dma((chunks, parts)), dma((chunks,))],
        compiler_params=pltpu.CompilerParams(
            collective_id=2, has_side_effects=True, vmem_limit_bytes=60 * 1024 * 1024
        ),
    )(
        neighbours[0], block_level, distribution.reshape(count, width).T, collide_mask[None],
        gain_first, gain_second, loss_rates[None], jnp.asarray(planes), jnp.asarray(speed),
    )


def shards(
    distribution, neighbours, block_level, collide_mask, gain_first, gain_second, loss_rates
):
    blocks, cell_count, width = distribution.shape
    assert blocks == 1
    parts = lax.axis_size("vel")
    plane = VDIM * VDIM
    if width % plane == 0 and ACT % (parts * GROUP) == 0:
        cells = fused(
            distribution, neighbours, block_level, collide_mask, gain_first, gain_second, loss_rates
        )
        return cells.T.reshape(blocks, cell_count, width)
    density = distribution.reshape(cell_count, width)
    speeds = speed_rows(lax.axis_index("vel") * width, width)
    ratio = courant * jnp.exp2(block_level.astype(jnp.float32))
    offset = neighbours[0] - (lax.axis_index("space") - 1)
    source = (offset[:, None] == jnp.arange(3)) & (neighbours[0] >= 0)[:, None]
    source = source.astype(jnp.float32).reshape(-1)

    section_two = transport(source, ratio, tiled(density), tiled(speeds))

    parts = lax.axis_size("vel")
    each = ACT // parts
    cell_index = jnp.arange(cell_count)
    rank = jnp.sum(jnp.where(cell_index[:, None] < cell_index, collide_mask[:, None], 0), axis=0)
    hit = (rank[:, None] == jnp.arange(ACT)) & (collide_mask > 0)[:, None]
    chosen = jnp.sum(jnp.where(hit, cell_index[:, None], 0), axis=0)
    held = jnp.sum(collide_mask)[None]

    plane = VDIM * VDIM
    operands = collision_operands(gain_first, gain_second, loss_rates)
    if width % plane == 0 and each % GROUP == 0:
        sent = gather(chosen, section_two, (ACT // GROUP, width // plane, GROUP, plane))
        change = swap_collide(sent, operands)
    else:
        sent = gather(chosen, section_two, (parts, 1, each, width))
        got = lax.all_to_all(sent, "vel", split_axis=0, concat_axis=0, tiled=True)
        got = jnp.transpose(got.reshape(parts, each, width), (1, 0, 2))
        got = got.reshape(each, VDIM, plane).transpose(1, 0, 2)
        change = collide(got, operands).transpose(1, 0, 2).reshape(each, parts, width)
        change = change.transpose(1, 0, 2)[:, None]
        change = lax.all_to_all(change, "vel", split_axis=0, concat_axis=0, tiled=True)
    return scatter(chosen, held, section_two, change).reshape(blocks, cell_count, width)


def solution(mesh):
    in_specs = (P("space", None, "vel"), P("space", None), P("space"), P("space"), P(), P(), P())
    out_specs = P("space", None, "vel")
    return jax.shard_map(shards, mesh=mesh, in_specs=in_specs, out_specs=out_specs, check_vma=False)
```

```python
import functools

import jax
import jax.numpy as jnp
import numpy as np
from jax import lax
from jax.experimental import pallas as pl
from jax.experimental.pallas import tpu as pltpu
from jax.sharding import PartitionSpec as P

BSIDE = 16
VDIM = 24
ACT = 128
LANES = 128
GROUP = 8


weno_eps = 1e-06
courant = 0.2


def speed_rows(vel_start, vel_width):
    index = vel_start + jnp.arange(vel_width, dtype=jnp.int32)
    half = (VDIM - 1) / 2.0
    first = ((index // (VDIM * VDIM)).astype(jnp.float32) - half) / half
    second = ((index // VDIM % VDIM).astype(jnp.float32) - half) / half
    rows = [jnp.abs(first), jnp.abs(second), jnp.where(first < 0, 1.0, 0.0), jnp.where(second < 0, 1.0, 0.0)]
    return jnp.stack(rows + [jnp.zeros_like(first)] * 4)


def pack_strips(cells_ref, against_first, against_second, strips_ref):
    side = BSIDE

    def first(n):
        return cells_ref[n * side : (n + 1) * side]

    def second(n):
        return cells_ref[pl.ds(n, side, stride=side), :]

    at = 0
    for line, against in ((first, against_first), (second, against_second)):
        far = jnp.where(against, line(2), line(side - 3))
        for layer in (line(0), line(1), far, line(side - 2), line(side - 1)):
            strips_ref[at : at + side] = layer
            at += side


def sweep(line, against, speed, flux_ref):
    side = BSIDE

    def oriented(n):
        return jnp.where(against, line(side + 5 - n), line(n))

    values = [oriented(n) for n in range(4)]
    slopes = [values[n + 1] - values[n] for n in range(3)]
    bends = []
    for n in range(2):
        bend = slopes[n + 1] - slopes[n]
        bends.append(bend * bend * (13.0 / 3.0) + 4.0 * weno_eps)
    before = None
    for i in range(side + 1):
        values.append(oriented(i + 4))
        slopes.append(values[i + 4] - values[i + 3])
        bend = slopes[i + 3] - slopes[i + 2]
        bends.append(bend * bend * (13.0 / 3.0) + 4.0 * weno_eps)
        d0, d1, d2, d3 = slopes[i : i + 4]
        tilt_low = 3.0 * d1 - d0
        tilt_mid = d1 + d2
        tilt_high = d3 - 3.0 * d2
        rough_low = bends[i] + tilt_low * tilt_low
        rough_mid = bends[i + 1] + tilt_mid * tilt_mid
        rough_high = bends[i + 2] + tilt_high * tilt_high
        low2 = rough_low * rough_low
        mid2 = rough_mid * rough_mid
        high2 = rough_high * rough_high
        weight_low = mid2 * high2
        low3 = 3.0 * low2
        weight_mid = (low3 + low3) * high2
        weight_high = low3 * mid2
        guess_low = 5.0 * d1 - 2.0 * d0
        guess_mid = d1 + (d2 + d2)
        guess_high = 4.0 * d2 - d3
        above = weight_low * guess_low + weight_mid * guess_mid + weight_high * guess_high
        below = weight_low + weight_mid + weight_high
        edge = values[i + 2] + above / (6.0 * below)
        if before is not None:
            flux_ref[(i - 1) * side : i * side] = speed * (edge - before)
        before = edge


def advance(source_ref, ratio, u_ref, base_ref, left_ref, right_ref, speed_ref, out_ref, fluxes):
    side = BSIDE
    lanes = u_ref.shape[1]
    flux_one, flux_two, flux_turned = fluxes

    def first_line(n):
        return u_ref[n * side : (n + 1) * side]

    def second_line(n):
        return u_ref[pl.ds(n, side, stride=side), :]

    def ghost(face, block, own):
        at = block * side
        return (
            source_ref[3 * face] * left_ref[at : at + side]
            + source_ref[3 * face + 1] * own
            + source_ref[3 * face + 2] * right_ref[at : at + side]
        )

    def padded(line, faces, start):
        ghosts = {}
        for layer in range(3):
            ghosts[layer] = ghost(faces[0], start + 2 + layer, line(side - 3 + layer))
            ghosts[side + 3 + layer] = ghost(faces[1], start + layer, line(layer))
        return lambda n: ghosts[n] if n in ghosts else line(n - 3)

    against_first, against_second = against_masks(speed_ref)
    sweep(padded(first_line, (0, 1), 0), against_first, spread(speed_ref, 0), flux_one)
    sweep(padded(second_line, (2, 3), 5), against_second, spread(speed_ref, 1), flux_two)
    for n in range(side):
        back = side - 1 - n
        flux_turned[n * side : (n + 1) * side] = jnp.where(
            against_second, flux_two[back * side : (back + 1) * side], flux_two[n * side : (n + 1) * side]
        )
    for n in range(side):
        back = side - 1 - n
        rows = slice(n * side, (n + 1) * side)
        change = jnp.where(against_first, flux_one[back * side : (back + 1) * side], flux_one[rows])
        change = change + flux_turned[pl.ds(n, side, stride=side), :]
        moved = u_ref[rows] - ratio * change
        if base_ref is not None:
            moved = 0.5 * base_ref[rows] + 0.5 * moved
        out_ref[rows] = moved


def spread(speed_ref, row):
    return jnp.broadcast_to(speed_ref[row : row + 1], (BSIDE, speed_ref.shape[1]))


def against_masks(speed_ref):
    return spread(speed_ref, 2) > 0.5, spread(speed_ref, 3) > 0.5


def transport_kernel(
    source_ref, ratio_ref, u_ref, speed_ref, out_ref,
    one_ref, flux_one, flux_two, flux_turned,
    strips, from_left, from_right, sent_left, sent_right, got_left, got_right,
):
    tiles = u_ref.shape[0]
    me = lax.axis_index("space")
    count = lax.axis_size("space")
    has_left, has_right = me > 0, me < count - 1
    left, right = lax.rem(me + count - 1, count), lax.rem(me + 1, count)
    mesh_ids = pl.DeviceIdType.MESH
    ratio = ratio_ref[0]
    fluxes = (flux_one, flux_two, flux_turned)

    barrier = pltpu.get_barrier_semaphore()

    @pl.when(has_left)
    def _():
        pl.semaphore_signal(barrier, inc=1, device_id={"space": left}, device_id_type=mesh_ids)

    @pl.when(has_right)
    def _():
        pl.semaphore_signal(barrier, inc=1, device_id={"space": right}, device_id_type=mesh_ids)

    pl.semaphore_wait(barrier, has_left.astype(jnp.int32) + has_right.astype(jnp.int32))

    def to_right(turn, tile):
        return pltpu.make_async_remote_copy(
            src_ref=strips.at[turn, tile], dst_ref=from_left.at[turn, tile],
            send_sem=sent_right.at[turn, tile], recv_sem=got_left.at[turn, tile],
            device_id={"space": right}, device_id_type=mesh_ids,
        )

    def to_left(turn, tile):
        return pltpu.make_async_remote_copy(
            src_ref=strips.at[turn, tile], dst_ref=from_right.at[turn, tile],
            send_sem=sent_left.at[turn, tile], recv_sem=got_right.at[turn, tile],
            device_id={"space": left}, device_id_type=mesh_ids,
        )

    def send(turn, tile, cells_ref):
        pack_strips(cells_ref.at[tile], *against_masks(speed_ref.at[tile]), strips.at[turn, tile])

        @pl.when(has_right)
        def _():
            to_right(turn, tile).start()

        @pl.when(has_left)
        def _():
            to_left(turn, tile).start()

    def receive(turn, tile):
        @pl.when(has_left)
        def _():
            to_right(turn, tile).wait_recv()

        @pl.when(has_right)
        def _():
            to_left(turn, tile).wait_recv()

    def begin(tile, carry):
        send(0, tile, u_ref)
        return carry

    lax.fori_loop(0, tiles, begin, 0)

    @pl.when(me == 0)
    def _():
        from_left[...] = jnp.zeros_like(from_left)

    @pl.when(me == count - 1)
    def _():
        from_right[...] = jnp.zeros_like(from_right)

    def first(tile, carry):
        receive(0, tile)
        advance(
            source_ref, ratio, u_ref.at[tile], None, from_left.at[0, tile], from_right.at[0, tile],
            speed_ref.at[tile], one_ref.at[tile], fluxes,
        )
        send(1, tile, one_ref)
        return carry

    lax.fori_loop(0, tiles, first, 0)

    def second(tile, carry):
        receive(1, tile)
        advance(
            source_ref, ratio, one_ref.at[tile], u_ref.at[tile], from_left.at[1, tile], from_right.at[1, tile],
            speed_ref.at[tile], out_ref.at[tile], fluxes,
        )
        return carry

    lax.fori_loop(0, tiles, second, 0)

    def finish(tile, carry):
        for turn in range(2):

            @pl.when(has_right)
            def _():
                to_right(turn, tile).wait_send()

            @pl.when(has_left)
            def _():
                to_left(turn, tile).wait_send()

        return carry

    lax.fori_loop(0, tiles, finish, 0)


def transport(source, ratio, cells, speeds):
    tiles, count, lanes = cells.shape
    smem = pl.BlockSpec(memory_space=pltpu.SMEM)
    vmem = pl.BlockSpec(memory_space=pltpu.VMEM)
    strips = pltpu.VMEM((2, tiles, 10 * BSIDE, lanes), jnp.float32)
    return pl.pallas_call(
        transport_kernel,
        in_specs=[smem, smem, vmem, vmem],
        out_specs=vmem,
        out_shape=jax.ShapeDtypeStruct(cells.shape, jnp.float32),
        scratch_shapes=[pltpu.VMEM(cells.shape, jnp.float32)]
        + [pltpu.VMEM((count, lanes), jnp.float32)] * 3
        + [strips] * 3
        + [pltpu.SemaphoreType.DMA((2, tiles))] * 4,
        compiler_params=pltpu.CompilerParams(
            collective_id=0, has_side_effects=True, vmem_limit_bytes=48 * 1024 * 1024
        ),
    )(source, ratio, cells, speeds)


def tiled(rows):
    count, width = rows.shape
    tiles = pl.cdiv(width, LANES)
    rows = jnp.pad(rows, ((0, 0), (0, tiles * LANES - width)))
    return rows.reshape(count, tiles, LANES).transpose(1, 0, 2)


def lane_pieces(tiles, width):
    return [(t, t * LANES, min(width, (t + 1) * LANES)) for t in range(tiles)]


def gather_kernel(chosen_ref, cells_ref, out_ref, picked_ref, rows_ref):
    parts, planes, each, plane = out_ref.shape
    tiles = cells_ref.shape[0]

    def one(slot, carry):
        row = chosen_ref[slot]
        for tile in range(tiles):
            picked_ref[tile, pl.ds(slot, 1), :] = cells_ref[tile, pl.ds(row, 1), :]
        return carry

    lax.fori_loop(0, parts * each, one, 0, unroll=8)
    for tile in range(tiles):
        rows_ref[:, tile * LANES : (tile + 1) * LANES] = picked_ref[tile]
    for part in range(parts):
        for n in range(planes):
            out_ref[part, n] = rows_ref[part * each : (part + 1) * each, n * plane : (n + 1) * plane]


def gather(chosen, cells, shape):
    return pl.pallas_call(
        gather_kernel,
        in_specs=[pl.BlockSpec(memory_space=pltpu.SMEM), pl.BlockSpec(memory_space=pltpu.VMEM)],
        out_specs=pl.BlockSpec(memory_space=pltpu.VMEM),
        out_shape=jax.ShapeDtypeStruct(shape, jnp.float32),
        scratch_shapes=[
            pltpu.VMEM((cells.shape[0], shape[0] * shape[2], LANES), jnp.float32),
            pltpu.VMEM((shape[0] * shape[2], cells.shape[0] * LANES), jnp.float32),
        ],
    )(chosen, cells)


def scatter_kernel(chosen_ref, count_ref, cells_ref, change_ref, out_ref, rows_ref):
    parts, planes, each, plane = change_ref.shape
    for tile, begin, end in lane_pieces(cells_ref.shape[0], out_ref.shape[1]):
        out_ref[:, begin:end] = cells_ref[tile, :, : end - begin]
    for part in range(parts):
        for n in range(planes):
            rows_ref[part * each : (part + 1) * each, n * plane : (n + 1) * plane] = change_ref[part, n]

    def one(slot, carry):
        row = pl.ds(chosen_ref[slot], 1)
        out_ref[row, :] += rows_ref[pl.ds(slot, 1), :]
        return carry

    lax.fori_loop(0, count_ref[0], one, 0)


def scatter(chosen, count, cells, change):
    smem = pl.BlockSpec(memory_space=pltpu.SMEM)
    vmem = pl.BlockSpec(memory_space=pltpu.VMEM)
    parts, planes, each, plane = change.shape
    return pl.pallas_call(
        scatter_kernel,
        in_specs=[smem, smem, vmem, vmem],
        out_specs=vmem,
        out_shape=jax.ShapeDtypeStruct((cells.shape[1], planes * plane), jnp.float32),
        scratch_shapes=[pltpu.VMEM((parts * each, planes * plane), jnp.float32)],
    )(chosen, count, cells, change)


def halves(table):
    high = table.astype(jnp.bfloat16)
    low = (table - high.astype(jnp.float32)).astype(jnp.bfloat16)
    return high, low


def dot(left, right):
    return jnp.dot(left, right, preferred_element_type=jnp.float32)


def collision(values, tables, depth):
    first_ref, second_ref, loss_ref, plane_ref, line_ref = tables
    size, plane = values.shape
    group = size // depth

    def transforms(cubes):
        high, low = halves(jnp.concatenate(cubes, axis=0) if len(cubes) > 1 else cubes[0])
        rows = high.shape[0]
        wide = dot(jnp.concatenate([high, low], axis=0), plane_ref[0])
        mapped = wide[:rows] + (wide[rows:] + dot(high, plane_ref[1]))
        results = []
        for n in range(len(cubes)):
            high, low = halves(mapped[n * size : (n + 1) * size])
            wide = dot(line_ref[...], high)
            results.append(wide[:size] + (wide[size:] + dot(line_ref[:size], low)))
        return results

    spectrum = transforms([values])[0].reshape(depth, group, plane)

    def scaled(multiplier):
        return (spectrum * multiplier[:, None, :]).reshape(size, plane)

    total = -values * transforms([scaled(loss_ref[...])])[0]

    def one(term, total):
        image_one, image_two = transforms([scaled(first_ref[term]), scaled(second_ref[term])])
        return total + image_one * image_two

    return lax.fori_loop(0, first_ref.shape[0], one, total)


def collide_kernel(cells_ref, *refs):
    depth, group, plane = cells_ref.shape
    out_ref = refs[-1]
    total = collision(cells_ref[...].reshape(depth * group, plane), refs[:-1], depth)
    out_ref[...] = total.reshape(depth, group, plane)


def swap_collide_kernel(
    cells_ref, first_ref, second_ref, loss_ref, plane_ref, line_ref, out_ref,
    first_cube, second_cube, loss_cube,
    got, result, sent_in, got_in, own_in, sent_out, got_out, own_out,
):
    parts = lax.axis_size("vel")
    blocks, planes, group, plane = cells_ref.shape
    chunks = blocks // parts
    me = lax.axis_index("vel")
    mesh_ids = pl.DeviceIdType.MESH
    peers = [lax.rem(me + n, parts) for n in range(parts)]
    tables = (first_cube, second_cube, loss_cube, plane_ref, line_ref)

    barrier = pltpu.get_barrier_semaphore()
    for peer in peers[1:]:
        pl.semaphore_signal(barrier, inc=1, device_id={"vel": peer}, device_id_type=mesh_ids)
    pl.semaphore_wait(barrier, parts - 1)

    def swap(chunk, from_ref, to_ref, send_sem, recv_sem, own_sem):
        mine = chunk * parts + me
        copies = []
        for n, peer in enumerate(peers):
            source = from_ref.at[chunk * parts + peer]
            if n == 0:
                copies.append(pltpu.make_async_copy(source, to_ref.at[mine], own_sem.at[chunk]))
            else:
                copies.append(
                    pltpu.make_async_remote_copy(
                        src_ref=source, dst_ref=to_ref.at[mine],
                        send_sem=send_sem.at[chunk, n], recv_sem=recv_sem.at[chunk, n],
                        device_id={"vel": peer}, device_id_type=mesh_ids,
                    )
                )
            copies[-1].start()
        return copies

    incoming = [swap(chunk, cells_ref, got, sent_in, got_in, own_in) for chunk in range(chunks)]
    for row in range(parts * planes):
        columns = slice(row * plane, (row + 1) * plane)
        for term in range(first_ref.shape[0]):
            first_cube[term, row : row + 1, :] = first_ref[term : term + 1, columns]
            second_cube[term, row : row + 1, :] = second_ref[term : term + 1, columns]
        loss_cube[row : row + 1, :] = loss_ref[:, columns]
    outgoing = []
    for chunk in range(chunks):
        for copy in incoming[chunk][1:]:
            copy.wait_recv()
        incoming[chunk][0].wait()
        held = slice(chunk * parts, (chunk + 1) * parts)
        values = got[held].reshape(parts * planes * group, plane)
        result[held] = collision(values, tables, parts * planes).reshape(parts, planes, group, plane)
        outgoing.append(swap(chunk, result, out_ref, sent_out, got_out, own_out))
    for copies in outgoing:
        copies[0].wait()
        for copy in copies[1:]:
            copy.wait_recv()
    for copies in incoming + outgoing:
        for copy in copies[1:]:
            copy.wait_send()


def hartley_tables(vdim):
    index = np.arange(vdim, dtype=np.float64)
    angle = 2.0 * np.pi * np.outer(index, index) / vdim
    table = (np.cos(angle) + np.sin(angle)) / np.sqrt(vdim)

    def split(wide):
        wide = wide.astype(np.float32)
        high = wide.astype(jnp.bfloat16)
        return np.stack([high, (wide - high.astype(np.float32)).astype(jnp.bfloat16)])

    return split(np.kron(table, table)), np.concatenate(split(np.kron(table, np.eye(GROUP))))


def collision_operands(gain_first, gain_second, loss_rates):
    plane_table, line_table = hartley_tables(VDIM)
    return gain_first, gain_second, loss_rates[None], jnp.asarray(plane_table), jnp.asarray(line_table)


def collide(cells, operands):
    depth, count, plane = cells.shape
    gain_first, gain_second, loss_rates = operands[:3]
    cube = (gain_first.shape[0], depth, plane)
    operands = (gain_first.reshape(cube), gain_second.reshape(cube), loss_rates.reshape(cube[1:])) + operands[3:]
    spare = -count % GROUP
    if spare:
        cells = jnp.pad(cells, ((0, 0), (0, spare), (0, 0)))
    cell_spec = pl.BlockSpec((depth, GROUP, plane), lambda n: (0, n, 0))

    def whole(shape):
        return pl.BlockSpec(shape, lambda n: (0,) * len(shape))

    result = pl.pallas_call(
        collide_kernel,
        grid=((count + spare) // GROUP,),
        in_specs=[cell_spec] + [whole(array.shape) for array in operands],
        out_specs=cell_spec,
        out_shape=jax.ShapeDtypeStruct(cells.shape, jnp.float32),
        compiler_params=pltpu.CompilerParams(vmem_limit_bytes=56 * 1024 * 1024),
    )(cells, *operands)
    return result[:, :count]


def swap_collide(cells, operands):
    chunks, parts = cells.shape[0] // lax.axis_size("vel"), lax.axis_size("vel")
    vmem = pl.BlockSpec(memory_space=pltpu.VMEM)
    across = pltpu.SemaphoreType.DMA((chunks, parts))
    own = pltpu.SemaphoreType.DMA((chunks,))
    cube = (VDIM, cells.shape[3])
    gains = pltpu.VMEM((operands[0].shape[0],) + cube, jnp.float32)
    return pl.pallas_call(
        swap_collide_kernel,
        in_specs=[vmem] * (1 + len(operands)),
        out_specs=vmem,
        out_shape=jax.ShapeDtypeStruct(cells.shape, jnp.float32),
        scratch_shapes=[gains, gains, pltpu.VMEM(cube, jnp.float32)]
        + [pltpu.VMEM(cells.shape, jnp.float32)] * 2
        + [across, across, own] * 2,
        compiler_params=pltpu.CompilerParams(
            collective_id=1, has_side_effects=True, vmem_limit_bytes=56 * 1024 * 1024
        ),
    )(cells, *operands)


def dht8(x):
    e = [x[n] + x[n + 4] for n in range(4)]
    o = [x[n] - x[n + 4] for n in range(4)]
    a, b = e[0] + e[2], e[0] - e[2]
    c, d = e[1] + e[3], e[1] - e[3]
    p, q = o[0] + o[2], o[0] - o[2]
    root = float(np.sqrt(2.0))
    r, s = root * o[1], root * o[3]
    return [a + c, p + r, b + d, q + s, a - c, p - r, b - d, q - s]


def dht24(x):
    plain, even, odd = [], [], []
    for n in range(8):
        x0, x1, x2 = x[(3 * n) % 24], x[(3 * n + 8) % 24], x[(3 * n + 16) % 24]
        total = x1 + x2
        plain.append(x0 + total)
        even.append(x0 - 0.5 * total)
        odd.append(float(np.sqrt(0.75)) * (x1 - x2))
    plain, even, odd = dht8(plain), dht8(even), dht8(odd)
    result = []
    for f in range(24):
        back = odd[-f % 8]
        result.append((plain[f % 8], even[f % 8] + back, even[f % 8] - back)[f % 3])
    return result


LAG = 2
AHEAD = 3


def fused_kernel(
    near_hbm, level_hbm, x_hbm, mask_hbm, first_hbm, second_hbm, loss_hbm, plane_hbm, speed_hbm, out_ref,
    near_ref, level_ref, x_ref, mask_ref, first_ref, second_ref, loss_ref, plane_ref, speed_ref,
    u_ref, one_ref, two_ref, flux_one, flux_two, flux_turned, speeds, strips, from_left, from_right,
    pick, spread_back, table, first_cube, second_cube, loss_cube, lhs, mapped, spectrum, total,
    sent, got, result, back,
    sent_left, sent_right, got_left, got_right, sent_in, got_in, own_in, sent_out, got_out, own_out,
    x_here, here,
):
    tiles, count, lanes = u_ref.shape
    width = x_hbm.shape[0]
    parts, each, wide = got.shape
    chunks = result.shape[0]
    plane = VDIM * VDIM
    planes = width // plane
    terms = first_ref.shape[0]
    me = lax.axis_index("vel")
    row = lax.axis_index("space")
    rows = lax.axis_size("space")
    has_left, has_right = row > 0, row < rows - 1
    left, right = lax.rem(row + rows - 1, rows), lax.rem(row + 1, rows)
    peers = [lax.rem(me + n, parts) for n in range(parts)]
    mesh_ids = pl.DeviceIdType.MESH
    fluxes = (flux_one, flux_two, flux_turned)

    early_rows = AHEAD * lanes
    cells_here = [
        pltpu.make_async_copy(x_hbm.at[:early_rows], x_ref.at[:early_rows], x_here.at[0]),
        pltpu.make_async_copy(x_hbm.at[early_rows:], x_ref.at[early_rows:width], x_here.at[1]),
    ]
    near_here, level_here, mask_here, first_here, second_here, loss_here, plane_here, speed_here = [
        pltpu.make_async_copy(source, target, here.at[n])
        for n, (source, target) in enumerate(
            (
                (near_hbm, near_ref), (level_hbm, level_ref), (mask_hbm, mask_ref), (first_hbm, first_ref),
                (second_hbm, second_ref), (loss_hbm, loss_ref), (plane_hbm, plane_ref), (speed_hbm, speed_ref),
            )
        )
    ]
    speed_here.start()
    for copy in cells_here:
        copy.start()
    for copy in (near_here, level_here, mask_here, plane_here, first_here, second_here, loss_here):
        copy.start()

    barrier = pltpu.get_barrier_semaphore()

    @pl.when(has_left)
    def _():
        pl.semaphore_signal(barrier, inc=1, device_id={"space": left}, device_id_type=mesh_ids)

    @pl.when(has_right)
    def _():
        pl.semaphore_signal(barrier, inc=1, device_id={"space": right}, device_id_type=mesh_ids)

    for peer in peers[1:]:
        pl.semaphore_signal(barrier, inc=1, device_id={"vel": peer}, device_id_type=mesh_ids)

    speed_here.wait()
    half = (VDIM - 1) / 2.0
    start = (me * planes).astype(jnp.float32)
    toward = (speed_ref[:, 0, :] + start - half) / half
    across = speed_ref[:, 1, :]
    for n, value in enumerate(
        (jnp.abs(toward), jnp.abs(across), jnp.where(toward < 0, 1.0, 0.0), jnp.where(across < 0, 1.0, 0.0))
    ):
        speeds[:, n, :] = value
    full = width // lanes
    rest = width - full * lanes

    x_ref[width:] = jnp.zeros_like(x_ref[width:])

    pl.semaphore_wait(barrier, has_left.astype(jnp.int32) + has_right.astype(jnp.int32) + (parts - 1))

    def to_right(turn, tile):
        return pltpu.make_async_remote_copy(
            src_ref=strips.at[turn, tile], dst_ref=from_left.at[turn, tile],
            send_sem=sent_right.at[turn, tile], recv_sem=got_left.at[turn, tile],
            device_id={"space": right}, device_id_type=mesh_ids,
        )

    def to_left(turn, tile):
        return pltpu.make_async_remote_copy(
            src_ref=strips.at[turn, tile], dst_ref=from_right.at[turn, tile],
            send_sem=sent_left.at[turn, tile], recv_sem=got_right.at[turn, tile],
            device_id={"space": left}, device_id_type=mesh_ids,
        )

    def send(turn, tile, cells_ref):
        pack_strips(cells_ref.at[tile], *against_masks(speeds.at[tile]), strips.at[turn, tile])

        @pl.when(has_right)
        def _():
            to_right(turn, tile).start()

        @pl.when(has_left)
        def _():
            to_left(turn, tile).start()

    def receive(turn, tile):
        @pl.when(has_left)
        def _():
            to_right(turn, tile).wait_recv()

        @pl.when(has_right)
        def _():
            to_left(turn, tile).wait_recv()

    def launch(tile):
        u_ref[tile] = x_ref[pl.ds(pl.multiple_of(tile * lanes, lanes), lanes), :].T
        send(0, tile, u_ref)

    def begin(tile, carry):
        launch(tile)
        return carry

    cells_here[0].wait()
    lax.fori_loop(0, AHEAD, begin, 0)

    @pl.when(row == 0)
    def _():
        from_left[...] = jnp.zeros_like(from_left)

    @pl.when(row == rows - 1)
    def _():
        from_right[...] = jnp.zeros_like(from_right)

    near_here.wait()
    level_here.wait()
    ratio = courant * jnp.left_shift(1, level_ref[0]).astype(jnp.float32)
    source = []
    for face in range(4):
        for step in (-1, 0, 1):
            held = (near_ref[0, face] == row + step) & (near_ref[0, face] >= 0)
            source.append(jnp.where(held, 1.0, 0.0))
    mask_here.wait()
    marks = jnp.broadcast_to(mask_ref[...], (GROUP, count)).astype(jnp.float32)
    before = lax.broadcasted_iota(jnp.int32, (count, count), 0) < lax.broadcasted_iota(jnp.int32, (count, count), 1)
    rank = dot(marks.astype(jnp.bfloat16), jnp.where(before, 1.0, 0.0).astype(jnp.bfloat16))
    rank = jnp.where(marks > 0.5, rank, -1.0)[:1].astype(jnp.int32)
    slot = lax.broadcasted_iota(jnp.int32, (ACT, count), 0)
    hit = jnp.where(slot == rank, 1.0, 0.0).astype(jnp.bfloat16)
    pick[:, :count] = hit
    pick[:, count:] = hit
    slot = lax.broadcasted_iota(jnp.int32, (parts * GROUP, count), 0)
    for chunk in range(chunks):
        home = (slot // GROUP) * each + chunk * GROUP + slot % GROUP
        hit = jnp.where(home == rank, 1.0, 0.0).astype(jnp.bfloat16)
        spread_back[chunk, : parts * GROUP] = hit
        spread_back[chunk, parts * GROUP :] = hit

    for copy in (plane_here, first_here, second_here, loss_here, cells_here[1]):
        copy.wait()
    body = plane // 256 * 256
    tail = plane - body
    table[0:body] = plane_ref[0, :body]
    table[body : 2 * body] = plane_ref[0, :body]
    table[2 * body : 3 * body] = plane_ref[1, :body]
    at = 3 * body
    for part in (0, 0, 1):
        table[at : at + tail] = plane_ref[part, body:]
        at += tail
    if at < table.shape[0]:
        table[at:] = jnp.zeros_like(table[at:])
    for i in range(VDIM):
        columns = slice(i * plane, (i + 1) * plane)
        first_cube[i] = first_ref[:, columns]
        second_cube[i] = second_ref[:, columns]
        done = 0
        while done < plane:
            line_at, lane_at = divmod(i * plane + done, lanes)
            span = min(lanes - lane_at, plane - done)
            loss_cube[i : i + 1, done : done + span] = loss_ref[line_at : line_at + 1, lane_at : lane_at + span]
            done += span

    def in_copy(tile, n):
        lane = pl.ds(pl.multiple_of(tile * 2 * lanes, 2 * lanes), 2 * lanes)
        if n == 0:
            return pltpu.make_async_copy(sent.at[tile, me], got.at[me, :, lane], own_in.at[tile])
        return pltpu.make_async_remote_copy(
            src_ref=sent.at[tile, peers[n]], dst_ref=got.at[me, :, lane],
            send_sem=sent_in.at[tile, n], recv_sem=got_in.at[tile, n],
            device_id={"vel": peers[n]}, device_id_type=mesh_ids,
        )

    def first(tile):
        receive(0, tile)
        advance(
            source, ratio, u_ref.at[tile], None, from_left.at[0, tile], from_right.at[0, tile],
            speeds.at[tile], one_ref.at[tile], fluxes,
        )
        send(1, tile, one_ref)

    def second(tile):
        receive(1, tile)
        advance(
            source, ratio, one_ref.at[tile], u_ref.at[tile], from_left.at[1, tile], from_right.at[1, tile],
            speeds.at[tile], two_ref.at[tile], fluxes,
        )
        high, low = halves(two_ref[tile])
        picked = dot(pick[...], jnp.concatenate([high, low], axis=0)).reshape(parts, each, lanes)
        side = lax.rem(tile, 2)
        sent[tile // 2, :, :, pl.ds(pl.multiple_of(side * lanes, lanes), lanes)] = picked

        @pl.when(side == 1)
        def _():
            for n in range(parts):
                in_copy(tile // 2, n).start()

    def early(tile, carry):
        launch(tile + AHEAD)
        first(tile)
        return carry

    def steady(tile, carry):
        @pl.when(tile + AHEAD < tiles)
        def _():
            launch(tile + AHEAD)

        first(tile)
        second(tile - LAG)
        return carry

    def late(tile, carry):
        second(tile)
        return carry

    lax.fori_loop(0, LAG, early, 0)
    lax.fori_loop(LAG, tiles, steady, 0)
    lax.fori_loop(tiles - LAG, tiles, late, 0)

    def arrive(tile, carry):
        in_copy(tile, 0).wait()
        for n in range(1, parts):
            in_copy(tile, n).wait_recv()
        return carry

    lax.fori_loop(0, tiles // 2, arrive, 0)

    def write_lhs(at, value):
        high, low = halves(value)
        span = slice(at, at + value.shape[0])
        lhs[span, :body] = high[:, :body]
        lhs[span, body : 2 * body] = low[:, :body]
        lhs[span, 2 * body : 3 * body] = high[:, :body]
        pieces = [high[:, body:], low[:, body:], high[:, body:]]
        spare = lhs.shape[1] - 3 * plane
        if spare:
            pieces.append(jnp.zeros((value.shape[0], spare), jnp.bfloat16))
        lhs[span, 3 * body :] = jnp.concatenate(pieces, axis=1)

    column_slices = [slice(c, min(c + LANES, plane)) for c in range(0, plane, LANES)]

    def transform(size):
        mapped[:size] = dot(lhs[:size], table[...])

    def line(columns, step, offset):
        return dht24(
            [mapped[i * step + offset : i * step + offset + GROUP, columns] for i in range(VDIM)]
        )

    def out_copy(chunk, n):
        if n == 0:
            return pltpu.make_async_copy(result.at[chunk, me], back.at[chunk, me], own_out.at[chunk])
        return pltpu.make_async_remote_copy(
            src_ref=result.at[chunk, peers[n]], dst_ref=back.at[chunk, me],
            send_sem=sent_out.at[chunk, n], recv_sem=got_out.at[chunk, n],
            device_id={"vel": peers[n]}, device_id_type=mesh_ids,
        )

    for chunk in range(chunks):
        cells = slice(chunk * GROUP, (chunk + 1) * GROUP)

        def cube(i):
            v, r = divmod(i, planes)
            return got[v, cells, r * plane : (r + 1) * plane]

        for i in range(0, VDIM, 2):
            pair = jnp.concatenate([cube(i), cube(i + 1)], axis=0)
            total[i * GROUP : (i + 2) * GROUP] = -pair
            write_lhs(i * GROUP, pair)
        transform(VDIM * GROUP)
        for columns in column_slices:
            for i, value in enumerate(line(columns, GROUP, 0)):
                spectrum[i * GROUP : (i + 1) * GROUP, columns] = value
        for i in range(0, VDIM, 2):
            pair = [
                spectrum[n * GROUP : (n + 1) * GROUP] * loss_cube[n : n + 1] for n in (i, i + 1)
            ]
            write_lhs(i * GROUP, jnp.concatenate(pair, axis=0))
        transform(VDIM * GROUP)
        for columns in column_slices:
            for i, value in enumerate(line(columns, GROUP, 0)):
                at = slice(i * GROUP, (i + 1) * GROUP)
                total[at, columns] = total[at, columns] * value

        def one(term, carry):
            for i in range(VDIM):
                value = spectrum[i * GROUP : (i + 1) * GROUP]
                pair = [value * cube_ref[i, pl.ds(term, 1), :] for cube_ref in (first_cube, second_cube)]
                write_lhs(i * 2 * GROUP, jnp.concatenate(pair, axis=0))
            transform(2 * VDIM * GROUP)
            for columns in column_slices:
                image_one = line(columns, 2 * GROUP, 0)
                image_two = line(columns, 2 * GROUP, GROUP)
                for i in range(VDIM):
                    at = slice(i * GROUP, (i + 1) * GROUP)
                    total[at, columns] += image_one[i] * image_two[i]
            return carry

        lax.fori_loop(0, terms, one, 0)
        for i in range(VDIM):
            v, r = divmod(i, planes)
            result[chunk, v, :, r * plane : (r + 1) * plane] = total[i * GROUP : (i + 1) * GROUP]
        for n in range(parts):
            out_copy(chunk, n).start()

    def sent_all(tile, carry):
        for turn in range(2):

            @pl.when(has_right)
            def _():
                to_right(turn, tile).wait_send()

            @pl.when(has_left)
            def _():
                to_left(turn, tile).wait_send()

        return carry

    lax.fori_loop(0, tiles, sent_all, 0)

    def inward_sent(pair, carry):
        for n in range(1, parts):
            in_copy(pair, n).wait_send()
        return carry

    lax.fori_loop(0, tiles // 2, inward_sent, 0)

    held = parts * GROUP
    for chunk in range(chunks):
        last = chunk == chunks - 1
        out_copy(chunk, 0).wait()
        for n in range(1, parts):
            out_copy(chunk, n).wait_recv()

        def change(tile):
            at = tile * lanes if last else pl.multiple_of(tile * lanes, lanes)
            turned = back[chunk, :, :, pl.ds(at, lanes)].reshape(held, lanes).T
            high, low = halves(turned)
            return dot(jnp.concatenate([high, low], axis=1), spread_back[chunk])

        def settle(tile, carry):
            at = pl.ds(pl.multiple_of(tile * lanes, lanes), lanes)
            if chunk == 0:
                out_ref[at, :] = two_ref[tile].T + change(tile)
            else:
                out_ref[at, :] += change(tile)
            return carry

        if last and chunk > 0:
            for tile in range(full):
                out_ref[tile * lanes : (tile + 1) * lanes, :] += change(tile)
        else:
            lax.fori_loop(0, full, settle, 0)
        if rest:
            if chunk == 0:
                out_ref[full * lanes :, :] = (two_ref[full].T + change(full))[:rest]
            else:
                out_ref[full * lanes :, :] += change(full)[:rest]
        for n in range(1, parts):
            out_copy(chunk, n).wait_send()


def fused_tables(width):
    plane = VDIM * VDIM
    tiles = 2 * -(-width // (2 * LANES))
    index = np.arange(tiles * LANES) % width
    half = (VDIM - 1) / 2.0
    speed = np.zeros((tiles, 8, LANES), np.float32)
    speed[:, 0] = (index // plane).reshape(tiles, LANES)
    second = ((index // VDIM % VDIM).astype(np.float32) - np.float32(half)) / np.float32(half)
    speed[:, 1] = second.reshape(tiles, LANES)
    grid = np.arange(VDIM, dtype=np.float64)
    angle = 2.0 * np.pi * np.outer(grid, grid) / VDIM
    line = (np.cos(angle) + np.sin(angle)) / np.sqrt(VDIM)
    wide = (np.kron(line, line) / np.sqrt(VDIM)).astype(np.float32)
    high = wide.astype(jnp.bfloat16)
    return speed, np.stack([high, (wide - high.astype(np.float32)).astype(jnp.bfloat16)])


def fused(distribution, neighbours, block_level, collide_mask, gain_first, gain_second, loss_rates):
    _, count, width = distribution.shape
    parts = lax.axis_size("vel")
    plane = VDIM * VDIM
    tiles = 2 * pl.cdiv(width, 2 * LANES)
    wide = tiles * LANES
    each = ACT // parts
    chunks = each // GROUP
    terms = gain_first.shape[0]
    depth = pl.cdiv(3 * plane, 256) * 256
    smem, f32, bf16 = pltpu.SMEM, jnp.float32, jnp.bfloat16
    speed, planes = fused_tables(width)
    strips = pltpu.VMEM((2, tiles, 10 * BSIDE, LANES), f32)
    dma = pltpu.SemaphoreType.DMA
    return pl.pallas_call(
        fused_kernel,
        in_specs=[pl.BlockSpec(memory_space=pltpu.HBM)] * 9,
        out_specs=pl.BlockSpec(memory_space=pltpu.VMEM),
        out_shape=pltpu.VMEM((width, count), f32),
        scratch_shapes=[smem((1, 4), jnp.int32), smem((1,), jnp.int32), pltpu.VMEM((wide, count), f32)]
        + [pltpu.VMEM((1, count), jnp.int32)]
        + [pltpu.VMEM(gain_first.shape, f32)] * 2
        + [pltpu.VMEM((loss_rates.size // LANES, LANES), f32)]
        + [pltpu.VMEM(planes.shape, bf16), pltpu.VMEM(speed.shape, f32)]
        + [pltpu.VMEM((tiles, count, LANES), f32)] * 3
        + [pltpu.VMEM((count, LANES), f32)] * 3
        + [pltpu.VMEM((tiles, 8, LANES), f32)]
        + [strips] * 3
        + [pltpu.VMEM((ACT, 2 * count), bf16), pltpu.VMEM((chunks, 2 * parts * GROUP, count), bf16)]
        + [pltpu.VMEM((depth, plane), bf16)]
        + [pltpu.VMEM((VDIM, terms, plane), f32)] * 2
        + [pltpu.VMEM((VDIM, plane), f32)]
        + [pltpu.VMEM((2 * VDIM * GROUP, depth), bf16), pltpu.VMEM((2 * VDIM * GROUP, plane), f32)]
        + [pltpu.VMEM((VDIM * GROUP, plane), f32)] * 2
        + [pltpu.VMEM((tiles // 2, parts, each, 2 * LANES), f32), pltpu.VMEM((parts, each, wide), f32)]
        + [pltpu.VMEM((chunks, parts, GROUP, wide), f32)] * 2
        + [dma((2, tiles))] * 4
        + [dma((tiles // 2, parts)), dma((tiles // 2, parts)), dma((tiles // 2,))]
        + [dma((chunks, parts)), dma((chunks, parts)), dma((chunks,)), dma((2,)), dma((8,))],
        compiler_params=pltpu.CompilerParams(
            collective_id=2, has_side_effects=True, vmem_limit_bytes=56 * 1024 * 1024
        ),
    )(
        neighbours, block_level, distribution.reshape(count, width).T, collide_mask[None],
        gain_first, gain_second, loss_rates.reshape(-1, LANES), jnp.asarray(planes), jnp.asarray(speed),
    )


def shards(
    distribution, neighbours, block_level, collide_mask, gain_first, gain_second, loss_rates
):
    blocks, cell_count, width = distribution.shape
    assert blocks == 1
    parts = lax.axis_size("vel")
    plane = VDIM * VDIM
    if width % plane == 0 and ACT % (parts * GROUP) == 0:
        cells = fused(
            distribution, neighbours, block_level, collide_mask, gain_first, gain_second, loss_rates
        )
        return cells.T.reshape(blocks, cell_count, width)
    density = distribution.reshape(cell_count, width)
    speeds = speed_rows(lax.axis_index("vel") * width, width)
    ratio = courant * jnp.exp2(block_level.astype(jnp.float32))
    offset = neighbours[0] - (lax.axis_index("space") - 1)
    source = (offset[:, None] == jnp.arange(3)) & (neighbours[0] >= 0)[:, None]
    source = source.astype(jnp.float32).reshape(-1)

    section_two = transport(source, ratio, tiled(density), tiled(speeds))

    parts = lax.axis_size("vel")
    each = ACT // parts
    cell_index = jnp.arange(cell_count)
    rank = jnp.sum(jnp.where(cell_index[:, None] < cell_index, collide_mask[:, None], 0), axis=0)
    hit = (rank[:, None] == jnp.arange(ACT)) & (collide_mask > 0)[:, None]
    chosen = jnp.sum(jnp.where(hit, cell_index[:, None], 0), axis=0)
    held = jnp.sum(collide_mask)[None]

    plane = VDIM * VDIM
    operands = collision_operands(gain_first, gain_second, loss_rates)
    if width % plane == 0 and each % GROUP == 0:
        sent = gather(chosen, section_two, (ACT // GROUP, width // plane, GROUP, plane))
        change = swap_collide(sent, operands)
    else:
        sent = gather(chosen, section_two, (parts, 1, each, width))
        got = lax.all_to_all(sent, "vel", split_axis=0, concat_axis=0, tiled=True)
        got = jnp.transpose(got.reshape(parts, each, width), (1, 0, 2))
        got = got.reshape(each, VDIM, plane).transpose(1, 0, 2)
        change = collide(got, operands).transpose(1, 0, 2).reshape(each, parts, width)
        change = change.transpose(1, 0, 2)[:, None]
        change = lax.all_to_all(change, "vel", split_axis=0, concat_axis=0, tiled=True)
    return scatter(chosen, held, section_two, change).reshape(blocks, cell_count, width)


def solution(mesh):
    in_specs = (P("space", None, "vel"), P("space", None), P("space"), P("space"), P(), P(), P())
    out_specs = P("space", None, "vel")
    return jax.shard_map(shards, mesh=mesh, in_specs=in_specs, out_specs=out_specs, check_vma=False)
```

```python
import functools

import jax
import jax.numpy as jnp
import numpy as np
from jax import lax
from jax.experimental import pallas as pl
from jax.experimental.pallas import tpu as pltpu
from jax.sharding import PartitionSpec as P

BSIDE = 16
VDIM = 24
ACT = 128
LANES = 128
GROUP = 8


weno_eps = 1e-06
courant = 0.2


def speed_rows(vel_start, vel_width):
    index = vel_start + jnp.arange(vel_width, dtype=jnp.int32)
    half = (VDIM - 1) / 2.0
    first = ((index // (VDIM * VDIM)).astype(jnp.float32) - half) / half
    second = ((index // VDIM % VDIM).astype(jnp.float32) - half) / half
    rows = [jnp.abs(first), jnp.abs(second), jnp.where(first < 0, 1.0, 0.0), jnp.where(second < 0, 1.0, 0.0)]
    return jnp.stack(rows + [jnp.zeros_like(first)] * 4)


def pack_strips(cells_ref, against_first, against_second, strips_ref):
    side = BSIDE

    def first(n):
        return cells_ref[n * side : (n + 1) * side]

    def second(n):
        return cells_ref[pl.ds(n, side, stride=side), :]

    at = 0
    for line, against in ((first, against_first), (second, against_second)):
        far = jnp.where(against, line(2), line(side - 3))
        for layer in (line(0), line(1), far, line(side - 2), line(side - 1)):
            strips_ref[at : at + side] = layer
            at += side


def sweep(line, against, speed, flux_ref):
    side = BSIDE

    def oriented(n):
        return jnp.where(against, line(side + 5 - n), line(n))

    values = [oriented(n) for n in range(4)]
    slopes = [values[n + 1] - values[n] for n in range(3)]
    bends = []
    for n in range(2):
        bend = slopes[n + 1] - slopes[n]
        bends.append(bend * bend * (13.0 / 3.0) + 4.0 * weno_eps)
    before = None
    for i in range(side + 1):
        values.append(oriented(i + 4))
        slopes.append(values[i + 4] - values[i + 3])
        bend = slopes[i + 3] - slopes[i + 2]
        bends.append(bend * bend * (13.0 / 3.0) + 4.0 * weno_eps)
        d0, d1, d2, d3 = slopes[i : i + 4]
        tilt_low = 3.0 * d1 - d0
        tilt_mid = d1 + d2
        tilt_high = d3 - 3.0 * d2
        rough_low = bends[i] + tilt_low * tilt_low
        rough_mid = bends[i + 1] + tilt_mid * tilt_mid
        rough_high = bends[i + 2] + tilt_high * tilt_high
        low2 = rough_low * rough_low
        mid2 = rough_mid * rough_mid
        high2 = rough_high * rough_high
        weight_low = mid2 * high2
        low3 = 3.0 * low2
        weight_mid = (low3 + low3) * high2
        weight_high = low3 * mid2
        guess_low = 5.0 * d1 - 2.0 * d0
        guess_mid = d1 + (d2 + d2)
        guess_high = 4.0 * d2 - d3
        above = weight_low * guess_low + weight_mid * guess_mid + weight_high * guess_high
        below = weight_low + weight_mid + weight_high
        edge = values[i + 2] + above / (6.0 * below)
        if before is not None:
            flux_ref[(i - 1) * side : i * side] = speed * (edge - before)
        before = edge


def advance(source_ref, ratio, u_ref, base_ref, left_ref, right_ref, speed_ref, out_ref, fluxes):
    side = BSIDE
    lanes = u_ref.shape[1]
    flux_one, flux_two, flux_turned = fluxes

    def first_line(n):
        return u_ref[n * side : (n + 1) * side]

    def second_line(n):
        return u_ref[pl.ds(n, side, stride=side), :]

    def ghost(face, block, own):
        at = block * side
        return (
            source_ref[3 * face] * left_ref[at : at + side]
            + source_ref[3 * face + 1] * own
            + source_ref[3 * face + 2] * right_ref[at : at + side]
        )

    def padded(line, faces, start):
        ghosts = {}
        for layer in range(3):
            ghosts[layer] = ghost(faces[0], start + 2 + layer, line(side - 3 + layer))
            ghosts[side + 3 + layer] = ghost(faces[1], start + layer, line(layer))
        return lambda n: ghosts[n] if n in ghosts else line(n - 3)

    against_first, against_second = against_masks(speed_ref)
    sweep(padded(first_line, (0, 1), 0), against_first, spread(speed_ref, 0), flux_one)
    sweep(padded(second_line, (2, 3), 5), against_second, spread(speed_ref, 1), flux_two)
    for n in range(side):
        back = side - 1 - n
        flux_turned[n * side : (n + 1) * side] = jnp.where(
            against_second, flux_two[back * side : (back + 1) * side], flux_two[n * side : (n + 1) * side]
        )
    for n in range(side):
        back = side - 1 - n
        rows = slice(n * side, (n + 1) * side)
        change = jnp.where(against_first, flux_one[back * side : (back + 1) * side], flux_one[rows])
        change = change + flux_turned[pl.ds(n, side, stride=side), :]
        moved = u_ref[rows] - ratio * change
        if base_ref is not None:
            moved = 0.5 * base_ref[rows] + 0.5 * moved
        out_ref[rows] = moved


def spread(speed_ref, row):
    return jnp.broadcast_to(speed_ref[row : row + 1], (BSIDE, speed_ref.shape[1]))


def against_masks(speed_ref):
    return spread(speed_ref, 2) > 0.5, spread(speed_ref, 3) > 0.5


def transport_kernel(
    source_ref, ratio_ref, u_ref, speed_ref, out_ref,
    one_ref, flux_one, flux_two, flux_turned,
    strips, from_left, from_right, sent_left, sent_right, got_left, got_right,
):
    tiles = u_ref.shape[0]
    me = lax.axis_index("space")
    count = lax.axis_size("space")
    has_left, has_right = me > 0, me < count - 1
    left, right = lax.rem(me + count - 1, count), lax.rem(me + 1, count)
    mesh_ids = pl.DeviceIdType.MESH
    ratio = ratio_ref[0]
    fluxes = (flux_one, flux_two, flux_turned)

    barrier = pltpu.get_barrier_semaphore()

    @pl.when(has_left)
    def _():
        pl.semaphore_signal(barrier, inc=1, device_id={"space": left}, device_id_type=mesh_ids)

    @pl.when(has_right)
    def _():
        pl.semaphore_signal(barrier, inc=1, device_id={"space": right}, device_id_type=mesh_ids)

    pl.semaphore_wait(barrier, has_left.astype(jnp.int32) + has_right.astype(jnp.int32))

    def to_right(turn, tile):
        return pltpu.make_async_remote_copy(
            src_ref=strips.at[turn, tile], dst_ref=from_left.at[turn, tile],
            send_sem=sent_right.at[turn, tile], recv_sem=got_left.at[turn, tile],
            device_id={"space": right}, device_id_type=mesh_ids,
        )

    def to_left(turn, tile):
        return pltpu.make_async_remote_copy(
            src_ref=strips.at[turn, tile], dst_ref=from_right.at[turn, tile],
            send_sem=sent_left.at[turn, tile], recv_sem=got_right.at[turn, tile],
            device_id={"space": left}, device_id_type=mesh_ids,
        )

    def send(turn, tile, cells_ref):
        pack_strips(cells_ref.at[tile], *against_masks(speed_ref.at[tile]), strips.at[turn, tile])

        @pl.when(has_right)
        def _():
            to_right(turn, tile).start()

        @pl.when(has_left)
        def _():
            to_left(turn, tile).start()

    def receive(turn, tile):
        @pl.when(has_left)
        def _():
            to_right(turn, tile).wait_recv()

        @pl.when(has_right)
        def _():
            to_left(turn, tile).wait_recv()

    def begin(tile, carry):
        send(0, tile, u_ref)
        return carry

    lax.fori_loop(0, tiles, begin, 0)

    @pl.when(me == 0)
    def _():
        from_left[...] = jnp.zeros_like(from_left)

    @pl.when(me == count - 1)
    def _():
        from_right[...] = jnp.zeros_like(from_right)

    def first(tile, carry):
        receive(0, tile)
        advance(
            source_ref, ratio, u_ref.at[tile], None, from_left.at[0, tile], from_right.at[0, tile],
            speed_ref.at[tile], one_ref.at[tile], fluxes,
        )
        send(1, tile, one_ref)
        return carry

    lax.fori_loop(0, tiles, first, 0)

    def second(tile, carry):
        receive(1, tile)
        advance(
            source_ref, ratio, one_ref.at[tile], u_ref.at[tile], from_left.at[1, tile], from_right.at[1, tile],
            speed_ref.at[tile], out_ref.at[tile], fluxes,
        )
        return carry

    lax.fori_loop(0, tiles, second, 0)

    def finish(tile, carry):
        for turn in range(2):

            @pl.when(has_right)
            def _():
                to_right(turn, tile).wait_send()

            @pl.when(has_left)
            def _():
                to_left(turn, tile).wait_send()

        return carry

    lax.fori_loop(0, tiles, finish, 0)


def transport(source, ratio, cells, speeds):
    tiles, count, lanes = cells.shape
    smem = pl.BlockSpec(memory_space=pltpu.SMEM)
    vmem = pl.BlockSpec(memory_space=pltpu.VMEM)
    strips = pltpu.VMEM((2, tiles, 10 * BSIDE, lanes), jnp.float32)
    return pl.pallas_call(
        transport_kernel,
        in_specs=[smem, smem, vmem, vmem],
        out_specs=vmem,
        out_shape=jax.ShapeDtypeStruct(cells.shape, jnp.float32),
        scratch_shapes=[pltpu.VMEM(cells.shape, jnp.float32)]
        + [pltpu.VMEM((count, lanes), jnp.float32)] * 3
        + [strips] * 3
        + [pltpu.SemaphoreType.DMA((2, tiles))] * 4,
        compiler_params=pltpu.CompilerParams(
            collective_id=0, has_side_effects=True, vmem_limit_bytes=48 * 1024 * 1024
        ),
    )(source, ratio, cells, speeds)


def tiled(rows):
    count, width = rows.shape
    tiles = pl.cdiv(width, LANES)
    rows = jnp.pad(rows, ((0, 0), (0, tiles * LANES - width)))
    return rows.reshape(count, tiles, LANES).transpose(1, 0, 2)


def lane_pieces(tiles, width):
    return [(t, t * LANES, min(width, (t + 1) * LANES)) for t in range(tiles)]


def gather_kernel(chosen_ref, cells_ref, out_ref, picked_ref, rows_ref):
    parts, planes, each, plane = out_ref.shape
    tiles = cells_ref.shape[0]

    def one(slot, carry):
        row = chosen_ref[slot]
        for tile in range(tiles):
            picked_ref[tile, pl.ds(slot, 1), :] = cells_ref[tile, pl.ds(row, 1), :]
        return carry

    lax.fori_loop(0, parts * each, one, 0, unroll=8)
    for tile in range(tiles):
        rows_ref[:, tile * LANES : (tile + 1) * LANES] = picked_ref[tile]
    for part in range(parts):
        for n in range(planes):
            out_ref[part, n] = rows_ref[part * each : (part + 1) * each, n * plane : (n + 1) * plane]


def gather(chosen, cells, shape):
    return pl.pallas_call(
        gather_kernel,
        in_specs=[pl.BlockSpec(memory_space=pltpu.SMEM), pl.BlockSpec(memory_space=pltpu.VMEM)],
        out_specs=pl.BlockSpec(memory_space=pltpu.VMEM),
        out_shape=jax.ShapeDtypeStruct(shape, jnp.float32),
        scratch_shapes=[
            pltpu.VMEM((cells.shape[0], shape[0] * shape[2], LANES), jnp.float32),
            pltpu.VMEM((shape[0] * shape[2], cells.shape[0] * LANES), jnp.float32),
        ],
    )(chosen, cells)


def scatter_kernel(chosen_ref, count_ref, cells_ref, change_ref, out_ref, rows_ref):
    parts, planes, each, plane = change_ref.shape
    for tile, begin, end in lane_pieces(cells_ref.shape[0], out_ref.shape[1]):
        out_ref[:, begin:end] = cells_ref[tile, :, : end - begin]
    for part in range(parts):
        for n in range(planes):
            rows_ref[part * each : (part + 1) * each, n * plane : (n + 1) * plane] = change_ref[part, n]

    def one(slot, carry):
        row = pl.ds(chosen_ref[slot], 1)
        out_ref[row, :] += rows_ref[pl.ds(slot, 1), :]
        return carry

    lax.fori_loop(0, count_ref[0], one, 0)


def scatter(chosen, count, cells, change):
    smem = pl.BlockSpec(memory_space=pltpu.SMEM)
    vmem = pl.BlockSpec(memory_space=pltpu.VMEM)
    parts, planes, each, plane = change.shape
    return pl.pallas_call(
        scatter_kernel,
        in_specs=[smem, smem, vmem, vmem],
        out_specs=vmem,
        out_shape=jax.ShapeDtypeStruct((cells.shape[1], planes * plane), jnp.float32),
        scratch_shapes=[pltpu.VMEM((parts * each, planes * plane), jnp.float32)],
    )(chosen, count, cells, change)


def halves(table):
    high = table.astype(jnp.bfloat16)
    low = (table - high.astype(jnp.float32)).astype(jnp.bfloat16)
    return high, low


def dot(left, right):
    return jnp.dot(left, right, preferred_element_type=jnp.float32)


def collision(values, tables, depth):
    first_ref, second_ref, loss_ref, plane_ref, line_ref = tables
    size, plane = values.shape
    group = size // depth

    def transforms(cubes):
        high, low = halves(jnp.concatenate(cubes, axis=0) if len(cubes) > 1 else cubes[0])
        rows = high.shape[0]
        wide = dot(jnp.concatenate([high, low], axis=0), plane_ref[0])
        mapped = wide[:rows] + (wide[rows:] + dot(high, plane_ref[1]))
        results = []
        for n in range(len(cubes)):
            high, low = halves(mapped[n * size : (n + 1) * size])
            wide = dot(line_ref[...], high)
            results.append(wide[:size] + (wide[size:] + dot(line_ref[:size], low)))
        return results

    spectrum = transforms([values])[0].reshape(depth, group, plane)

    def scaled(multiplier):
        return (spectrum * multiplier[:, None, :]).reshape(size, plane)

    total = -values * transforms([scaled(loss_ref[...])])[0]

    def one(term, total):
        image_one, image_two = transforms([scaled(first_ref[term]), scaled(second_ref[term])])
        return total + image_one * image_two

    return lax.fori_loop(0, first_ref.shape[0], one, total)


def collide_kernel(cells_ref, *refs):
    depth, group, plane = cells_ref.shape
    out_ref = refs[-1]
    total = collision(cells_ref[...].reshape(depth * group, plane), refs[:-1], depth)
    out_ref[...] = total.reshape(depth, group, plane)


def swap_collide_kernel(
    cells_ref, first_ref, second_ref, loss_ref, plane_ref, line_ref, out_ref,
    first_cube, second_cube, loss_cube,
    got, result, sent_in, got_in, own_in, sent_out, got_out, own_out,
):
    parts = lax.axis_size("vel")
    blocks, planes, group, plane = cells_ref.shape
    chunks = blocks // parts
    me = lax.axis_index("vel")
    mesh_ids = pl.DeviceIdType.MESH
    peers = [lax.rem(me + n, parts) for n in range(parts)]
    tables = (first_cube, second_cube, loss_cube, plane_ref, line_ref)

    barrier = pltpu.get_barrier_semaphore()
    for peer in peers[1:]:
        pl.semaphore_signal(barrier, inc=1, device_id={"vel": peer}, device_id_type=mesh_ids)
    pl.semaphore_wait(barrier, parts - 1)

    def swap(chunk, from_ref, to_ref, send_sem, recv_sem, own_sem):
        mine = chunk * parts + me
        copies = []
        for n, peer in enumerate(peers):
            source = from_ref.at[chunk * parts + peer]
            if n == 0:
                copies.append(pltpu.make_async_copy(source, to_ref.at[mine], own_sem.at[chunk]))
            else:
                copies.append(
                    pltpu.make_async_remote_copy(
                        src_ref=source, dst_ref=to_ref.at[mine],
                        send_sem=send_sem.at[chunk, n], recv_sem=recv_sem.at[chunk, n],
                        device_id={"vel": peer}, device_id_type=mesh_ids,
                    )
                )
            copies[-1].start()
        return copies

    incoming = [swap(chunk, cells_ref, got, sent_in, got_in, own_in) for chunk in range(chunks)]
    for row in range(parts * planes):
        columns = slice(row * plane, (row + 1) * plane)
        for term in range(first_ref.shape[0]):
            first_cube[term, row : row + 1, :] = first_ref[term : term + 1, columns]
            second_cube[term, row : row + 1, :] = second_ref[term : term + 1, columns]
        loss_cube[row : row + 1, :] = loss_ref[:, columns]
    outgoing = []
    for chunk in range(chunks):
        for copy in incoming[chunk][1:]:
            copy.wait_recv()
        incoming[chunk][0].wait()
        held = slice(chunk * parts, (chunk + 1) * parts)
        values = got[held].reshape(parts * planes * group, plane)
        result[held] = collision(values, tables, parts * planes).reshape(parts, planes, group, plane)
        outgoing.append(swap(chunk, result, out_ref, sent_out, got_out, own_out))
    for copies in outgoing:
        copies[0].wait()
        for copy in copies[1:]:
            copy.wait_recv()
    for copies in incoming + outgoing:
        for copy in copies[1:]:
            copy.wait_send()


def hartley_tables(vdim):
    index = np.arange(vdim, dtype=np.float64)
    angle = 2.0 * np.pi * np.outer(index, index) / vdim
    table = (np.cos(angle) + np.sin(angle)) / np.sqrt(vdim)

    def split(wide):
        wide = wide.astype(np.float32)
        high = wide.astype(jnp.bfloat16)
        return np.stack([high, (wide - high.astype(np.float32)).astype(jnp.bfloat16)])

    return split(np.kron(table, table)), np.concatenate(split(np.kron(table, np.eye(GROUP))))


def collision_operands(gain_first, gain_second, loss_rates):
    plane_table, line_table = hartley_tables(VDIM)
    return gain_first, gain_second, loss_rates[None], jnp.asarray(plane_table), jnp.asarray(line_table)


def collide(cells, operands):
    depth, count, plane = cells.shape
    gain_first, gain_second, loss_rates = operands[:3]
    cube = (gain_first.shape[0], depth, plane)
    operands = (gain_first.reshape(cube), gain_second.reshape(cube), loss_rates.reshape(cube[1:])) + operands[3:]
    spare = -count % GROUP
    if spare:
        cells = jnp.pad(cells, ((0, 0), (0, spare), (0, 0)))
    cell_spec = pl.BlockSpec((depth, GROUP, plane), lambda n: (0, n, 0))

    def whole(shape):
        return pl.BlockSpec(shape, lambda n: (0,) * len(shape))

    result = pl.pallas_call(
        collide_kernel,
        grid=((count + spare) // GROUP,),
        in_specs=[cell_spec] + [whole(array.shape) for array in operands],
        out_specs=cell_spec,
        out_shape=jax.ShapeDtypeStruct(cells.shape, jnp.float32),
        compiler_params=pltpu.CompilerParams(vmem_limit_bytes=56 * 1024 * 1024),
    )(cells, *operands)
    return result[:, :count]


def swap_collide(cells, operands):
    chunks, parts = cells.shape[0] // lax.axis_size("vel"), lax.axis_size("vel")
    vmem = pl.BlockSpec(memory_space=pltpu.VMEM)
    across = pltpu.SemaphoreType.DMA((chunks, parts))
    own = pltpu.SemaphoreType.DMA((chunks,))
    cube = (VDIM, cells.shape[3])
    gains = pltpu.VMEM((operands[0].shape[0],) + cube, jnp.float32)
    return pl.pallas_call(
        swap_collide_kernel,
        in_specs=[vmem] * (1 + len(operands)),
        out_specs=vmem,
        out_shape=jax.ShapeDtypeStruct(cells.shape, jnp.float32),
        scratch_shapes=[gains, gains, pltpu.VMEM(cube, jnp.float32)]
        + [pltpu.VMEM(cells.shape, jnp.float32)] * 2
        + [across, across, own] * 2,
        compiler_params=pltpu.CompilerParams(
            collective_id=1, has_side_effects=True, vmem_limit_bytes=56 * 1024 * 1024
        ),
    )(cells, *operands)


def dht8(x):
    e = [x[n] + x[n + 4] for n in range(4)]
    o = [x[n] - x[n + 4] for n in range(4)]
    a, b = e[0] + e[2], e[0] - e[2]
    c, d = e[1] + e[3], e[1] - e[3]
    p, q = o[0] + o[2], o[0] - o[2]
    root = float(np.sqrt(2.0))
    r, s = root * o[1], root * o[3]
    return [a + c, p + r, b + d, q + s, a - c, p - r, b - d, q - s]


def dht24(x):
    plain, even, odd = [], [], []
    for n in range(8):
        x0, x1, x2 = x[(3 * n) % 24], x[(3 * n + 8) % 24], x[(3 * n + 16) % 24]
        total = x1 + x2
        plain.append(x0 + total)
        even.append(x0 - 0.5 * total)
        odd.append(float(np.sqrt(0.75)) * (x1 - x2))
    plain, even, odd = dht8(plain), dht8(even), dht8(odd)
    result = []
    for f in range(24):
        back = odd[-f % 8]
        result.append((plain[f % 8], even[f % 8] + back, even[f % 8] - back)[f % 3])
    return result


HALF = GROUP // 2
LAG = 2
AHEAD = 3


def fused_kernel(
    near_hbm, level_hbm, x_hbm, mask_hbm, first_hbm, second_hbm, loss_hbm, plane_hbm, speed_hbm, out_ref,
    near_ref, level_ref, x_ref, mask_ref, first_ref, second_ref, loss_ref, plane_ref, speed_ref,
    u_ref, one_ref, two_ref, turned, flux_one, flux_two, flux_turned, speeds, strips, from_left, from_right,
    pick, spread_back, table, first_cube, second_cube, gains, loss_cube, lhs, mapped, spectrum, doubled, loss, total, flat,
    sent, got, result, back,
    sent_left, sent_right, got_left, got_right, sent_in, got_in, own_in, sent_out, got_out, own_out,
    x_here, here,
):
    tiles, count, lanes = u_ref.shape
    width = x_hbm.shape[0]
    parts, each, wide = got.shape
    chunks = result.shape[0]
    plane = VDIM * VDIM
    planes = width // plane
    terms = first_ref.shape[0]
    me = lax.axis_index("vel")
    row = lax.axis_index("space")
    rows = lax.axis_size("space")
    has_left, has_right = row > 0, row < rows - 1
    left, right = lax.rem(row + rows - 1, rows), lax.rem(row + 1, rows)
    peers = [lax.rem(me + n, parts) for n in range(parts)]
    mesh_ids = pl.DeviceIdType.MESH
    fluxes = (flux_one, flux_two, flux_turned)

    early_rows = AHEAD * lanes
    cells_here = [
        pltpu.make_async_copy(x_hbm.at[:early_rows], x_ref.at[:early_rows], x_here.at[0]),
        pltpu.make_async_copy(x_hbm.at[early_rows:], x_ref.at[early_rows:width], x_here.at[1]),
    ]
    near_here, level_here, mask_here, first_here, second_here, loss_here, plane_here, speed_here = [
        pltpu.make_async_copy(source, target, here.at[n])
        for n, (source, target) in enumerate(
            (
                (near_hbm, near_ref), (level_hbm, level_ref), (mask_hbm, mask_ref), (first_hbm, first_ref),
                (second_hbm, second_ref), (loss_hbm, loss_ref), (plane_hbm, plane_ref), (speed_hbm, speed_ref),
            )
        )
    ]
    speed_here.start()
    for copy in cells_here:
        copy.start()
    for copy in (near_here, level_here, mask_here, plane_here, first_here, second_here, loss_here):
        copy.start()

    barrier = pltpu.get_barrier_semaphore()

    @pl.when(has_left)
    def _():
        pl.semaphore_signal(barrier, inc=1, device_id={"space": left}, device_id_type=mesh_ids)

    @pl.when(has_right)
    def _():
        pl.semaphore_signal(barrier, inc=1, device_id={"space": right}, device_id_type=mesh_ids)

    for peer in peers[1:]:
        pl.semaphore_signal(barrier, inc=1, device_id={"vel": peer}, device_id_type=mesh_ids)

    speed_here.wait()
    half = (VDIM - 1) / 2.0
    start = (me * planes).astype(jnp.float32)
    toward = (speed_ref[:, 0, :] + start - half) / half
    across = speed_ref[:, 1, :]
    for n, value in enumerate(
        (jnp.abs(toward), jnp.abs(across), jnp.where(toward < 0, 1.0, 0.0), jnp.where(across < 0, 1.0, 0.0))
    ):
        speeds[:, n, :] = value
    x_ref[width:] = jnp.zeros_like(x_ref[width:])

    pl.semaphore_wait(barrier, has_left.astype(jnp.int32) + has_right.astype(jnp.int32) + (parts - 1))

    def to_right(turn, tile):
        return pltpu.make_async_remote_copy(
            src_ref=strips.at[turn, tile], dst_ref=from_left.at[turn, tile],
            send_sem=sent_right.at[turn, tile], recv_sem=got_left.at[turn, tile],
            device_id={"space": right}, device_id_type=mesh_ids,
        )

    def to_left(turn, tile):
        return pltpu.make_async_remote_copy(
            src_ref=strips.at[turn, tile], dst_ref=from_right.at[turn, tile],
            send_sem=sent_left.at[turn, tile], recv_sem=got_right.at[turn, tile],
            device_id={"space": left}, device_id_type=mesh_ids,
        )

    def send(turn, tile, cells_ref):
        pack_strips(cells_ref.at[tile], *against_masks(speeds.at[tile]), strips.at[turn, tile])

        @pl.when(has_right)
        def _():
            to_right(turn, tile).start()

        @pl.when(has_left)
        def _():
            to_left(turn, tile).start()

    def receive(turn, tile):
        @pl.when(has_left)
        def _():
            to_right(turn, tile).wait_recv()

        @pl.when(has_right)
        def _():
            to_left(turn, tile).wait_recv()

    def launch(tile):
        u_ref[tile] = x_ref[pl.ds(pl.multiple_of(tile * lanes, lanes), lanes), :].T
        send(0, tile, u_ref)

    def begin(tile, carry):
        launch(tile)
        return carry

    cells_here[0].wait()
    lax.fori_loop(0, AHEAD, begin, 0)

    @pl.when(row == 0)
    def _():
        from_left[...] = jnp.zeros_like(from_left)

    @pl.when(row == rows - 1)
    def _():
        from_right[...] = jnp.zeros_like(from_right)

    near_here.wait()
    level_here.wait()
    ratio = courant * jnp.left_shift(1, level_ref[0]).astype(jnp.float32)
    source = []
    for face in range(4):
        for step in (-1, 0, 1):
            held = (near_ref[0, face] == row + step) & (near_ref[0, face] >= 0)
            source.append(jnp.where(held, 1.0, 0.0))
    mask_here.wait()
    marks = jnp.broadcast_to(mask_ref[...], (GROUP, count)).astype(jnp.float32)
    before = lax.broadcasted_iota(jnp.int32, (count, count), 0) < lax.broadcasted_iota(jnp.int32, (count, count), 1)
    rank = dot(marks.astype(jnp.bfloat16), jnp.where(before, 1.0, 0.0).astype(jnp.bfloat16))
    rank = jnp.where(marks > 0.5, rank, -1.0)[:1].astype(jnp.int32)
    slot = lax.broadcasted_iota(jnp.int32, (ACT, count), 0)
    hit = jnp.where(slot == rank, 1.0, 0.0).astype(jnp.bfloat16)
    pick[:, :count] = hit
    pick[:, count:] = hit
    held = parts * GROUP
    slot = lax.broadcasted_iota(jnp.int32, (held, count), 0)
    for chunk in range(chunks):
        home = (slot // GROUP) * each + chunk * HALF + slot % HALF
        for side in range(2):
            own = (home == rank) & (slot % GROUP // HALF == side)
            hit = jnp.where(own, 1.0, 0.0).astype(jnp.bfloat16)
            for at in (chunk % 2 * held, (2 + chunk % 2) * held):
                spread_back[chunk // 2, side, at : at + held] = hit

    for copy in (plane_here, first_here, second_here, loss_here, cells_here[1]):
        copy.wait()
    body = plane // 256 * 256
    tail = plane - body
    table[0:body] = plane_ref[0, :body]
    table[body : 2 * body] = plane_ref[0, :body]
    table[2 * body : 3 * body] = plane_ref[1, :body]
    at = 3 * body
    for part in (0, 0, 1):
        table[at : at + tail] = plane_ref[part, body:]
        at += tail
    if at < table.shape[0]:
        table[at:] = jnp.zeros_like(table[at:])
    for i in range(VDIM):
        columns = slice(i * plane, (i + 1) * plane)
        first_cube[i] = first_ref[:, columns]
        second_cube[i] = second_ref[:, columns]
        done = 0
        while done < plane:
            line_at, lane_at = divmod(i * plane + done, lanes)
            span = min(lanes - lane_at, plane - done)
            loss_cube[i : i + 1, done : done + span] = loss_ref[line_at : line_at + 1, lane_at : lane_at + span]
            done += span

    upper = lax.broadcasted_iota(jnp.int32, (GROUP, plane), 0) < HALF

    def lay(i, carry):
        for term in range(terms):
            one_row = jnp.broadcast_to(first_cube[i, term : term + 1, :], (GROUP, plane))
            two_row = jnp.broadcast_to(second_cube[i, term : term + 1, :], (GROUP, plane))
            gains[term, i] = jnp.where(upper, one_row, two_row)
        return carry

    lax.fori_loop(0, VDIM, lay, 0)

    def all_of(ref, sem):
        pltpu.make_async_copy(ref, ref, sem).wait()

    def in_copy(tile, n):
        lane = pl.ds(pl.multiple_of(tile * 2 * lanes, 2 * lanes), 2 * lanes)
        if n == 0:
            return pltpu.make_async_copy(sent.at[tile, me], got.at[me, :, lane], own_in.at[tile])
        return pltpu.make_async_remote_copy(
            src_ref=sent.at[tile, peers[n]], dst_ref=got.at[me, :, lane],
            send_sem=sent_in.at[tile], recv_sem=got_in.at[tile],
            device_id={"vel": peers[n]}, device_id_type=mesh_ids,
        )

    def first(tile):
        receive(0, tile)
        advance(
            source, ratio, u_ref.at[tile], None, from_left.at[0, tile], from_right.at[0, tile],
            speeds.at[tile], one_ref.at[tile], fluxes,
        )
        send(1, tile, one_ref)

    def second(tile):
        receive(1, tile)
        advance(
            source, ratio, one_ref.at[tile], u_ref.at[tile], from_left.at[1, tile], from_right.at[1, tile],
            speeds.at[tile], two_ref, fluxes,
        )
        turned[tile] = two_ref[...].T
        high, low = halves(two_ref[...])
        picked = dot(pick[...], jnp.concatenate([high, low], axis=0)).reshape(parts, each, lanes)
        side = lax.rem(tile, 2)
        sent[tile // 2, :, :, pl.ds(pl.multiple_of(side * lanes, lanes), lanes)] = picked

        @pl.when(side == 1)
        def _():
            for n in range(parts):
                in_copy(tile // 2, n).start()

    def early(tile, carry):
        launch(tile + AHEAD)
        first(tile)
        return carry

    def steady(tile, carry):
        @pl.when(tile + AHEAD < tiles)
        def _():
            launch(tile + AHEAD)

        first(tile)
        second(tile - LAG)
        return carry

    def late(tile, carry):
        second(tile)
        return carry

    lax.fori_loop(0, LAG, early, 0)
    lax.fori_loop(LAG, tiles, steady, 0)
    lax.fori_loop(tiles - LAG, tiles, late, 0)

    def arrive(tile, carry):
        in_copy(tile, 0).wait()
        all_of(got.at[1:, :, pl.ds(pl.multiple_of(tile * 2 * lanes, 2 * lanes), 2 * lanes)], got_in.at[tile])
        return carry

    lax.fori_loop(0, tiles // 2, arrive, 0)

    def write_lhs(at, value):
        high, low = halves(value)
        span = slice(at, at + value.shape[0])
        lhs[span, :body] = high[:, :body]
        lhs[span, body : 2 * body] = low[:, :body]
        lhs[span, 2 * body : 3 * body] = high[:, :body]
        pieces = [high[:, body:], low[:, body:], high[:, body:]]
        spare = lhs.shape[1] - 3 * plane
        if spare:
            pieces.append(jnp.zeros((value.shape[0], spare), jnp.bfloat16))
        lhs[span, 3 * body :] = jnp.concatenate(pieces, axis=1)

    column_slices = [slice(c, min(c + LANES, plane)) for c in range(0, plane, LANES)]

    def transform(size):
        mapped[:size] = dot(lhs[:size], table[...])

    def line(columns, many=1, n=0):
        starts = [(i * many + n) * GROUP for i in range(VDIM)]
        return dht24([mapped[at : at + GROUP, columns] for at in starts])

    def out_copy(chunk, n):
        if n == 0:
            return pltpu.make_async_copy(result.at[chunk, me], back.at[chunk, me], own_out.at[chunk])
        return pltpu.make_async_remote_copy(
            src_ref=result.at[chunk, peers[n]], dst_ref=back.at[chunk, me],
            send_sem=sent_out.at[chunk], recv_sem=got_out.at[chunk],
            device_id={"vel": peers[n]}, device_id_type=mesh_ids,
        )

    def double(value, half):
        other = pltpu.roll(value, HALF, 0)
        return jnp.where(upper, value, other) if half == 0 else jnp.where(upper, other, value)

    part = wide // 2
    for group in range(chunks // 2):
        cells = slice(group * GROUP, (group + 1) * GROUP)

        def cube(i):
            v, r = divmod(i, planes)
            return got[v, cells, r * plane : (r + 1) * plane]

        for i in range(0, VDIM, 2):
            pair = jnp.concatenate([cube(i), cube(i + 1)], axis=0)
            loss[i * GROUP : (i + 2) * GROUP] = -pair
            write_lhs(i * GROUP, pair)
        transform(VDIM * GROUP)
        for columns in column_slices:
            for i, value in enumerate(line(columns)):
                spectrum[i * GROUP : (i + 1) * GROUP, columns] = value
        for i in range(0, VDIM, 2):
            pair = [
                spectrum[n * GROUP : (n + 1) * GROUP] * loss_cube[n : n + 1] for n in (i, i + 1)
            ]
            write_lhs(i * GROUP, jnp.concatenate(pair, axis=0))
        transform(VDIM * GROUP)
        for columns in column_slices:
            for i, value in enumerate(line(columns)):
                at = slice(i * GROUP, (i + 1) * GROUP)
                loss[at, columns] = loss[at, columns] * value

        for half in range(2):
            chunk = 2 * group + half
            for i in range(VDIM):
                at = slice(i * GROUP, (i + 1) * GROUP)
                doubled[at] = double(spectrum[at], half)
                total[at] = double(loss[at], half)

            def some(step, carry):
                for i in range(VDIM):
                    value = doubled[i * GROUP : (i + 1) * GROUP]
                    pair = [value * gains[2 * step + n, i] for n in range(2)]
                    write_lhs(i * 2 * GROUP, jnp.concatenate(pair, axis=0))
                transform(2 * VDIM * GROUP)
                for columns in column_slices:
                    images = [line(columns, 2, n) for n in range(2)]
                    for i in range(VDIM):
                        at = slice(i * GROUP, (i + 1) * GROUP)
                        both = [image[i] * pltpu.roll(image[i], HALF, 0) for image in images]
                        total[at, columns] += both[0] + both[1]
                return carry

            lax.fori_loop(0, terms // 2, some, 0)
            low_rows = upper[:, :LANES]
            for v in range(parts):
                for r in range(planes):
                    i = v * planes + r
                    flat[v, :, r * plane : (r + 1) * plane] = total[i * GROUP : (i + 1) * GROUP]
                for at in range(0, part, LANES):
                    result[chunk, v, :, at : at + LANES] = jnp.where(
                        low_rows, flat[v, :, at : at + LANES], flat[v, :, part + at : part + at + LANES]
                    )
            for n in range(parts):
                out_copy(chunk, n).start()

    def sent_all(tile, carry):
        for turn in range(2):

            @pl.when(has_right)
            def _():
                to_right(turn, tile).wait_send()

            @pl.when(has_left)
            def _():
                to_left(turn, tile).wait_send()

        return carry

    lax.fori_loop(0, tiles, sent_all, 0)

    def inward_sent(pair, carry):
        all_of(sent.at[pair, 1:], sent_in.at[pair])
        return carry

    lax.fori_loop(0, tiles // 2, inward_sent, 0)

    half_tiles = tiles // 2
    for chunk in range(chunks - 1):
        all_of(result.at[chunk, 1:], sent_out.at[chunk])

    def change(pair, side, column):
        blocks = [
            back[chunk, :, :, pl.ds(column, lanes)].reshape(held, lanes) for chunk in (2 * pair, 2 * pair + 1)
        ]
        high, low = halves(jnp.concatenate(blocks, axis=0).T)
        return dot(jnp.concatenate([high, low], axis=1), spread_back[pair, side])

    pairs = chunks // 2
    for pair in range(pairs):
        for chunk in (2 * pair, 2 * pair + 1):
            out_copy(chunk, 0).wait()
            all_of(back.at[chunk, 1:], got_out.at[chunk])
        if pair < pairs - 1:
            for side in range(2):

                def settle(tile, carry):
                    column = pl.multiple_of(tile * lanes, lanes)
                    turned[side * half_tiles + tile] += change(pair, side, column)
                    return carry

                lax.fori_loop(0, half_tiles, settle, 0)
        else:
            for tile in range(tiles):
                side, column = divmod(tile, half_tiles)
                size = min(lanes, width - tile * lanes)
                if size > 0:
                    value = turned[tile] + change(pair, side, column * lanes)
                    out_ref[tile * lanes : tile * lanes + size, :] = value[:size]
    all_of(result.at[chunks - 1, 1:], sent_out.at[chunks - 1])


def fused_tables(width):
    plane = VDIM * VDIM
    tiles = 2 * -(-width // (2 * LANES))
    index = np.arange(tiles * LANES) % width
    half = (VDIM - 1) / 2.0
    speed = np.zeros((tiles, 8, LANES), np.float32)
    speed[:, 0] = (index // plane).reshape(tiles, LANES)
    second = ((index // VDIM % VDIM).astype(np.float32) - np.float32(half)) / np.float32(half)
    speed[:, 1] = second.reshape(tiles, LANES)
    grid = np.arange(VDIM, dtype=np.float64)
    angle = 2.0 * np.pi * np.outer(grid, grid) / VDIM
    line = (np.cos(angle) + np.sin(angle)) / np.sqrt(VDIM)
    wide = (np.kron(line, line) / np.sqrt(VDIM)).astype(np.float32)
    high = wide.astype(jnp.bfloat16)
    return speed, np.stack([high, (wide - high.astype(np.float32)).astype(jnp.bfloat16)])


def fused(distribution, neighbours, block_level, collide_mask, gain_first, gain_second, loss_rates):
    _, count, width = distribution.shape
    parts = lax.axis_size("vel")
    plane = VDIM * VDIM
    tiles = 2 * pl.cdiv(width, 2 * LANES)
    wide = tiles * LANES
    each = ACT // parts
    chunks = each // HALF
    assert gain_first.shape[0] % 2 == 0
    terms = gain_first.shape[0]
    depth = pl.cdiv(3 * plane, 256) * 256
    smem, f32, bf16 = pltpu.SMEM, jnp.float32, jnp.bfloat16
    speed, planes = fused_tables(width)
    strips = pltpu.VMEM((2, tiles, 10 * BSIDE, LANES), f32)
    dma = pltpu.SemaphoreType.DMA
    return pl.pallas_call(
        fused_kernel,
        in_specs=[pl.BlockSpec(memory_space=pltpu.HBM)] * 9,
        out_specs=pl.BlockSpec(memory_space=pltpu.VMEM),
        out_shape=pltpu.VMEM((width, count), f32),
        scratch_shapes=[smem((1, 4), jnp.int32), smem((1,), jnp.int32), pltpu.VMEM((wide, count), f32)]
        + [pltpu.VMEM((1, count), jnp.int32)]
        + [pltpu.VMEM(gain_first.shape, f32)] * 2
        + [pltpu.VMEM((loss_rates.size // LANES, LANES), f32)]
        + [pltpu.VMEM(planes.shape, bf16), pltpu.VMEM(speed.shape, f32)]
        + [pltpu.VMEM((tiles, count, LANES), f32)] * 2
        + [pltpu.VMEM((count, LANES), f32), pltpu.VMEM((tiles, LANES, count), f32)]
        + [pltpu.VMEM((count, LANES), f32)] * 3
        + [pltpu.VMEM((tiles, 8, LANES), f32)]
        + [strips] * 3
        + [pltpu.VMEM((ACT, 2 * count), bf16), pltpu.VMEM((chunks // 2, 2, 4 * parts * GROUP, count), bf16)]
        + [pltpu.VMEM((depth, plane), bf16)]
        + [pltpu.VMEM((VDIM, terms, plane), f32)] * 2
        + [pltpu.VMEM((terms, VDIM, GROUP, plane), f32), pltpu.VMEM((VDIM, plane), f32)]
        + [pltpu.VMEM((2 * VDIM * GROUP, depth), bf16), pltpu.VMEM((2 * VDIM * GROUP, plane), f32)]
        + [pltpu.VMEM((VDIM * GROUP, plane), f32)] * 4
        + [pltpu.VMEM((parts, GROUP, wide), f32)]
        + [pltpu.VMEM((tiles // 2, parts, each, 2 * LANES), f32), pltpu.VMEM((parts, each, wide), f32)]
        + [pltpu.VMEM((chunks, parts, GROUP, wide // 2), f32)] * 2
        + [dma((2, tiles))] * 4
        + [dma((tiles // 2,))] * 3
        + [dma((chunks,))] * 3 + [dma((2,)), dma((8,))],
        compiler_params=pltpu.CompilerParams(
            collective_id=2, has_side_effects=True, vmem_limit_bytes=56 * 1024 * 1024
        ),
    )(
        neighbours, block_level, distribution.reshape(count, width).T, collide_mask[None],
        gain_first, gain_second, loss_rates.reshape(-1, LANES), jnp.asarray(planes), jnp.asarray(speed),
    )


def shards(
    distribution, neighbours, block_level, collide_mask, gain_first, gain_second, loss_rates
):
    blocks, cell_count, width = distribution.shape
    assert blocks == 1
    parts = lax.axis_size("vel")
    plane = VDIM * VDIM
    if width % plane == 0 and ACT % (parts * GROUP) == 0:
        cells = fused(
            distribution, neighbours, block_level, collide_mask, gain_first, gain_second, loss_rates
        )
        return cells.T.reshape(blocks, cell_count, width)
    density = distribution.reshape(cell_count, width)
    speeds = speed_rows(lax.axis_index("vel") * width, width)
    ratio = courant * jnp.exp2(block_level.astype(jnp.float32))
    offset = neighbours[0] - (lax.axis_index("space") - 1)
    source = (offset[:, None] == jnp.arange(3)) & (neighbours[0] >= 0)[:, None]
    source = source.astype(jnp.float32).reshape(-1)

    section_two = transport(source, ratio, tiled(density), tiled(speeds))

    parts = lax.axis_size("vel")
    each = ACT // parts
    cell_index = jnp.arange(cell_count)
    rank = jnp.sum(jnp.where(cell_index[:, None] < cell_index, collide_mask[:, None], 0), axis=0)
    hit = (rank[:, None] == jnp.arange(ACT)) & (collide_mask > 0)[:, None]
    chosen = jnp.sum(jnp.where(hit, cell_index[:, None], 0), axis=0)
    held = jnp.sum(collide_mask)[None]

    plane = VDIM * VDIM
    operands = collision_operands(gain_first, gain_second, loss_rates)
    if width % plane == 0 and each % GROUP == 0:
        sent = gather(chosen, section_two, (ACT // GROUP, width // plane, GROUP, plane))
        change = swap_collide(sent, operands)
    else:
        sent = gather(chosen, section_two, (parts, 1, each, width))
        got = lax.all_to_all(sent, "vel", split_axis=0, concat_axis=0, tiled=True)
        got = jnp.transpose(got.reshape(parts, each, width), (1, 0, 2))
        got = got.reshape(each, VDIM, plane).transpose(1, 0, 2)
        change = collide(got, operands).transpose(1, 0, 2).reshape(each, parts, width)
        change = change.transpose(1, 0, 2)[:, None]
        change = lax.all_to_all(change, "vel", split_axis=0, concat_axis=0, tiled=True)
    return scatter(chosen, held, section_two, change).reshape(blocks, cell_count, width)


def solution(mesh):
    in_specs = (P("space", None, "vel"), P("space", None), P("space"), P("space"), P(), P(), P())
    out_specs = P("space", None, "vel")
    return jax.shard_map(shards, mesh=mesh, in_specs=in_specs, out_specs=out_specs, check_vma=False)
```

```python
import functools

import jax
import jax.numpy as jnp
import numpy as np
from jax import lax
from jax.experimental import pallas as pl
from jax.experimental.pallas import tpu as pltpu
from jax.sharding import PartitionSpec as P

BSIDE = 16
VDIM = 24
ACT = 128
LANES = 128
GROUP = 8


weno_eps = 1e-06
courant = 0.2


def speed_rows(vel_start, vel_width):
    index = vel_start + jnp.arange(vel_width, dtype=jnp.int32)
    half = (VDIM - 1) / 2.0
    first = ((index // (VDIM * VDIM)).astype(jnp.float32) - half) / half
    second = ((index // VDIM % VDIM).astype(jnp.float32) - half) / half
    rows = [jnp.abs(first), jnp.abs(second), jnp.where(first < 0, 1.0, 0.0), jnp.where(second < 0, 1.0, 0.0)]
    return jnp.stack(rows + [jnp.zeros_like(first)] * 4)


def pack_strips(cells_ref, against_first, against_second, strips_ref):
    side = BSIDE

    def first(n):
        return cells_ref[n * side : (n + 1) * side]

    def second(n):
        return cells_ref[pl.ds(n, side, stride=side), :]

    at = 0
    for line, against in ((first, against_first), (second, against_second)):
        far = jnp.where(against, line(2), line(side - 3))
        for layer in (line(0), line(1), far, line(side - 2), line(side - 1)):
            strips_ref[at : at + side] = layer
            at += side


def sweep(line, against, speed, flux_ref):
    side = BSIDE

    def oriented(n):
        return jnp.where(against, line(side + 5 - n), line(n))

    values = [oriented(n) for n in range(4)]
    slopes = [values[n + 1] - values[n] for n in range(3)]
    bends = []
    for n in range(2):
        bend = slopes[n + 1] - slopes[n]
        bends.append(bend * bend * (13.0 / 3.0) + 4.0 * weno_eps)
    before = None
    for i in range(side + 1):
        values.append(oriented(i + 4))
        slopes.append(values[i + 4] - values[i + 3])
        bend = slopes[i + 3] - slopes[i + 2]
        bends.append(bend * bend * (13.0 / 3.0) + 4.0 * weno_eps)
        d0, d1, d2, d3 = slopes[i : i + 4]
        tilt_low = 3.0 * d1 - d0
        tilt_mid = d1 + d2
        tilt_high = d3 - 3.0 * d2
        rough_low = bends[i] + tilt_low * tilt_low
        rough_mid = bends[i + 1] + tilt_mid * tilt_mid
        rough_high = bends[i + 2] + tilt_high * tilt_high
        low2 = rough_low * rough_low
        mid2 = rough_mid * rough_mid
        high2 = rough_high * rough_high
        weight_low = mid2 * high2
        low3 = 3.0 * low2
        weight_mid = (low3 + low3) * high2
        weight_high = low3 * mid2
        guess_low = 5.0 * d1 - 2.0 * d0
        guess_mid = d1 + (d2 + d2)
        guess_high = 4.0 * d2 - d3
        above = weight_low * guess_low + weight_mid * guess_mid + weight_high * guess_high
        below = weight_low + weight_mid + weight_high
        edge = values[i + 2] + above / (6.0 * below)
        if before is not None:
            flux_ref[(i - 1) * side : i * side] = speed * (edge - before)
        before = edge


def advance(source_ref, ratio, u_ref, base_ref, edge_of, speed_ref, out_ref, fluxes):
    side = BSIDE
    lanes = u_ref.shape[1]
    flux_one, flux_two, flux_turned = fluxes

    def first_line(n):
        return u_ref[n * side : (n + 1) * side]

    def second_line(n):
        return u_ref[pl.ds(n, side, stride=side), :]

    def ghost(face, block, own):
        return (
            source_ref[3 * face] * edge_of(0, block)
            + source_ref[3 * face + 1] * own
            + source_ref[3 * face + 2] * edge_of(1, block)
        )

    def padded(line, faces, start):
        ghosts = {}
        for layer in range(3):
            ghosts[layer] = ghost(faces[0], start + 2 + layer, line(side - 3 + layer))
            ghosts[side + 3 + layer] = ghost(faces[1], start + layer, line(layer))
        return lambda n: ghosts[n] if n in ghosts else line(n - 3)

    against_first, against_second = against_masks(speed_ref)
    sweep(padded(first_line, (0, 1), 0), against_first, spread(speed_ref, 0), flux_one)
    sweep(padded(second_line, (2, 3), 5), against_second, spread(speed_ref, 1), flux_two)
    for n in range(side):
        back = side - 1 - n
        flux_turned[n * side : (n + 1) * side] = jnp.where(
            against_second, flux_two[back * side : (back + 1) * side], flux_two[n * side : (n + 1) * side]
        )
    for n in range(side):
        back = side - 1 - n
        rows = slice(n * side, (n + 1) * side)
        change = jnp.where(against_first, flux_one[back * side : (back + 1) * side], flux_one[rows])
        change = change + flux_turned[pl.ds(n, side, stride=side), :]
        moved = u_ref[rows] - ratio * change
        if base_ref is not None:
            moved = 0.5 * base_ref[rows] + 0.5 * moved
        out_ref[rows] = moved


def spread(speed_ref, row):
    return jnp.broadcast_to(speed_ref[row : row + 1], (BSIDE, speed_ref.shape[1]))


def against_masks(speed_ref):
    return spread(speed_ref, 2) > 0.5, spread(speed_ref, 3) > 0.5


def plain_edges(left_ref, right_ref):
    return lambda n, block: (left_ref, right_ref)[n][block * BSIDE : (block + 1) * BSIDE]


def transport_kernel(
    source_ref, ratio_ref, u_ref, speed_ref, out_ref,
    one_ref, flux_one, flux_two, flux_turned,
    strips, from_left, from_right, sent_left, sent_right, got_left, got_right,
):
    tiles = u_ref.shape[0]
    me = lax.axis_index("space")
    count = lax.axis_size("space")
    has_left, has_right = me > 0, me < count - 1
    left, right = lax.rem(me + count - 1, count), lax.rem(me + 1, count)
    mesh_ids = pl.DeviceIdType.MESH
    ratio = ratio_ref[0]
    fluxes = (flux_one, flux_two, flux_turned)

    barrier = pltpu.get_barrier_semaphore()

    @pl.when(has_left)
    def _():
        pl.semaphore_signal(barrier, inc=1, device_id={"space": left}, device_id_type=mesh_ids)

    @pl.when(has_right)
    def _():
        pl.semaphore_signal(barrier, inc=1, device_id={"space": right}, device_id_type=mesh_ids)

    pl.semaphore_wait(barrier, has_left.astype(jnp.int32) + has_right.astype(jnp.int32))

    def to_right(turn, tile):
        return pltpu.make_async_remote_copy(
            src_ref=strips.at[turn, tile], dst_ref=from_left.at[turn, tile],
            send_sem=sent_right.at[turn, tile], recv_sem=got_left.at[turn, tile],
            device_id={"space": right}, device_id_type=mesh_ids,
        )

    def to_left(turn, tile):
        return pltpu.make_async_remote_copy(
            src_ref=strips.at[turn, tile], dst_ref=from_right.at[turn, tile],
            send_sem=sent_left.at[turn, tile], recv_sem=got_right.at[turn, tile],
            device_id={"space": left}, device_id_type=mesh_ids,
        )

    def send(turn, tile, cells_ref):
        pack_strips(cells_ref.at[tile], *against_masks(speed_ref.at[tile]), strips.at[turn, tile])

        @pl.when(has_right)
        def _():
            to_right(turn, tile).start()

        @pl.when(has_left)
        def _():
            to_left(turn, tile).start()

    def receive(turn, tile):
        @pl.when(has_left)
        def _():
            to_right(turn, tile).wait_recv()

        @pl.when(has_right)
        def _():
            to_left(turn, tile).wait_recv()

    def begin(tile, carry):
        send(0, tile, u_ref)
        return carry

    lax.fori_loop(0, tiles, begin, 0)

    @pl.when(me == 0)
    def _():
        from_left[...] = jnp.zeros_like(from_left)

    @pl.when(me == count - 1)
    def _():
        from_right[...] = jnp.zeros_like(from_right)

    def first(tile, carry):
        receive(0, tile)
        advance(
            source_ref, ratio, u_ref.at[tile], None, plain_edges(from_left.at[0, tile], from_right.at[0, tile]),
            speed_ref.at[tile], one_ref.at[tile], fluxes,
        )
        send(1, tile, one_ref)
        return carry

    lax.fori_loop(0, tiles, first, 0)

    def second(tile, carry):
        receive(1, tile)
        advance(
            source_ref, ratio, one_ref.at[tile], u_ref.at[tile], plain_edges(from_left.at[1, tile], from_right.at[1, tile]),
            speed_ref.at[tile], out_ref.at[tile], fluxes,
        )
        return carry

    lax.fori_loop(0, tiles, second, 0)

    def finish(tile, carry):
        for turn in range(2):

            @pl.when(has_right)
            def _():
                to_right(turn, tile).wait_send()

            @pl.when(has_left)
            def _():
                to_left(turn, tile).wait_send()

        return carry

    lax.fori_loop(0, tiles, finish, 0)


def transport(source, ratio, cells, speeds):
    tiles, count, lanes = cells.shape
    smem = pl.BlockSpec(memory_space=pltpu.SMEM)
    vmem = pl.BlockSpec(memory_space=pltpu.VMEM)
    strips = pltpu.VMEM((2, tiles, 10 * BSIDE, lanes), jnp.float32)
    return pl.pallas_call(
        transport_kernel,
        in_specs=[smem, smem, vmem, vmem],
        out_specs=vmem,
        out_shape=jax.ShapeDtypeStruct(cells.shape, jnp.float32),
        scratch_shapes=[pltpu.VMEM(cells.shape, jnp.float32)]
        + [pltpu.VMEM((count, lanes), jnp.float32)] * 3
        + [strips] * 3
        + [pltpu.SemaphoreType.DMA((2, tiles))] * 4,
        compiler_params=pltpu.CompilerParams(
            collective_id=0, has_side_effects=True, vmem_limit_bytes=48 * 1024 * 1024
        ),
    )(source, ratio, cells, speeds)


def tiled(rows):
    count, width = rows.shape
    tiles = pl.cdiv(width, LANES)
    rows = jnp.pad(rows, ((0, 0), (0, tiles * LANES - width)))
    return rows.reshape(count, tiles, LANES).transpose(1, 0, 2)


def lane_pieces(tiles, width):
    return [(t, t * LANES, min(width, (t + 1) * LANES)) for t in range(tiles)]


def gather_kernel(chosen_ref, cells_ref, out_ref, picked_ref, rows_ref):
    parts, planes, each, plane = out_ref.shape
    tiles = cells_ref.shape[0]

    def one(slot, carry):
        row = chosen_ref[slot]
        for tile in range(tiles):
            picked_ref[tile, pl.ds(slot, 1), :] = cells_ref[tile, pl.ds(row, 1), :]
        return carry

    lax.fori_loop(0, parts * each, one, 0, unroll=8)
    for tile in range(tiles):
        rows_ref[:, tile * LANES : (tile + 1) * LANES] = picked_ref[tile]
    for part in range(parts):
        for n in range(planes):
            out_ref[part, n] = rows_ref[part * each : (part + 1) * each, n * plane : (n + 1) * plane]


def gather(chosen, cells, shape):
    return pl.pallas_call(
        gather_kernel,
        in_specs=[pl.BlockSpec(memory_space=pltpu.SMEM), pl.BlockSpec(memory_space=pltpu.VMEM)],
        out_specs=pl.BlockSpec(memory_space=pltpu.VMEM),
        out_shape=jax.ShapeDtypeStruct(shape, jnp.float32),
        scratch_shapes=[
            pltpu.VMEM((cells.shape[0], shape[0] * shape[2], LANES), jnp.float32),
            pltpu.VMEM((shape[0] * shape[2], cells.shape[0] * LANES), jnp.float32),
        ],
    )(chosen, cells)


def scatter_kernel(chosen_ref, count_ref, cells_ref, change_ref, out_ref, rows_ref):
    parts, planes, each, plane = change_ref.shape
    for tile, begin, end in lane_pieces(cells_ref.shape[0], out_ref.shape[1]):
        out_ref[:, begin:end] = cells_ref[tile, :, : end - begin]
    for part in range(parts):
        for n in range(planes):
            rows_ref[part * each : (part + 1) * each, n * plane : (n + 1) * plane] = change_ref[part, n]

    def one(slot, carry):
        row = pl.ds(chosen_ref[slot], 1)
        out_ref[row, :] += rows_ref[pl.ds(slot, 1), :]
        return carry

    lax.fori_loop(0, count_ref[0], one, 0)


def scatter(chosen, count, cells, change):
    smem = pl.BlockSpec(memory_space=pltpu.SMEM)
    vmem = pl.BlockSpec(memory_space=pltpu.VMEM)
    parts, planes, each, plane = change.shape
    return pl.pallas_call(
        scatter_kernel,
        in_specs=[smem, smem, vmem, vmem],
        out_specs=vmem,
        out_shape=jax.ShapeDtypeStruct((cells.shape[1], planes * plane), jnp.float32),
        scratch_shapes=[pltpu.VMEM((parts * each, planes * plane), jnp.float32)],
    )(chosen, count, cells, change)


def halves(table):
    high = table.astype(jnp.bfloat16)
    low = (table - high.astype(jnp.float32)).astype(jnp.bfloat16)
    return high, low


def dot(left, right):
    return jnp.dot(left, right, preferred_element_type=jnp.float32)


def collision(values, tables, depth):
    first_ref, second_ref, loss_ref, plane_ref, line_ref = tables
    size, plane = values.shape
    group = size // depth

    def transforms(cubes):
        high, low = halves(jnp.concatenate(cubes, axis=0) if len(cubes) > 1 else cubes[0])
        rows = high.shape[0]
        wide = dot(jnp.concatenate([high, low], axis=0), plane_ref[0])
        mapped = wide[:rows] + (wide[rows:] + dot(high, plane_ref[1]))
        results = []
        for n in range(len(cubes)):
            high, low = halves(mapped[n * size : (n + 1) * size])
            wide = dot(line_ref[...], high)
            results.append(wide[:size] + (wide[size:] + dot(line_ref[:size], low)))
        return results

    spectrum = transforms([values])[0].reshape(depth, group, plane)

    def scaled(multiplier):
        return (spectrum * multiplier[:, None, :]).reshape(size, plane)

    total = -values * transforms([scaled(loss_ref[...])])[0]

    def one(term, total):
        image_one, image_two = transforms([scaled(first_ref[term]), scaled(second_ref[term])])
        return total + image_one * image_two

    return lax.fori_loop(0, first_ref.shape[0], one, total)


def collide_kernel(cells_ref, *refs):
    depth, group, plane = cells_ref.shape
    out_ref = refs[-1]
    total = collision(cells_ref[...].reshape(depth * group, plane), refs[:-1], depth)
    out_ref[...] = total.reshape(depth, group, plane)


def swap_collide_kernel(
    cells_ref, first_ref, second_ref, loss_ref, plane_ref, line_ref, out_ref,
    first_cube, second_cube, loss_cube,
    got, result, sent_in, got_in, own_in, sent_out, got_out, own_out,
):
    parts = lax.axis_size("vel")
    blocks, planes, group, plane = cells_ref.shape
    chunks = blocks // parts
    me = lax.axis_index("vel")
    mesh_ids = pl.DeviceIdType.MESH
    peers = [lax.rem(me + n, parts) for n in range(parts)]
    tables = (first_cube, second_cube, loss_cube, plane_ref, line_ref)

    barrier = pltpu.get_barrier_semaphore()
    for peer in peers[1:]:
        pl.semaphore_signal(barrier, inc=1, device_id={"vel": peer}, device_id_type=mesh_ids)
    pl.semaphore_wait(barrier, parts - 1)

    def swap(chunk, from_ref, to_ref, send_sem, recv_sem, own_sem):
        mine = chunk * parts + me
        copies = []
        for n, peer in enumerate(peers):
            source = from_ref.at[chunk * parts + peer]
            if n == 0:
                copies.append(pltpu.make_async_copy(source, to_ref.at[mine], own_sem.at[chunk]))
            else:
                copies.append(
                    pltpu.make_async_remote_copy(
                        src_ref=source, dst_ref=to_ref.at[mine],
                        send_sem=send_sem.at[chunk, n], recv_sem=recv_sem.at[chunk, n],
                        device_id={"vel": peer}, device_id_type=mesh_ids,
                    )
                )
            copies[-1].start()
        return copies

    incoming = [swap(chunk, cells_ref, got, sent_in, got_in, own_in) for chunk in range(chunks)]
    for row in range(parts * planes):
        columns = slice(row * plane, (row + 1) * plane)
        for term in range(first_ref.shape[0]):
            first_cube[term, row : row + 1, :] = first_ref[term : term + 1, columns]
            second_cube[term, row : row + 1, :] = second_ref[term : term + 1, columns]
        loss_cube[row : row + 1, :] = loss_ref[:, columns]
    outgoing = []
    for chunk in range(chunks):
        for copy in incoming[chunk][1:]:
            copy.wait_recv()
        incoming[chunk][0].wait()
        held = slice(chunk * parts, (chunk + 1) * parts)
        values = got[held].reshape(parts * planes * group, plane)
        result[held] = collision(values, tables, parts * planes).reshape(parts, planes, group, plane)
        outgoing.append(swap(chunk, result, out_ref, sent_out, got_out, own_out))
    for copies in outgoing:
        copies[0].wait()
        for copy in copies[1:]:
            copy.wait_recv()
    for copies in incoming + outgoing:
        for copy in copies[1:]:
            copy.wait_send()


def hartley_tables(vdim):
    index = np.arange(vdim, dtype=np.float64)
    angle = 2.0 * np.pi * np.outer(index, index) / vdim
    table = (np.cos(angle) + np.sin(angle)) / np.sqrt(vdim)

    def split(wide):
        wide = wide.astype(np.float32)
        high = wide.astype(jnp.bfloat16)
        return np.stack([high, (wide - high.astype(np.float32)).astype(jnp.bfloat16)])

    return split(np.kron(table, table)), np.concatenate(split(np.kron(table, np.eye(GROUP))))


def collision_operands(gain_first, gain_second, loss_rates):
    plane_table, line_table = hartley_tables(VDIM)
    return gain_first, gain_second, loss_rates[None], jnp.asarray(plane_table), jnp.asarray(line_table)


def collide(cells, operands):
    depth, count, plane = cells.shape
    gain_first, gain_second, loss_rates = operands[:3]
    cube = (gain_first.shape[0], depth, plane)
    operands = (gain_first.reshape(cube), gain_second.reshape(cube), loss_rates.reshape(cube[1:])) + operands[3:]
    spare = -count % GROUP
    if spare:
        cells = jnp.pad(cells, ((0, 0), (0, spare), (0, 0)))
    cell_spec = pl.BlockSpec((depth, GROUP, plane), lambda n: (0, n, 0))

    def whole(shape):
        return pl.BlockSpec(shape, lambda n: (0,) * len(shape))

    result = pl.pallas_call(
        collide_kernel,
        grid=((count + spare) // GROUP,),
        in_specs=[cell_spec] + [whole(array.shape) for array in operands],
        out_specs=cell_spec,
        out_shape=jax.ShapeDtypeStruct(cells.shape, jnp.float32),
        compiler_params=pltpu.CompilerParams(vmem_limit_bytes=56 * 1024 * 1024),
    )(cells, *operands)
    return result[:, :count]


def swap_collide(cells, operands):
    chunks, parts = cells.shape[0] // lax.axis_size("vel"), lax.axis_size("vel")
    vmem = pl.BlockSpec(memory_space=pltpu.VMEM)
    across = pltpu.SemaphoreType.DMA((chunks, parts))
    own = pltpu.SemaphoreType.DMA((chunks,))
    cube = (VDIM, cells.shape[3])
    gains = pltpu.VMEM((operands[0].shape[0],) + cube, jnp.float32)
    return pl.pallas_call(
        swap_collide_kernel,
        in_specs=[vmem] * (1 + len(operands)),
        out_specs=vmem,
        out_shape=jax.ShapeDtypeStruct(cells.shape, jnp.float32),
        scratch_shapes=[gains, gains, pltpu.VMEM(cube, jnp.float32)]
        + [pltpu.VMEM(cells.shape, jnp.float32)] * 2
        + [across, across, own] * 2,
        compiler_params=pltpu.CompilerParams(
            collective_id=1, has_side_effects=True, vmem_limit_bytes=56 * 1024 * 1024
        ),
    )(cells, *operands)


def dht8(x):
    e = [x[n] + x[n + 4] for n in range(4)]
    o = [x[n] - x[n + 4] for n in range(4)]
    a, b = e[0] + e[2], e[0] - e[2]
    c, d = e[1] + e[3], e[1] - e[3]
    p, q = o[0] + o[2], o[0] - o[2]
    root = float(np.sqrt(2.0))
    r, s = root * o[1], root * o[3]
    return [a + c, p + r, b + d, q + s, a - c, p - r, b - d, q - s]


def dht24(x):
    plain, even, odd = [], [], []
    for n in range(8):
        x0, x1, x2 = x[(3 * n) % 24], x[(3 * n + 8) % 24], x[(3 * n + 16) % 24]
        total = x1 + x2
        plain.append(x0 + total)
        even.append(x0 - 0.5 * total)
        odd.append(float(np.sqrt(0.75)) * (x1 - x2))
    plain, even, odd = dht8(plain), dht8(even), dht8(odd)
    result = []
    for f in range(24):
        back = odd[-f % 8]
        result.append((plain[f % 8], even[f % 8] + back, even[f % 8] - back)[f % 3])
    return result


HALF = GROUP // 2
LAG = 2
AHEAD = 3


INSET = 2
INNER = BSIDE - 2 * INSET
STRIP = -(-(5 * BSIDE + 5 * INNER) // GROUP) * GROUP


def pack_edges(cells_ref, against_first, against_second, strips_ref):
    side = BSIDE

    def first(n):
        return cells_ref[n * side : (n + 1) * side]

    def second(n):
        return cells_ref[pl.ds(n + INSET * side, INNER, stride=side), :]

    at = 0
    for line, against, size in ((first, against_first, side), (second, against_second[:INNER], INNER)):
        far = jnp.where(against, line(2), line(side - 3))
        for layer in (line(0), line(1), far, line(side - 2), line(side - 1)):
            strips_ref[at : at + size] = layer
            at += size


def unpack_edges(strips_ref, against_second, edges_ref):
    side = BSIDE
    for n, at in enumerate((0, 1, None, side - 2, side - 1)):
        inner = 5 * side + n * INNER
        edges_ref[n, INSET : INSET + INNER] = strips_ref[inner : inner + INNER]
        for rows, layer in ((0, 0), (side - INSET, 3)):
            if at is None:
                ends = [strips_ref[pl.ds(layer * side + j, INSET, stride=side), :] for j in (2, side - 3)]
                value = jnp.where(against_second[:INSET], ends[0], ends[1])
            else:
                value = strips_ref[pl.ds(layer * side + at, INSET, stride=side), :]
            edges_ref[n, rows : rows + INSET] = value


def fused_kernel(
    near_hbm, level_hbm, x_hbm, mask_hbm, first_hbm, second_hbm, loss_hbm, plane_hbm, speed_hbm, out_ref,
    near_ref, level_ref, x_ref, mask_ref, first_ref, second_ref, loss_ref, plane_ref, speed_ref,
    u_ref, one_ref, two_ref, turned, flux_one, flux_two, flux_turned, speeds, strips, from_left, from_right,
    pick, spread_back, table, first_cube, second_cube, gains, loss_cube, lhs, mapped, spectrum, doubled, loss, total, flat, edges,
    sent, got, result, back,
    sent_left, sent_right, got_left, got_right, sent_in, got_in, own_in, sent_out, got_out, own_out,
    x_here, here,
):
    tiles, count, lanes = u_ref.shape
    width = x_hbm.shape[0]
    parts, each, wide = got.shape
    chunks = result.shape[0]
    plane = VDIM * VDIM
    planes = width // plane
    terms = first_ref.shape[0]
    me = lax.axis_index("vel")
    row = lax.axis_index("space")
    rows = lax.axis_size("space")
    has_left, has_right = row > 0, row < rows - 1
    left, right = lax.rem(row + rows - 1, rows), lax.rem(row + 1, rows)
    peers = [lax.rem(me + n, parts) for n in range(parts)]
    mesh_ids = pl.DeviceIdType.MESH
    fluxes = (flux_one, flux_two, flux_turned)

    early_rows = AHEAD * lanes
    cells_here = [
        pltpu.make_async_copy(x_hbm.at[:early_rows], x_ref.at[:early_rows], x_here.at[0]),
        pltpu.make_async_copy(x_hbm.at[early_rows:], x_ref.at[early_rows:width], x_here.at[1]),
    ]
    near_here, level_here, mask_here, first_here, second_here, loss_here, plane_here, speed_here = [
        pltpu.make_async_copy(source, target, here.at[n])
        for n, (source, target) in enumerate(
            (
                (near_hbm, near_ref), (level_hbm, level_ref), (mask_hbm, mask_ref), (first_hbm, first_ref),
                (second_hbm, second_ref), (loss_hbm, loss_ref), (plane_hbm, plane_ref), (speed_hbm, speed_ref),
            )
        )
    ]
    speed_here.start()
    for copy in cells_here:
        copy.start()
    for copy in (near_here, level_here, mask_here, plane_here, first_here, second_here, loss_here):
        copy.start()

    barrier = pltpu.get_barrier_semaphore()

    @pl.when(has_left)
    def _():
        pl.semaphore_signal(barrier, inc=1, device_id={"space": left}, device_id_type=mesh_ids)

    @pl.when(has_right)
    def _():
        pl.semaphore_signal(barrier, inc=1, device_id={"space": right}, device_id_type=mesh_ids)

    for peer in peers[1:]:
        pl.semaphore_signal(barrier, inc=1, device_id={"vel": peer}, device_id_type=mesh_ids)

    speed_here.wait()
    half = (VDIM - 1) / 2.0
    start = (me * planes).astype(jnp.float32)
    toward = (speed_ref[:, 0, :] + start - half) / half
    across = speed_ref[:, 1, :]
    for n, value in enumerate(
        (jnp.abs(toward), jnp.abs(across), jnp.where(toward < 0, 1.0, 0.0), jnp.where(across < 0, 1.0, 0.0))
    ):
        speeds[:, n, :] = value
    x_ref[width:] = jnp.zeros_like(x_ref[width:])

    pl.semaphore_wait(barrier, has_left.astype(jnp.int32) + has_right.astype(jnp.int32) + (parts - 1))

    def to_right(turn, tile):
        return pltpu.make_async_remote_copy(
            src_ref=strips.at[turn, tile], dst_ref=from_left.at[turn, tile],
            send_sem=sent_right.at[turn, tile], recv_sem=got_left.at[turn, tile],
            device_id={"space": right}, device_id_type=mesh_ids,
        )

    def to_left(turn, tile):
        return pltpu.make_async_remote_copy(
            src_ref=strips.at[turn, tile], dst_ref=from_right.at[turn, tile],
            send_sem=sent_left.at[turn, tile], recv_sem=got_right.at[turn, tile],
            device_id={"space": left}, device_id_type=mesh_ids,
        )

    def send(turn, tile, cells_ref):
        pack_edges(cells_ref.at[tile], *against_masks(speeds.at[tile]), strips.at[turn, tile])

        @pl.when(has_right)
        def _():
            to_right(turn, tile).start()

        @pl.when(has_left)
        def _():
            to_left(turn, tile).start()

    def receive(turn, tile):
        @pl.when(has_left)
        def _():
            to_right(turn, tile).wait_recv()

        @pl.when(has_right)
        def _():
            to_left(turn, tile).wait_recv()

    def launch(tile):
        u_ref[tile] = x_ref[pl.ds(pl.multiple_of(tile * lanes, lanes), lanes), :].T
        send(0, tile, u_ref)

    def begin(tile, carry):
        launch(tile)
        return carry

    cells_here[0].wait()
    lax.fori_loop(0, AHEAD, begin, 0)

    @pl.when(row == 0)
    def _():
        from_left[...] = jnp.zeros_like(from_left)

    @pl.when(row == rows - 1)
    def _():
        from_right[...] = jnp.zeros_like(from_right)

    near_here.wait()
    level_here.wait()
    ratio = courant * jnp.left_shift(1, level_ref[0]).astype(jnp.float32)
    source = []
    for face in range(4):
        for step in (-1, 0, 1):
            held = (near_ref[0, face] == row + step) & (near_ref[0, face] >= 0)
            source.append(jnp.where(held, 1.0, 0.0))
    mask_here.wait()
    marks = jnp.broadcast_to(mask_ref[...], (GROUP, count)).astype(jnp.float32)
    before = lax.broadcasted_iota(jnp.int32, (count, count), 0) < lax.broadcasted_iota(jnp.int32, (count, count), 1)
    rank = dot(marks.astype(jnp.bfloat16), jnp.where(before, 1.0, 0.0).astype(jnp.bfloat16))
    rank = jnp.where(marks > 0.5, rank, -1.0)[:1].astype(jnp.int32)
    slot = lax.broadcasted_iota(jnp.int32, (ACT, count), 0)
    hit = jnp.where(slot == rank, 1.0, 0.0).astype(jnp.bfloat16)
    pick[:, :count] = hit
    pick[:, count:] = hit
    held = parts * GROUP
    slot = lax.broadcasted_iota(jnp.int32, (held, count), 0)
    for chunk in range(chunks):
        home = (slot // GROUP) * each + chunk * HALF + slot % HALF
        for side in range(2):
            own = (home == rank) & (slot % GROUP // HALF == side)
            hit = jnp.where(own, 1.0, 0.0).astype(jnp.bfloat16)
            for at in (chunk % 2 * held, (2 + chunk % 2) * held):
                spread_back[chunk // 2, side, at : at + held] = hit

    for copy in (plane_here, first_here, second_here, loss_here, cells_here[1]):
        copy.wait()
    body = plane // 256 * 256
    tail = plane - body
    table[0:body] = plane_ref[0, :body]
    table[body : 2 * body] = plane_ref[0, :body]
    table[2 * body : 3 * body] = plane_ref[1, :body]
    at = 3 * body
    for part in (0, 0, 1):
        table[at : at + tail] = plane_ref[part, body:]
        at += tail
    if at < table.shape[0]:
        table[at:] = jnp.zeros_like(table[at:])
    for i in range(VDIM):
        columns = slice(i * plane, (i + 1) * plane)
        first_cube[i] = first_ref[:, columns]
        second_cube[i] = second_ref[:, columns]
        done = 0
        while done < plane:
            line_at, lane_at = divmod(i * plane + done, lanes)
            span = min(lanes - lane_at, plane - done)
            loss_cube[i : i + 1, done : done + span] = loss_ref[line_at : line_at + 1, lane_at : lane_at + span]
            done += span

    upper = lax.broadcasted_iota(jnp.int32, (GROUP, plane), 0) < HALF

    def lay(i, carry):
        for term in range(terms):
            one_row = jnp.broadcast_to(first_cube[i, term : term + 1, :], (GROUP, plane))
            two_row = jnp.broadcast_to(second_cube[i, term : term + 1, :], (GROUP, plane))
            gains[term, i] = jnp.where(upper, one_row, two_row)
        return carry

    lax.fori_loop(0, VDIM, lay, 0)

    def all_of(ref, sem):
        pltpu.make_async_copy(ref, ref, sem).wait()

    def in_copy(tile, n):
        lane = pl.ds(pl.multiple_of(tile * 2 * lanes, 2 * lanes), 2 * lanes)
        if n == 0:
            return pltpu.make_async_copy(sent.at[tile, me], got.at[me, :, lane], own_in.at[tile])
        return pltpu.make_async_remote_copy(
            src_ref=sent.at[tile, peers[n]], dst_ref=got.at[me, :, lane],
            send_sem=sent_in.at[tile], recv_sem=got_in.at[tile],
            device_id={"vel": peers[n]}, device_id_type=mesh_ids,
        )

    def ghosts(turn, tile):
        whole = (from_left.at[turn, tile], from_right.at[turn, tile])
        against = against_masks(speeds.at[tile])[1]
        for n in range(2):
            unpack_edges(whole[n], against, edges.at[turn, n])

        def edge(n, block):
            if block < 5:
                return whole[n][block * BSIDE : (block + 1) * BSIDE]
            return edges[turn, n, block - 5]

        return edge

    def single_copy(tile, n):
        lane = pl.ds(tile * lanes, lanes)
        at = tile % 2 * lanes
        place = tiles // 2 - 1 + tile % 2
        if n == 0:
            return pltpu.make_async_copy(
                sent.at[tile // 2, me, :, at : at + lanes], got.at[me, :, lane], own_in.at[place]
            )
        return pltpu.make_async_remote_copy(
            src_ref=sent.at[tile // 2, peers[n], :, at : at + lanes], dst_ref=got.at[me, :, lane],
            send_sem=sent_in.at[place], recv_sem=got_in.at[place],
            device_id={"vel": peers[n]}, device_id_type=mesh_ids,
        )

    def first(tile):
        receive(0, tile)
        advance(
            source, ratio, u_ref.at[tile], None, ghosts(0, tile),
            speeds.at[tile], one_ref.at[tile], fluxes,
        )
        send(1, tile, one_ref)

    def second(tile):
        receive(1, tile)
        advance(
            source, ratio, one_ref.at[tile], u_ref.at[tile], ghosts(1, tile),
            speeds.at[tile], two_ref, fluxes,
        )
        turned[tile] = two_ref[...].T
        high, low = halves(two_ref[...])
        picked = dot(pick[...], jnp.concatenate([high, low], axis=0)).reshape(parts, each, lanes)
        side = tile % 2 if isinstance(tile, int) else lax.rem(tile, 2)
        sent[tile // 2, :, :, pl.ds(side * lanes if isinstance(tile, int) else pl.multiple_of(side * lanes, lanes), lanes)] = picked

        if isinstance(tile, int):
            for n in range(parts):
                single_copy(tile, n).start()
        else:

            @pl.when(side == 1)
            def _():
                for n in range(parts):
                    in_copy(tile // 2, n).start()

    def early(tile, carry):
        launch(tile + AHEAD)
        first(tile)
        return carry

    def steady(tile, carry):
        @pl.when(tile + AHEAD < tiles)
        def _():
            launch(tile + AHEAD)

        first(tile)
        second(tile - LAG)
        return carry

    lax.fori_loop(0, LAG, early, 0)
    lax.fori_loop(LAG, tiles, steady, 0)
    for tile in range(tiles - LAG, tiles):
        second(tile)

    def arrive(tile, carry):
        in_copy(tile, 0).wait()
        all_of(got.at[1:, :, pl.ds(pl.multiple_of(tile * 2 * lanes, 2 * lanes), 2 * lanes)], got_in.at[tile])
        return carry

    lax.fori_loop(0, tiles // 2 - 1, arrive, 0)
    for tile in range(tiles - 2, tiles):
        single_copy(tile, 0).wait()
        all_of(got.at[1:, :, tile * lanes : (tile + 1) * lanes], got_in.at[tiles // 2 - 1 + tile % 2])

    def write_lhs(at, value):
        high, low = halves(value)
        span = slice(at, at + value.shape[0])
        lhs[span, :body] = high[:, :body]
        lhs[span, body : 2 * body] = low[:, :body]
        lhs[span, 2 * body : 3 * body] = high[:, :body]
        pieces = [high[:, body:], low[:, body:], high[:, body:]]
        spare = lhs.shape[1] - 3 * plane
        if spare:
            pieces.append(jnp.zeros((value.shape[0], spare), jnp.bfloat16))
        lhs[span, 3 * body :] = jnp.concatenate(pieces, axis=1)

    column_slices = [slice(c, min(c + LANES, plane)) for c in range(0, plane, LANES)]

    def transform(size):
        mapped[:size] = dot(lhs[:size], table[...])

    def line(columns, many=1, n=0):
        starts = [(i * many + n) * GROUP for i in range(VDIM)]
        return dht24([mapped[at : at + GROUP, columns] for at in starts])

    def out_copy(chunk, n):
        if n == 0:
            return pltpu.make_async_copy(result.at[chunk, me], back.at[chunk, me], own_out.at[chunk])
        return pltpu.make_async_remote_copy(
            src_ref=result.at[chunk, peers[n]], dst_ref=back.at[chunk, me],
            send_sem=sent_out.at[chunk], recv_sem=got_out.at[chunk],
            device_id={"vel": peers[n]}, device_id_type=mesh_ids,
        )

    def double(value, half):
        other = pltpu.roll(value, HALF, 0)
        return jnp.where(upper, value, other) if half == 0 else jnp.where(upper, other, value)

    part = wide // 2
    for group in range(chunks // 2):
        cells = slice(group * GROUP, (group + 1) * GROUP)

        def cube(i):
            v, r = divmod(i, planes)
            return got[v, cells, r * plane : (r + 1) * plane]

        for i in range(0, VDIM, 2):
            pair = jnp.concatenate([cube(i), cube(i + 1)], axis=0)
            loss[i * GROUP : (i + 2) * GROUP] = -pair
            write_lhs(i * GROUP, pair)
        transform(VDIM * GROUP)
        for columns in column_slices:
            for i, value in enumerate(line(columns)):
                spectrum[i * GROUP : (i + 1) * GROUP, columns] = value
        for i in range(0, VDIM, 2):
            pair = [
                spectrum[n * GROUP : (n + 1) * GROUP] * loss_cube[n : n + 1] for n in (i, i + 1)
            ]
            write_lhs(i * GROUP, jnp.concatenate(pair, axis=0))
        transform(VDIM * GROUP)
        for columns in column_slices:
            for i, value in enumerate(line(columns)):
                at = slice(i * GROUP, (i + 1) * GROUP)
                loss[at, columns] = loss[at, columns] * value

        for half in range(2):
            chunk = 2 * group + half
            for i in range(VDIM):
                at = slice(i * GROUP, (i + 1) * GROUP)
                doubled[at] = double(spectrum[at], half)
                total[at] = double(loss[at], half)

            def some(step, carry):
                for i in range(VDIM):
                    value = doubled[i * GROUP : (i + 1) * GROUP]
                    pair = [value * gains[2 * step + n, i] for n in range(2)]
                    write_lhs(i * 2 * GROUP, jnp.concatenate(pair, axis=0))
                transform(2 * VDIM * GROUP)
                for columns in column_slices:
                    images = [line(columns, 2, n) for n in range(2)]
                    for i in range(VDIM):
                        at = slice(i * GROUP, (i + 1) * GROUP)
                        both = [image[i] * pltpu.roll(image[i], HALF, 0) for image in images]
                        total[at, columns] += both[0] + both[1]
                return carry

            lax.fori_loop(0, terms // 2, some, 0)
            low_rows = upper[:, :LANES]
            for v in range(parts):
                for r in range(planes):
                    i = v * planes + r
                    flat[v, :, r * plane : (r + 1) * plane] = total[i * GROUP : (i + 1) * GROUP]
                for at in range(0, part, LANES):
                    result[chunk, v, :, at : at + LANES] = jnp.where(
                        low_rows, flat[v, :, at : at + LANES], flat[v, :, part + at : part + at + LANES]
                    )
            for n in range(parts):
                out_copy(chunk, n).start()

    def sent_all(tile, carry):
        for turn in range(2):

            @pl.when(has_right)
            def _():
                to_right(turn, tile).wait_send()

            @pl.when(has_left)
            def _():
                to_left(turn, tile).wait_send()

        return carry

    lax.fori_loop(0, tiles, sent_all, 0)

    def inward_sent(pair, carry):
        all_of(sent.at[pair, 1:], sent_in.at[pair])
        return carry

    lax.fori_loop(0, tiles // 2 - 1, inward_sent, 0)
    for tile in range(tiles - 2, tiles):
        at = tile % 2 * lanes
        all_of(sent.at[tiles // 2 - 1, 1:, :, at : at + lanes], sent_in.at[tiles // 2 - 1 + tile % 2])

    half_tiles = tiles // 2
    for chunk in range(chunks - 1):
        all_of(result.at[chunk, 1:], sent_out.at[chunk])

    def change(pair, side, column):
        blocks = [
            back[chunk, :, :, pl.ds(column, lanes)].reshape(held, lanes) for chunk in (2 * pair, 2 * pair + 1)
        ]
        high, low = halves(jnp.concatenate(blocks, axis=0).T)
        return dot(jnp.concatenate([high, low], axis=1), spread_back[pair, side])

    pairs = chunks // 2
    for pair in range(pairs):
        for chunk in (2 * pair, 2 * pair + 1):
            out_copy(chunk, 0).wait()
            all_of(back.at[chunk, 1:], got_out.at[chunk])
        if pair < pairs - 1:
            for side in range(2):

                def settle(tile, carry):
                    column = pl.multiple_of(tile * lanes, lanes)
                    turned[side * half_tiles + tile] += change(pair, side, column)
                    return carry

                lax.fori_loop(0, half_tiles, settle, 0)
        else:
            for tile in range(tiles):
                side, column = divmod(tile, half_tiles)
                size = min(lanes, width - tile * lanes)
                if size > 0:
                    value = turned[tile] + change(pair, side, column * lanes)
                    out_ref[tile * lanes : tile * lanes + size, :] = value[:size]
    all_of(result.at[chunks - 1, 1:], sent_out.at[chunks - 1])


def fused_tables(width):
    plane = VDIM * VDIM
    tiles = 2 * -(-width // (2 * LANES))
    index = np.arange(tiles * LANES) % width
    half = (VDIM - 1) / 2.0
    speed = np.zeros((tiles, 8, LANES), np.float32)
    speed[:, 0] = (index // plane).reshape(tiles, LANES)
    second = ((index // VDIM % VDIM).astype(np.float32) - np.float32(half)) / np.float32(half)
    speed[:, 1] = second.reshape(tiles, LANES)
    grid = np.arange(VDIM, dtype=np.float64)
    angle = 2.0 * np.pi * np.outer(grid, grid) / VDIM
    line = (np.cos(angle) + np.sin(angle)) / np.sqrt(VDIM)
    wide = (np.kron(line, line) / np.sqrt(VDIM)).astype(np.float32)
    high = wide.astype(jnp.bfloat16)
    return speed, np.stack([high, (wide - high.astype(np.float32)).astype(jnp.bfloat16)])


def fused(distribution, neighbours, block_level, collide_mask, gain_first, gain_second, loss_rates):
    _, count, width = distribution.shape
    parts = lax.axis_size("vel")
    plane = VDIM * VDIM
    tiles = 2 * pl.cdiv(width, 2 * LANES)
    wide = tiles * LANES
    each = ACT // parts
    chunks = each // HALF
    assert gain_first.shape[0] % 2 == 0
    terms = gain_first.shape[0]
    depth = pl.cdiv(3 * plane, 256) * 256
    smem, f32, bf16 = pltpu.SMEM, jnp.float32, jnp.bfloat16
    speed, planes = fused_tables(width)
    strips = pltpu.VMEM((2, tiles, STRIP, LANES), f32)
    dma = pltpu.SemaphoreType.DMA
    return pl.pallas_call(
        fused_kernel,
        in_specs=[pl.BlockSpec(memory_space=pltpu.HBM)] * 9,
        out_specs=pl.BlockSpec(memory_space=pltpu.VMEM),
        out_shape=pltpu.VMEM((width, count), f32),
        scratch_shapes=[smem((1, 4), jnp.int32), smem((1,), jnp.int32), pltpu.VMEM((wide, count), f32)]
        + [pltpu.VMEM((1, count), jnp.int32)]
        + [pltpu.VMEM(gain_first.shape, f32)] * 2
        + [pltpu.VMEM((loss_rates.size // LANES, LANES), f32)]
        + [pltpu.VMEM(planes.shape, bf16), pltpu.VMEM(speed.shape, f32)]
        + [pltpu.VMEM((tiles, count, LANES), f32)] * 2
        + [pltpu.VMEM((count, LANES), f32), pltpu.VMEM((tiles, LANES, count), f32)]
        + [pltpu.VMEM((count, LANES), f32)] * 3
        + [pltpu.VMEM((tiles, 8, LANES), f32)]
        + [strips] * 3
        + [pltpu.VMEM((ACT, 2 * count), bf16), pltpu.VMEM((chunks // 2, 2, 4 * parts * GROUP, count), bf16)]
        + [pltpu.VMEM((depth, plane), bf16)]
        + [pltpu.VMEM((VDIM, terms, plane), f32)] * 2
        + [pltpu.VMEM((terms, VDIM, GROUP, plane), f32), pltpu.VMEM((VDIM, plane), f32)]
        + [pltpu.VMEM((2 * VDIM * GROUP, depth), bf16), pltpu.VMEM((2 * VDIM * GROUP, plane), f32)]
        + [pltpu.VMEM((VDIM * GROUP, plane), f32)] * 4
        + [pltpu.VMEM((parts, GROUP, wide), f32), pltpu.VMEM((2, 2, 5, BSIDE, LANES), f32)]
        + [pltpu.VMEM((tiles // 2, parts, each, 2 * LANES), f32), pltpu.VMEM((parts, each, wide), f32)]
        + [pltpu.VMEM((chunks, parts, GROUP, wide // 2), f32)] * 2
        + [dma((2, tiles))] * 4
        + [dma((tiles // 2 + 1,))] * 3
        + [dma((chunks,))] * 3 + [dma((2,)), dma((8,))],
        compiler_params=pltpu.CompilerParams(
            collective_id=2, has_side_effects=True, vmem_limit_bytes=56 * 1024 * 1024
        ),
    )(
        neighbours, block_level, distribution.reshape(count, width).T, collide_mask[None],
        gain_first, gain_second, loss_rates.reshape(-1, LANES), jnp.asarray(planes), jnp.asarray(speed),
    )


def shards(
    distribution, neighbours, block_level, collide_mask, gain_first, gain_second, loss_rates
):
    blocks, cell_count, width = distribution.shape
    assert blocks == 1
    parts = lax.axis_size("vel")
    plane = VDIM * VDIM
    if width % plane == 0 and ACT % (parts * GROUP) == 0:
        cells = fused(
            distribution, neighbours, block_level, collide_mask, gain_first, gain_second, loss_rates
        )
        return cells.T.reshape(blocks, cell_count, width)
    density = distribution.reshape(cell_count, width)
    speeds = speed_rows(lax.axis_index("vel") * width, width)
    ratio = courant * jnp.exp2(block_level.astype(jnp.float32))
    offset = neighbours[0] - (lax.axis_index("space") - 1)
    source = (offset[:, None] == jnp.arange(3)) & (neighbours[0] >= 0)[:, None]
    source = source.astype(jnp.float32).reshape(-1)

    section_two = transport(source, ratio, tiled(density), tiled(speeds))

    parts = lax.axis_size("vel")
    each = ACT // parts
    cell_index = jnp.arange(cell_count)
    rank = jnp.sum(jnp.where(cell_index[:, None] < cell_index, collide_mask[:, None], 0), axis=0)
    hit = (rank[:, None] == jnp.arange(ACT)) & (collide_mask > 0)[:, None]
    chosen = jnp.sum(jnp.where(hit, cell_index[:, None], 0), axis=0)
    held = jnp.sum(collide_mask)[None]

    plane = VDIM * VDIM
    operands = collision_operands(gain_first, gain_second, loss_rates)
    if width % plane == 0 and each % GROUP == 0:
        sent = gather(chosen, section_two, (ACT // GROUP, width // plane, GROUP, plane))
        change = swap_collide(sent, operands)
    else:
        sent = gather(chosen, section_two, (parts, 1, each, width))
        got = lax.all_to_all(sent, "vel", split_axis=0, concat_axis=0, tiled=True)
        got = jnp.transpose(got.reshape(parts, each, width), (1, 0, 2))
        got = got.reshape(each, VDIM, plane).transpose(1, 0, 2)
        change = collide(got, operands).transpose(1, 0, 2).reshape(each, parts, width)
        change = change.transpose(1, 0, 2)[:, None]
        change = lax.all_to_all(change, "vel", split_axis=0, concat_axis=0, tiled=True)
    return scatter(chosen, held, section_two, change).reshape(blocks, cell_count, width)


def solution(mesh):
    in_specs = (P("space", None, "vel"), P("space", None), P("space"), P("space"), P(), P(), P())
    out_specs = P("space", None, "vel")
    return jax.shard_map(shards, mesh=mesh, in_specs=in_specs, out_specs=out_specs, check_vma=False)
```

```python
import functools

import jax
import jax.numpy as jnp
import numpy as np
from jax import lax
from jax.experimental import pallas as pl
from jax.experimental.pallas import tpu as pltpu
from jax.sharding import PartitionSpec as P

BSIDE = 16
VDIM = 24
ACT = 128
LANES = 128
GROUP = 8


weno_eps = 1e-06
courant = 0.2


def speed_rows(vel_start, vel_width):
    index = vel_start + jnp.arange(vel_width, dtype=jnp.int32)
    half = (VDIM - 1) / 2.0
    first = ((index // (VDIM * VDIM)).astype(jnp.float32) - half) / half
    second = ((index // VDIM % VDIM).astype(jnp.float32) - half) / half
    rows = [jnp.abs(first), jnp.abs(second), jnp.where(first < 0, 1.0, 0.0), jnp.where(second < 0, 1.0, 0.0)]
    return jnp.stack(rows + [jnp.zeros_like(first)] * 4)


def pack_strips(cells_ref, against_first, against_second, strips_ref):
    side = BSIDE

    def first(n):
        return cells_ref[n * side : (n + 1) * side]

    def second(n):
        return cells_ref[pl.ds(n, side, stride=side), :]

    at = 0
    for line, against in ((first, against_first), (second, against_second)):
        far = jnp.where(against, line(2), line(side - 3))
        for layer in (line(0), line(1), far, line(side - 2), line(side - 1)):
            strips_ref[at : at + side] = layer
            at += side


def sweep(line, against, speed, flux_ref):
    side = BSIDE

    def oriented(n):
        return jnp.where(against, line(side + 5 - n), line(n))

    values = [oriented(n) for n in range(4)]
    slopes = [values[n + 1] - values[n] for n in range(3)]
    bends = []
    for n in range(2):
        bend = slopes[n + 1] - slopes[n]
        bends.append(bend * bend * (13.0 / 3.0) + 4.0 * weno_eps)
    before = None
    for i in range(side + 1):
        values.append(oriented(i + 4))
        slopes.append(values[i + 4] - values[i + 3])
        bend = slopes[i + 3] - slopes[i + 2]
        bends.append(bend * bend * (13.0 / 3.0) + 4.0 * weno_eps)
        d0, d1, d2, d3 = slopes[i : i + 4]
        tilt_low = 3.0 * d1 - d0
        tilt_mid = d1 + d2
        tilt_high = d3 - 3.0 * d2
        rough_low = bends[i] + tilt_low * tilt_low
        rough_mid = bends[i + 1] + tilt_mid * tilt_mid
        rough_high = bends[i + 2] + tilt_high * tilt_high
        low2 = rough_low * rough_low
        mid2 = rough_mid * rough_mid
        high2 = rough_high * rough_high
        weight_low = mid2 * high2
        low3 = 3.0 * low2
        weight_mid = (low3 + low3) * high2
        weight_high = low3 * mid2
        guess_low = 5.0 * d1 - 2.0 * d0
        guess_mid = d1 + (d2 + d2)
        guess_high = 4.0 * d2 - d3
        above = weight_low * guess_low + weight_mid * guess_mid + weight_high * guess_high
        below = weight_low + weight_mid + weight_high
        edge = values[i + 2] + above / (6.0 * below)
        if before is not None:
            flux_ref[(i - 1) * side : i * side] = speed * (edge - before)
        before = edge


def advance(source_ref, ratio, u_ref, base_ref, edge_of, speed_ref, out_ref, fluxes):
    side = BSIDE
    lanes = u_ref.shape[1]
    flux_one, flux_two, flux_turned = fluxes

    def first_line(n):
        return u_ref[n * side : (n + 1) * side]

    def second_line(n):
        return u_ref[pl.ds(n, side, stride=side), :]

    def ghost(face, block, own):
        return (
            source_ref[3 * face] * edge_of(0, block)
            + source_ref[3 * face + 1] * own
            + source_ref[3 * face + 2] * edge_of(1, block)
        )

    def padded(line, faces, start):
        ghosts = {}
        for layer in range(3):
            ghosts[layer] = ghost(faces[0], start + 2 + layer, line(side - 3 + layer))
            ghosts[side + 3 + layer] = ghost(faces[1], start + layer, line(layer))
        return lambda n: ghosts[n] if n in ghosts else line(n - 3)

    against_first, against_second = against_masks(speed_ref)
    sweep(padded(first_line, (0, 1), 0), against_first, spread(speed_ref, 0), flux_one)
    sweep(padded(second_line, (2, 3), 5), against_second, spread(speed_ref, 1), flux_two)
    for n in range(side):
        back = side - 1 - n
        flux_turned[n * side : (n + 1) * side] = jnp.where(
            against_second, flux_two[back * side : (back + 1) * side], flux_two[n * side : (n + 1) * side]
        )
    for n in range(side):
        back = side - 1 - n
        rows = slice(n * side, (n + 1) * side)
        change = jnp.where(against_first, flux_one[back * side : (back + 1) * side], flux_one[rows])
        change = change + flux_turned[pl.ds(n, side, stride=side), :]
        moved = u_ref[rows] - ratio * change
        if base_ref is not None:
            moved = 0.5 * base_ref[rows] + 0.5 * moved
        out_ref[rows] = moved


def spread(speed_ref, row):
    return jnp.broadcast_to(speed_ref[row : row + 1], (BSIDE, speed_ref.shape[1]))


def against_masks(speed_ref):
    return spread(speed_ref, 2) > 0.5, spread(speed_ref, 3) > 0.5


def plain_edges(left_ref, right_ref):
    return lambda n, block: (left_ref, right_ref)[n][block * BSIDE : (block + 1) * BSIDE]


def transport_kernel(
    source_ref, ratio_ref, u_ref, speed_ref, out_ref,
    one_ref, flux_one, flux_two, flux_turned,
    strips, from_left, from_right, sent_left, sent_right, got_left, got_right,
):
    tiles = u_ref.shape[0]
    me = lax.axis_index("space")
    count = lax.axis_size("space")
    has_left, has_right = me > 0, me < count - 1
    left, right = lax.rem(me + count - 1, count), lax.rem(me + 1, count)
    mesh_ids = pl.DeviceIdType.MESH
    ratio = ratio_ref[0]
    fluxes = (flux_one, flux_two, flux_turned)

    barrier = pltpu.get_barrier_semaphore()

    @pl.when(has_left)
    def _():
        pl.semaphore_signal(barrier, inc=1, device_id={"space": left}, device_id_type=mesh_ids)

    @pl.when(has_right)
    def _():
        pl.semaphore_signal(barrier, inc=1, device_id={"space": right}, device_id_type=mesh_ids)

    pl.semaphore_wait(barrier, has_left.astype(jnp.int32) + has_right.astype(jnp.int32))

    def to_right(turn, tile):
        return pltpu.make_async_remote_copy(
            src_ref=strips.at[turn, tile], dst_ref=from_left.at[turn, tile],
            send_sem=sent_right.at[turn, tile], recv_sem=got_left.at[turn, tile],
            device_id={"space": right}, device_id_type=mesh_ids,
        )

    def to_left(turn, tile):
        return pltpu.make_async_remote_copy(
            src_ref=strips.at[turn, tile], dst_ref=from_right.at[turn, tile],
            send_sem=sent_left.at[turn, tile], recv_sem=got_right.at[turn, tile],
            device_id={"space": left}, device_id_type=mesh_ids,
        )

    def send(turn, tile, cells_ref):
        pack_strips(cells_ref.at[tile], *against_masks(speed_ref.at[tile]), strips.at[turn, tile])

        @pl.when(has_right)
        def _():
            to_right(turn, tile).start()

        @pl.when(has_left)
        def _():
            to_left(turn, tile).start()

    def receive(turn, tile):
        @pl.when(has_left)
        def _():
            to_right(turn, tile).wait_recv()

        @pl.when(has_right)
        def _():
            to_left(turn, tile).wait_recv()

    def begin(tile, carry):
        send(0, tile, u_ref)
        return carry

    lax.fori_loop(0, tiles, begin, 0)

    @pl.when(me == 0)
    def _():
        from_left[...] = jnp.zeros_like(from_left)

    @pl.when(me == count - 1)
    def _():
        from_right[...] = jnp.zeros_like(from_right)

    def first(tile, carry):
        receive(0, tile)
        advance(
            source_ref, ratio, u_ref.at[tile], None, plain_edges(from_left.at[0, tile], from_right.at[0, tile]),
            speed_ref.at[tile], one_ref.at[tile], fluxes,
        )
        send(1, tile, one_ref)
        return carry

    lax.fori_loop(0, tiles, first, 0)

    def second(tile, carry):
        receive(1, tile)
        advance(
            source_ref, ratio, one_ref.at[tile], u_ref.at[tile], plain_edges(from_left.at[1, tile], from_right.at[1, tile]),
            speed_ref.at[tile], out_ref.at[tile], fluxes,
        )
        return carry

    lax.fori_loop(0, tiles, second, 0)

    def finish(tile, carry):
        for turn in range(2):

            @pl.when(has_right)
            def _():
                to_right(turn, tile).wait_send()

            @pl.when(has_left)
            def _():
                to_left(turn, tile).wait_send()

        return carry

    lax.fori_loop(0, tiles, finish, 0)


def transport(source, ratio, cells, speeds):
    tiles, count, lanes = cells.shape
    smem = pl.BlockSpec(memory_space=pltpu.SMEM)
    vmem = pl.BlockSpec(memory_space=pltpu.VMEM)
    strips = pltpu.VMEM((2, tiles, 10 * BSIDE, lanes), jnp.float32)
    return pl.pallas_call(
        transport_kernel,
        in_specs=[smem, smem, vmem, vmem],
        out_specs=vmem,
        out_shape=jax.ShapeDtypeStruct(cells.shape, jnp.float32),
        scratch_shapes=[pltpu.VMEM(cells.shape, jnp.float32)]
        + [pltpu.VMEM((count, lanes), jnp.float32)] * 3
        + [strips] * 3
        + [pltpu.SemaphoreType.DMA((2, tiles))] * 4,
        compiler_params=pltpu.CompilerParams(
            collective_id=0, has_side_effects=True, vmem_limit_bytes=48 * 1024 * 1024
        ),
    )(source, ratio, cells, speeds)


def tiled(rows):
    count, width = rows.shape
    tiles = pl.cdiv(width, LANES)
    rows = jnp.pad(rows, ((0, 0), (0, tiles * LANES - width)))
    return rows.reshape(count, tiles, LANES).transpose(1, 0, 2)


def lane_pieces(tiles, width):
    return [(t, t * LANES, min(width, (t + 1) * LANES)) for t in range(tiles)]


def gather_kernel(chosen_ref, cells_ref, out_ref, picked_ref, rows_ref):
    parts, planes, each, plane = out_ref.shape
    tiles = cells_ref.shape[0]

    def one(slot, carry):
        row = chosen_ref[slot]
        for tile in range(tiles):
            picked_ref[tile, pl.ds(slot, 1), :] = cells_ref[tile, pl.ds(row, 1), :]
        return carry

    lax.fori_loop(0, parts * each, one, 0, unroll=8)
    for tile in range(tiles):
        rows_ref[:, tile * LANES : (tile + 1) * LANES] = picked_ref[tile]
    for part in range(parts):
        for n in range(planes):
            out_ref[part, n] = rows_ref[part * each : (part + 1) * each, n * plane : (n + 1) * plane]


def gather(chosen, cells, shape):
    return pl.pallas_call(
        gather_kernel,
        in_specs=[pl.BlockSpec(memory_space=pltpu.SMEM), pl.BlockSpec(memory_space=pltpu.VMEM)],
        out_specs=pl.BlockSpec(memory_space=pltpu.VMEM),
        out_shape=jax.ShapeDtypeStruct(shape, jnp.float32),
        scratch_shapes=[
            pltpu.VMEM((cells.shape[0], shape[0] * shape[2], LANES), jnp.float32),
            pltpu.VMEM((shape[0] * shape[2], cells.shape[0] * LANES), jnp.float32),
        ],
    )(chosen, cells)


def scatter_kernel(chosen_ref, count_ref, cells_ref, change_ref, out_ref, rows_ref):
    parts, planes, each, plane = change_ref.shape
    for tile, begin, end in lane_pieces(cells_ref.shape[0], out_ref.shape[1]):
        out_ref[:, begin:end] = cells_ref[tile, :, : end - begin]
    for part in range(parts):
        for n in range(planes):
            rows_ref[part * each : (part + 1) * each, n * plane : (n + 1) * plane] = change_ref[part, n]

    def one(slot, carry):
        row = pl.ds(chosen_ref[slot], 1)
        out_ref[row, :] += rows_ref[pl.ds(slot, 1), :]
        return carry

    lax.fori_loop(0, count_ref[0], one, 0)


def scatter(chosen, count, cells, change):
    smem = pl.BlockSpec(memory_space=pltpu.SMEM)
    vmem = pl.BlockSpec(memory_space=pltpu.VMEM)
    parts, planes, each, plane = change.shape
    return pl.pallas_call(
        scatter_kernel,
        in_specs=[smem, smem, vmem, vmem],
        out_specs=vmem,
        out_shape=jax.ShapeDtypeStruct((cells.shape[1], planes * plane), jnp.float32),
        scratch_shapes=[pltpu.VMEM((parts * each, planes * plane), jnp.float32)],
    )(chosen, count, cells, change)


def halves(table):
    high = table.astype(jnp.bfloat16)
    low = (table - high.astype(jnp.float32)).astype(jnp.bfloat16)
    return high, low


def dot(left, right):
    return jnp.dot(left, right, preferred_element_type=jnp.float32)


def collision(values, tables, depth):
    first_ref, second_ref, loss_ref, plane_ref, line_ref = tables
    size, plane = values.shape
    group = size // depth

    def transforms(cubes):
        high, low = halves(jnp.concatenate(cubes, axis=0) if len(cubes) > 1 else cubes[0])
        rows = high.shape[0]
        wide = dot(jnp.concatenate([high, low], axis=0), plane_ref[0])
        mapped = wide[:rows] + (wide[rows:] + dot(high, plane_ref[1]))
        results = []
        for n in range(len(cubes)):
            high, low = halves(mapped[n * size : (n + 1) * size])
            wide = dot(line_ref[...], high)
            results.append(wide[:size] + (wide[size:] + dot(line_ref[:size], low)))
        return results

    spectrum = transforms([values])[0].reshape(depth, group, plane)

    def scaled(multiplier):
        return (spectrum * multiplier[:, None, :]).reshape(size, plane)

    total = -values * transforms([scaled(loss_ref[...])])[0]

    def one(term, total):
        image_one, image_two = transforms([scaled(first_ref[term]), scaled(second_ref[term])])
        return total + image_one * image_two

    return lax.fori_loop(0, first_ref.shape[0], one, total)


def collide_kernel(cells_ref, *refs):
    depth, group, plane = cells_ref.shape
    out_ref = refs[-1]
    total = collision(cells_ref[...].reshape(depth * group, plane), refs[:-1], depth)
    out_ref[...] = total.reshape(depth, group, plane)


def swap_collide_kernel(
    cells_ref, first_ref, second_ref, loss_ref, plane_ref, line_ref, out_ref,
    first_cube, second_cube, loss_cube,
    got, result, sent_in, got_in, own_in, sent_out, got_out, own_out,
):
    parts = lax.axis_size("vel")
    blocks, planes, group, plane = cells_ref.shape
    chunks = blocks // parts
    me = lax.axis_index("vel")
    mesh_ids = pl.DeviceIdType.MESH
    peers = [lax.rem(me + n, parts) for n in range(parts)]
    tables = (first_cube, second_cube, loss_cube, plane_ref, line_ref)

    barrier = pltpu.get_barrier_semaphore()
    for peer in peers[1:]:
        pl.semaphore_signal(barrier, inc=1, device_id={"vel": peer}, device_id_type=mesh_ids)
    pl.semaphore_wait(barrier, parts - 1)

    def swap(chunk, from_ref, to_ref, send_sem, recv_sem, own_sem):
        mine = chunk * parts + me
        copies = []
        for n, peer in enumerate(peers):
            source = from_ref.at[chunk * parts + peer]
            if n == 0:
                copies.append(pltpu.make_async_copy(source, to_ref.at[mine], own_sem.at[chunk]))
            else:
                copies.append(
                    pltpu.make_async_remote_copy(
                        src_ref=source, dst_ref=to_ref.at[mine],
                        send_sem=send_sem.at[chunk, n], recv_sem=recv_sem.at[chunk, n],
                        device_id={"vel": peer}, device_id_type=mesh_ids,
                    )
                )
            copies[-1].start()
        return copies

    incoming = [swap(chunk, cells_ref, got, sent_in, got_in, own_in) for chunk in range(chunks)]
    for row in range(parts * planes):
        columns = slice(row * plane, (row + 1) * plane)
        for term in range(first_ref.shape[0]):
            first_cube[term, row : row + 1, :] = first_ref[term : term + 1, columns]
            second_cube[term, row : row + 1, :] = second_ref[term : term + 1, columns]
        loss_cube[row : row + 1, :] = loss_ref[:, columns]
    outgoing = []
    for chunk in range(chunks):
        for copy in incoming[chunk][1:]:
            copy.wait_recv()
        incoming[chunk][0].wait()
        held = slice(chunk * parts, (chunk + 1) * parts)
        values = got[held].reshape(parts * planes * group, plane)
        result[held] = collision(values, tables, parts * planes).reshape(parts, planes, group, plane)
        outgoing.append(swap(chunk, result, out_ref, sent_out, got_out, own_out))
    for copies in outgoing:
        copies[0].wait()
        for copy in copies[1:]:
            copy.wait_recv()
    for copies in incoming + outgoing:
        for copy in copies[1:]:
            copy.wait_send()


def hartley_tables(vdim):
    index = np.arange(vdim, dtype=np.float64)
    angle = 2.0 * np.pi * np.outer(index, index) / vdim
    table = (np.cos(angle) + np.sin(angle)) / np.sqrt(vdim)

    def split(wide):
        wide = wide.astype(np.float32)
        high = wide.astype(jnp.bfloat16)
        return np.stack([high, (wide - high.astype(np.float32)).astype(jnp.bfloat16)])

    return split(np.kron(table, table)), np.concatenate(split(np.kron(table, np.eye(GROUP))))


def collision_operands(gain_first, gain_second, loss_rates):
    plane_table, line_table = hartley_tables(VDIM)
    return gain_first, gain_second, loss_rates[None], jnp.asarray(plane_table), jnp.asarray(line_table)


def collide(cells, operands):
    depth, count, plane = cells.shape
    gain_first, gain_second, loss_rates = operands[:3]
    cube = (gain_first.shape[0], depth, plane)
    operands = (gain_first.reshape(cube), gain_second.reshape(cube), loss_rates.reshape(cube[1:])) + operands[3:]
    spare = -count % GROUP
    if spare:
        cells = jnp.pad(cells, ((0, 0), (0, spare), (0, 0)))
    cell_spec = pl.BlockSpec((depth, GROUP, plane), lambda n: (0, n, 0))

    def whole(shape):
        return pl.BlockSpec(shape, lambda n: (0,) * len(shape))

    result = pl.pallas_call(
        collide_kernel,
        grid=((count + spare) // GROUP,),
        in_specs=[cell_spec] + [whole(array.shape) for array in operands],
        out_specs=cell_spec,
        out_shape=jax.ShapeDtypeStruct(cells.shape, jnp.float32),
        compiler_params=pltpu.CompilerParams(vmem_limit_bytes=56 * 1024 * 1024),
    )(cells, *operands)
    return result[:, :count]


def swap_collide(cells, operands):
    chunks, parts = cells.shape[0] // lax.axis_size("vel"), lax.axis_size("vel")
    vmem = pl.BlockSpec(memory_space=pltpu.VMEM)
    across = pltpu.SemaphoreType.DMA((chunks, parts))
    own = pltpu.SemaphoreType.DMA((chunks,))
    cube = (VDIM, cells.shape[3])
    gains = pltpu.VMEM((operands[0].shape[0],) + cube, jnp.float32)
    return pl.pallas_call(
        swap_collide_kernel,
        in_specs=[vmem] * (1 + len(operands)),
        out_specs=vmem,
        out_shape=jax.ShapeDtypeStruct(cells.shape, jnp.float32),
        scratch_shapes=[gains, gains, pltpu.VMEM(cube, jnp.float32)]
        + [pltpu.VMEM(cells.shape, jnp.float32)] * 2
        + [across, across, own] * 2,
        compiler_params=pltpu.CompilerParams(
            collective_id=1, has_side_effects=True, vmem_limit_bytes=56 * 1024 * 1024
        ),
    )(cells, *operands)


def dht8(x):
    e = [x[n] + x[n + 4] for n in range(4)]
    o = [x[n] - x[n + 4] for n in range(4)]
    a, b = e[0] + e[2], e[0] - e[2]
    c, d = e[1] + e[3], e[1] - e[3]
    p, q = o[0] + o[2], o[0] - o[2]
    root = float(np.sqrt(2.0))
    r, s = root * o[1], root * o[3]
    return [a + c, p + r, b + d, q + s, a - c, p - r, b - d, q - s]


def dht24(x):
    plain, even, odd = [], [], []
    for n in range(8):
        x0, x1, x2 = x[(3 * n) % 24], x[(3 * n + 8) % 24], x[(3 * n + 16) % 24]
        total = x1 + x2
        plain.append(x0 + total)
        even.append(x0 - 0.5 * total)
        odd.append(float(np.sqrt(0.75)) * (x1 - x2))
    plain, even, odd = dht8(plain), dht8(even), dht8(odd)
    result = []
    for f in range(24):
        back = odd[-f % 8]
        result.append((plain[f % 8], even[f % 8] + back, even[f % 8] - back)[f % 3])
    return result


HALF = GROUP // 2
LAG = 2
AHEAD = 3


INSET = 2
INNER = BSIDE - 2 * INSET
STRIP = -(-(5 * BSIDE + 5 * INNER) // GROUP) * GROUP


def pack_edges(cells_ref, against_first, against_second, strips_ref):
    side = BSIDE

    def first(n):
        return cells_ref[n * side : (n + 1) * side]

    def second(n):
        return cells_ref[pl.ds(n + INSET * side, INNER, stride=side), :]

    at = 0
    for line, against, size in ((first, against_first, side), (second, against_second[:INNER], INNER)):
        far = jnp.where(against, line(2), line(side - 3))
        for layer in (line(0), line(1), far, line(side - 2), line(side - 1)):
            strips_ref[at : at + size] = layer
            at += size


def unpack_edges(strips_ref, against_second, edges_ref):
    side = BSIDE
    for n, at in enumerate((0, 1, None, side - 2, side - 1)):
        inner = 5 * side + n * INNER
        edges_ref[n, INSET : INSET + INNER] = strips_ref[inner : inner + INNER]
        for rows, layer in ((0, 0), (side - INSET, 3)):
            if at is None:
                ends = [strips_ref[pl.ds(layer * side + j, INSET, stride=side), :] for j in (2, side - 3)]
                value = jnp.where(against_second[:INSET], ends[0], ends[1])
            else:
                value = strips_ref[pl.ds(layer * side + at, INSET, stride=side), :]
            edges_ref[n, rows : rows + INSET] = value


def fused_kernel(
    near_hbm, level_hbm, x_hbm, mask_hbm, first_hbm, second_hbm, loss_hbm, plane_hbm, speed_hbm, out_ref,
    near_ref, level_ref, x_ref, mask_ref, first_ref, second_ref, loss_ref, plane_ref, speed_ref,
    u_ref, one_ref, two_ref, turned, flux_one, flux_two, flux_turned, speeds, strips, from_left, from_right,
    pick, spread_back, table, first_cube, second_cube, gains, loss_cube, lhs, mapped, spectrum, doubled, loss, total, flat, edges,
    sent, got, result, back,
    sent_left, sent_right, got_left, got_right, sent_in, got_in, own_in, sent_out, got_out, own_out,
    x_here, here,
):
    tiles, count, lanes = u_ref.shape
    width = x_hbm.shape[0]
    parts, each, wide = got.shape
    chunks = result.shape[0]
    plane = VDIM * VDIM
    planes = width // plane
    terms = first_ref.shape[0]
    me = lax.axis_index("vel")
    row = lax.axis_index("space")
    rows = lax.axis_size("space")
    has_left, has_right = row > 0, row < rows - 1
    left, right = lax.rem(row + rows - 1, rows), lax.rem(row + 1, rows)
    peers = [lax.rem(me + n, parts) for n in range(parts)]
    order_of = sorted(range(parts), key=lambda n: abs(n - parts // 2) if n else -1)
    mesh_ids = pl.DeviceIdType.MESH
    fluxes = (flux_one, flux_two, flux_turned)

    early_rows = AHEAD * lanes
    cells_here = [
        pltpu.make_async_copy(x_hbm.at[:early_rows], x_ref.at[:early_rows], x_here.at[0]),
        pltpu.make_async_copy(x_hbm.at[early_rows:], x_ref.at[early_rows:width], x_here.at[1]),
    ]
    near_here, level_here, mask_here, first_here, second_here, loss_here, plane_here, speed_here = [
        pltpu.make_async_copy(source, target, here.at[n])
        for n, (source, target) in enumerate(
            (
                (near_hbm, near_ref), (level_hbm, level_ref), (mask_hbm, mask_ref), (first_hbm, first_ref),
                (second_hbm, second_ref), (loss_hbm, loss_ref), (plane_hbm, plane_ref), (speed_hbm, speed_ref),
            )
        )
    ]
    speed_here.start()
    for copy in cells_here:
        copy.start()
    for copy in (near_here, level_here, mask_here, plane_here, first_here, second_here, loss_here):
        copy.start()

    barrier = pltpu.get_barrier_semaphore()

    @pl.when(has_left)
    def _():
        pl.semaphore_signal(barrier, inc=1, device_id={"space": left}, device_id_type=mesh_ids)

    @pl.when(has_right)
    def _():
        pl.semaphore_signal(barrier, inc=1, device_id={"space": right}, device_id_type=mesh_ids)

    for peer in peers[1:]:
        pl.semaphore_signal(barrier, inc=1, device_id={"vel": peer}, device_id_type=mesh_ids)

    speed_here.wait()
    half = (VDIM - 1) / 2.0
    start = (me * planes).astype(jnp.float32)
    toward = (speed_ref[:, 0, :] + start - half) / half
    across = speed_ref[:, 1, :]
    for n, value in enumerate(
        (jnp.abs(toward), jnp.abs(across), jnp.where(toward < 0, 1.0, 0.0), jnp.where(across < 0, 1.0, 0.0))
    ):
        speeds[:, n, :] = value
    x_ref[width:] = jnp.zeros_like(x_ref[width:])

    pl.semaphore_wait(barrier, has_left.astype(jnp.int32) + has_right.astype(jnp.int32) + (parts - 1))

    def to_right(turn, tile):
        return pltpu.make_async_remote_copy(
            src_ref=strips.at[turn, tile], dst_ref=from_left.at[turn, tile],
            send_sem=sent_right.at[turn, tile], recv_sem=got_left.at[turn, tile],
            device_id={"space": right}, device_id_type=mesh_ids,
        )

    def to_left(turn, tile):
        return pltpu.make_async_remote_copy(
            src_ref=strips.at[turn, tile], dst_ref=from_right.at[turn, tile],
            send_sem=sent_left.at[turn, tile], recv_sem=got_right.at[turn, tile],
            device_id={"space": left}, device_id_type=mesh_ids,
        )

    def send(turn, tile, cells_ref):
        pack_edges(cells_ref.at[tile], *against_masks(speeds.at[tile]), strips.at[turn, tile])

        @pl.when(has_right)
        def _():
            to_right(turn, tile).start()

        @pl.when(has_left)
        def _():
            to_left(turn, tile).start()

    def receive(turn, tile):
        @pl.when(has_left)
        def _():
            to_right(turn, tile).wait_recv()

        @pl.when(has_right)
        def _():
            to_left(turn, tile).wait_recv()

    def launch(tile):
        u_ref[tile] = x_ref[pl.ds(pl.multiple_of(tile * lanes, lanes), lanes), :].T
        send(0, tile, u_ref)

    def begin(tile, carry):
        launch(tile)
        return carry

    cells_here[0].wait()
    lax.fori_loop(0, AHEAD, begin, 0)

    @pl.when(row == 0)
    def _():
        from_left[...] = jnp.zeros_like(from_left)

    @pl.when(row == rows - 1)
    def _():
        from_right[...] = jnp.zeros_like(from_right)

    near_here.wait()
    level_here.wait()
    ratio = courant * jnp.left_shift(1, level_ref[0]).astype(jnp.float32)
    source = []
    for face in range(4):
        for step in (-1, 0, 1):
            held = (near_ref[0, face] == row + step) & (near_ref[0, face] >= 0)
            source.append(jnp.where(held, 1.0, 0.0))
    mask_here.wait()
    marks = jnp.broadcast_to(mask_ref[...], (GROUP, count)).astype(jnp.float32)
    before = lax.broadcasted_iota(jnp.int32, (count, count), 0) < lax.broadcasted_iota(jnp.int32, (count, count), 1)
    rank = dot(marks.astype(jnp.bfloat16), jnp.where(before, 1.0, 0.0).astype(jnp.bfloat16))
    rank = jnp.where(marks > 0.5, rank, -1.0)[:1].astype(jnp.int32)
    slot = lax.broadcasted_iota(jnp.int32, (ACT, count), 0)
    hit = jnp.where(slot == rank, 1.0, 0.0).astype(jnp.bfloat16)
    pick[:, :count] = hit
    pick[:, count:] = hit
    held = parts * GROUP
    slot = lax.broadcasted_iota(jnp.int32, (held, count), 0)
    for chunk in range(chunks):
        home = (slot // GROUP) * each + chunk * HALF + slot % HALF
        for side in range(2):
            own = (home == rank) & (slot % GROUP // HALF == side)
            hit = jnp.where(own, 1.0, 0.0).astype(jnp.bfloat16)
            for at in (chunk % 2 * held, (2 + chunk % 2) * held):
                spread_back[chunk // 2, side, at : at + held] = hit

    for copy in (plane_here, first_here, second_here, loss_here, cells_here[1]):
        copy.wait()
    body = plane // 256 * 256
    tail = plane - body
    table[0:body] = plane_ref[0, :body]
    table[body : 2 * body] = plane_ref[0, :body]
    table[2 * body : 3 * body] = plane_ref[1, :body]
    at = 3 * body
    for part in (0, 0, 1):
        table[at : at + tail] = plane_ref[part, body:]
        at += tail
    if at < table.shape[0]:
        table[at:] = jnp.zeros_like(table[at:])
    for i in range(VDIM):
        columns = slice(i * plane, (i + 1) * plane)
        first_cube[i] = first_ref[:, columns]
        second_cube[i] = second_ref[:, columns]
        done = 0
        while done < plane:
            line_at, lane_at = divmod(i * plane + done, lanes)
            span = min(lanes - lane_at, plane - done)
            loss_cube[i : i + 1, done : done + span] = loss_ref[line_at : line_at + 1, lane_at : lane_at + span]
            done += span

    upper = lax.broadcasted_iota(jnp.int32, (GROUP, plane), 0) < HALF

    def lay(i, carry):
        for term in range(terms):
            one_row = jnp.broadcast_to(first_cube[i, term : term + 1, :], (GROUP, plane))
            two_row = jnp.broadcast_to(second_cube[i, term : term + 1, :], (GROUP, plane))
            gains[term, i] = jnp.where(upper, one_row, two_row)
        return carry

    lax.fori_loop(0, VDIM, lay, 0)

    def all_of(ref, sem):
        pltpu.make_async_copy(ref, ref, sem).wait()

    def in_copy(tile, n):
        lane = pl.ds(pl.multiple_of(tile * lanes, lanes), lanes)
        if n == 0:
            return pltpu.make_async_copy(sent.at[tile, me], got.at[me, :, lane], own_in.at[tile])
        return pltpu.make_async_remote_copy(
            src_ref=sent.at[tile, peers[n]], dst_ref=got.at[me, :, lane],
            send_sem=sent_in.at[tile], recv_sem=got_in.at[tile],
            device_id={"vel": peers[n]}, device_id_type=mesh_ids,
        )

    def ghosts(turn, tile):
        whole = (from_left.at[turn, tile], from_right.at[turn, tile])
        against = against_masks(speeds.at[tile])[1]
        for n in range(2):
            unpack_edges(whole[n], against, edges.at[turn, n])

        def edge(n, block):
            if block < 5:
                return whole[n][block * BSIDE : (block + 1) * BSIDE]
            return edges[turn, n, block - 5]

        return edge

    def ghosts(turn, tile):
        whole = (from_left.at[turn, tile], from_right.at[turn, tile])
        against = against_masks(speeds.at[tile])[1]
        for n in range(2):
            unpack_edges(whole[n], against, edges.at[turn, n])

        def edge(n, block):
            if block < 5:
                return whole[n][block * BSIDE : (block + 1) * BSIDE]
            return edges[turn, n, block - 5]

        return edge

    def single_copy(tile, n):
        lane = pl.ds(tile * lanes, lanes)
        at = tile % 2 * lanes
        place = tiles // 2 - 1 + tile % 2
        if n == 0:
            return pltpu.make_async_copy(
                sent.at[tile // 2, me, :, at : at + lanes], got.at[me, :, lane], own_in.at[place]
            )
        return pltpu.make_async_remote_copy(
            src_ref=sent.at[tile // 2, peers[n], :, at : at + lanes], dst_ref=got.at[me, :, lane],
            send_sem=sent_in.at[place], recv_sem=got_in.at[place],
            device_id={"vel": peers[n]}, device_id_type=mesh_ids,
        )

    def first(tile):
        receive(0, tile)
        advance(
            source, ratio, u_ref.at[tile], None, ghosts(0, tile),
            speeds.at[tile], one_ref.at[tile], fluxes,
        )
        send(1, tile, one_ref)

    def second(tile):
        receive(1, tile)
        advance(
            source, ratio, one_ref.at[tile], u_ref.at[tile], ghosts(1, tile),
            speeds.at[tile], two_ref, fluxes,
        )
        turned[tile] = two_ref[...].T
        high, low = halves(two_ref[...])
        sent[tile] = dot(pick[...], jnp.concatenate([high, low], axis=0)).reshape(parts, each, lanes)
        for n in order_of:
            in_copy(tile, n).start()

    def early(tile, carry):
        launch(tile + AHEAD)
        first(tile)
        return carry

    def steady(tile, carry):
        @pl.when(tile + AHEAD < tiles)
        def _():
            launch(tile + AHEAD)

        first(tile)
        second(tile - LAG)
        return carry

    def late(tile, carry):
        second(tile)
        return carry

    lax.fori_loop(0, LAG, early, 0)
    lax.fori_loop(LAG, tiles, steady, 0)
    lax.fori_loop(tiles - LAG, tiles, late, 0)

    def arrive(tile, carry):
        in_copy(tile, 0).wait()
        all_of(got.at[1:, :, pl.ds(pl.multiple_of(tile * lanes, lanes), lanes)], got_in.at[tile])
        return carry

    lax.fori_loop(0, tiles, arrive, 0)

    def write_lhs(at, value):
        high, low = halves(value)
        span = slice(at, at + value.shape[0])
        lhs[span, :body] = high[:, :body]
        lhs[span, body : 2 * body] = low[:, :body]
        lhs[span, 2 * body : 3 * body] = high[:, :body]
        pieces = [high[:, body:], low[:, body:], high[:, body:]]
        spare = lhs.shape[1] - 3 * plane
        if spare:
            pieces.append(jnp.zeros((value.shape[0], spare), jnp.bfloat16))
        lhs[span, 3 * body :] = jnp.concatenate(pieces, axis=1)

    column_slices = [slice(c, min(c + LANES, plane)) for c in range(0, plane, LANES)]

    def transform(size):
        mapped[:size] = dot(lhs[:size], table[...])

    def line(columns, many=1, n=0):
        starts = [(i * many + n) * GROUP for i in range(VDIM)]
        return dht24([mapped[at : at + GROUP, columns] for at in starts])

    def out_copy(chunk, n):
        if n == 0:
            return pltpu.make_async_copy(result.at[chunk, me], back.at[chunk, me], own_out.at[chunk])
        return pltpu.make_async_remote_copy(
            src_ref=result.at[chunk, peers[n]], dst_ref=back.at[chunk, me],
            send_sem=sent_out.at[chunk], recv_sem=got_out.at[chunk],
            device_id={"vel": peers[n]}, device_id_type=mesh_ids,
        )

    def double(value, half):
        other = pltpu.roll(value, HALF, 0)
        return jnp.where(upper, value, other) if half == 0 else jnp.where(upper, other, value)

    part = wide // 2
    for group in range(chunks // 2):
        cells = slice(group * GROUP, (group + 1) * GROUP)

        def cube(i):
            v, r = divmod(i, planes)
            return got[v, cells, r * plane : (r + 1) * plane]

        for i in range(0, VDIM, 2):
            pair = jnp.concatenate([cube(i), cube(i + 1)], axis=0)
            loss[i * GROUP : (i + 2) * GROUP] = -pair
            write_lhs(i * GROUP, pair)
        transform(VDIM * GROUP)
        for columns in column_slices:
            for i, value in enumerate(line(columns)):
                spectrum[i * GROUP : (i + 1) * GROUP, columns] = value
        for i in range(0, VDIM, 2):
            pair = [
                spectrum[n * GROUP : (n + 1) * GROUP] * loss_cube[n : n + 1] for n in (i, i + 1)
            ]
            write_lhs(i * GROUP, jnp.concatenate(pair, axis=0))
        transform(VDIM * GROUP)
        for columns in column_slices:
            for i, value in enumerate(line(columns)):
                at = slice(i * GROUP, (i + 1) * GROUP)
                loss[at, columns] = loss[at, columns] * value

        for half in range(2):
            chunk = 2 * group + half
            for i in range(VDIM):
                at = slice(i * GROUP, (i + 1) * GROUP)
                doubled[at] = double(spectrum[at], half)
                total[at] = double(loss[at], half)

            def some(step, carry):
                for i in range(VDIM):
                    value = doubled[i * GROUP : (i + 1) * GROUP]
                    pair = [value * gains[2 * step + n, i] for n in range(2)]
                    write_lhs(i * 2 * GROUP, jnp.concatenate(pair, axis=0))
                transform(2 * VDIM * GROUP)
                for columns in column_slices:
                    images = [line(columns, 2, n) for n in range(2)]
                    for i in range(VDIM):
                        at = slice(i * GROUP, (i + 1) * GROUP)
                        both = [image[i] * pltpu.roll(image[i], HALF, 0) for image in images]
                        total[at, columns] += both[0] + both[1]
                return carry

            lax.fori_loop(0, terms // 2, some, 0)
            low_rows = upper[:, :LANES]
            for v in range(parts):
                for r in range(planes):
                    i = v * planes + r
                    flat[v, :, r * plane : (r + 1) * plane] = total[i * GROUP : (i + 1) * GROUP]
                for at in range(0, part, LANES):
                    result[chunk, v, :, at : at + LANES] = jnp.where(
                        low_rows, flat[v, :, at : at + LANES], flat[v, :, part + at : part + at + LANES]
                    )
            for n in range(parts):
                out_copy(chunk, n).start()

    def sent_all(tile, carry):
        for turn in range(2):

            @pl.when(has_right)
            def _():
                to_right(turn, tile).wait_send()

            @pl.when(has_left)
            def _():
                to_left(turn, tile).wait_send()

        return carry

    lax.fori_loop(0, tiles, sent_all, 0)

    def inward_sent(pair, carry):
        all_of(sent.at[pair, 1:], sent_in.at[pair])
        return carry

    lax.fori_loop(0, tiles, inward_sent, 0)

    half_tiles = tiles // 2
    for chunk in range(chunks - 1):
        all_of(result.at[chunk, 1:], sent_out.at[chunk])

    def change(pair, side, column):
        blocks = [
            back[chunk, :, :, pl.ds(column, lanes)].reshape(held, lanes) for chunk in (2 * pair, 2 * pair + 1)
        ]
        high, low = halves(jnp.concatenate(blocks, axis=0).T)
        return dot(jnp.concatenate([high, low], axis=1), spread_back[pair, side])

    pairs = chunks // 2
    for pair in range(pairs):
        for chunk in (2 * pair, 2 * pair + 1):
            out_copy(chunk, 0).wait()
            all_of(back.at[chunk, 1:], got_out.at[chunk])
        if pair < pairs - 1:
            for side in range(2):

                def settle(tile, carry):
                    column = pl.multiple_of(tile * lanes, lanes)
                    turned[side * half_tiles + tile] += change(pair, side, column)
                    return carry

                lax.fori_loop(0, half_tiles, settle, 0)
        else:
            for tile in range(tiles):
                side, column = divmod(tile, half_tiles)
                size = min(lanes, width - tile * lanes)
                if size > 0:
                    value = turned[tile] + change(pair, side, column * lanes)
                    out_ref[tile * lanes : tile * lanes + size, :] = value[:size]
    all_of(result.at[chunks - 1, 1:], sent_out.at[chunks - 1])


def fused_tables(width):
    plane = VDIM * VDIM
    tiles = 2 * -(-width // (2 * LANES))
    index = np.arange(tiles * LANES) % width
    half = (VDIM - 1) / 2.0
    speed = np.zeros((tiles, 8, LANES), np.float32)
    speed[:, 0] = (index // plane).reshape(tiles, LANES)
    second = ((index // VDIM % VDIM).astype(np.float32) - np.float32(half)) / np.float32(half)
    speed[:, 1] = second.reshape(tiles, LANES)
    grid = np.arange(VDIM, dtype=np.float64)
    angle = 2.0 * np.pi * np.outer(grid, grid) / VDIM
    line = (np.cos(angle) + np.sin(angle)) / np.sqrt(VDIM)
    wide = (np.kron(line, line) / np.sqrt(VDIM)).astype(np.float32)
    high = wide.astype(jnp.bfloat16)
    return speed, np.stack([high, (wide - high.astype(np.float32)).astype(jnp.bfloat16)])


def fused(distribution, neighbours, block_level, collide_mask, gain_first, gain_second, loss_rates):
    _, count, width = distribution.shape
    parts = lax.axis_size("vel")
    plane = VDIM * VDIM
    tiles = 2 * pl.cdiv(width, 2 * LANES)
    wide = tiles * LANES
    each = ACT // parts
    chunks = each // HALF
    assert gain_first.shape[0] % 2 == 0
    terms = gain_first.shape[0]
    depth = pl.cdiv(3 * plane, 256) * 256
    smem, f32, bf16 = pltpu.SMEM, jnp.float32, jnp.bfloat16
    speed, planes = fused_tables(width)
    strips = pltpu.VMEM((2, tiles, STRIP, LANES), f32)
    dma = pltpu.SemaphoreType.DMA
    return pl.pallas_call(
        fused_kernel,
        in_specs=[pl.BlockSpec(memory_space=pltpu.HBM)] * 9,
        out_specs=pl.BlockSpec(memory_space=pltpu.VMEM),
        out_shape=pltpu.VMEM((width, count), f32),
        scratch_shapes=[smem((1, 4), jnp.int32), smem((1,), jnp.int32), pltpu.VMEM((wide, count), f32)]
        + [pltpu.VMEM((1, count), jnp.int32)]
        + [pltpu.VMEM(gain_first.shape, f32)] * 2
        + [pltpu.VMEM((loss_rates.size // LANES, LANES), f32)]
        + [pltpu.VMEM(planes.shape, bf16), pltpu.VMEM(speed.shape, f32)]
        + [pltpu.VMEM((tiles, count, LANES), f32)] * 2
        + [pltpu.VMEM((count, LANES), f32), pltpu.VMEM((tiles, LANES, count), f32)]
        + [pltpu.VMEM((count, LANES), f32)] * 3
        + [pltpu.VMEM((tiles, 8, LANES), f32)]
        + [strips] * 3
        + [pltpu.VMEM((ACT, 2 * count), bf16), pltpu.VMEM((chunks // 2, 2, 4 * parts * GROUP, count), bf16)]
        + [pltpu.VMEM((depth, plane), bf16)]
        + [pltpu.VMEM((VDIM, terms, plane), f32)] * 2
        + [pltpu.VMEM((terms, VDIM, GROUP, plane), f32), pltpu.VMEM((VDIM, plane), f32)]
        + [pltpu.VMEM((2 * VDIM * GROUP, depth), bf16), pltpu.VMEM((2 * VDIM * GROUP, plane), f32)]
        + [pltpu.VMEM((VDIM * GROUP, plane), f32)] * 4
        + [pltpu.VMEM((parts, GROUP, wide), f32), pltpu.VMEM((2, 2, 5, BSIDE, LANES), f32)]
        + [pltpu.VMEM((tiles, parts, each, LANES), f32), pltpu.VMEM((parts, each, wide), f32)]
        + [pltpu.VMEM((chunks, parts, GROUP, wide // 2), f32)] * 2
        + [dma((2, tiles))] * 4
        + [dma((tiles,))] * 3
        + [dma((chunks,))] * 3 + [dma((2,)), dma((8,))],
        compiler_params=pltpu.CompilerParams(
            collective_id=2, has_side_effects=True, vmem_limit_bytes=56 * 1024 * 1024
        ),
    )(
        neighbours, block_level, distribution.reshape(count, width).T, collide_mask[None],
        gain_first, gain_second, loss_rates.reshape(-1, LANES), jnp.asarray(planes), jnp.asarray(speed),
    )


def shards(
    distribution, neighbours, block_level, collide_mask, gain_first, gain_second, loss_rates
):
    blocks, cell_count, width = distribution.shape
    assert blocks == 1
    parts = lax.axis_size("vel")
    plane = VDIM * VDIM
    if width % plane == 0 and ACT % (parts * GROUP) == 0:
        cells = fused(
            distribution, neighbours, block_level, collide_mask, gain_first, gain_second, loss_rates
        )
        return cells.T.reshape(blocks, cell_count, width)
    density = distribution.reshape(cell_count, width)
    speeds = speed_rows(lax.axis_index("vel") * width, width)
    ratio = courant * jnp.exp2(block_level.astype(jnp.float32))
    offset = neighbours[0] - (lax.axis_index("space") - 1)
    source = (offset[:, None] == jnp.arange(3)) & (neighbours[0] >= 0)[:, None]
    source = source.astype(jnp.float32).reshape(-1)

    section_two = transport(source, ratio, tiled(density), tiled(speeds))

    parts = lax.axis_size("vel")
    each = ACT // parts
    cell_index = jnp.arange(cell_count)
    rank = jnp.sum(jnp.where(cell_index[:, None] < cell_index, collide_mask[:, None], 0), axis=0)
    hit = (rank[:, None] == jnp.arange(ACT)) & (collide_mask > 0)[:, None]
    chosen = jnp.sum(jnp.where(hit, cell_index[:, None], 0), axis=0)
    held = jnp.sum(collide_mask)[None]

    plane = VDIM * VDIM
    operands = collision_operands(gain_first, gain_second, loss_rates)
    if width % plane == 0 and each % GROUP == 0:
        sent = gather(chosen, section_two, (ACT // GROUP, width // plane, GROUP, plane))
        change = swap_collide(sent, operands)
    else:
        sent = gather(chosen, section_two, (parts, 1, each, width))
        got = lax.all_to_all(sent, "vel", split_axis=0, concat_axis=0, tiled=True)
        got = jnp.transpose(got.reshape(parts, each, width), (1, 0, 2))
        got = got.reshape(each, VDIM, plane).transpose(1, 0, 2)
        change = collide(got, operands).transpose(1, 0, 2).reshape(each, parts, width)
        change = change.transpose(1, 0, 2)[:, None]
        change = lax.all_to_all(change, "vel", split_axis=0, concat_axis=0, tiled=True)
    return scatter(chosen, held, section_two, change).reshape(blocks, cell_count, width)


def solution(mesh):
    in_specs = (P("space", None, "vel"), P("space", None), P("space"), P("space"), P(), P(), P())
    out_specs = P("space", None, "vel")
    return jax.shard_map(shards, mesh=mesh, in_specs=in_specs, out_specs=out_specs, check_vma=False)
```
